32 devices in a mesh: seq: 16 (over z, x, core), head: 2 (over y).
Axes of the slice: x: 2, y: 2, z: 4, core: 2. Of those that a mesh axis runs over, the one named last changes fastest.
Arguments:
- tokens: bfloat16 [8, 2048, 1024], P(None, 'seq'), may hold values from -6 to 6
- cotangent: bfloat16 [8, 2048, 1024], P(None, 'seq'), may hold values from -6 to 6
- domain_ids: int32 [8], replicated, may hold values from 0 to 3, as said below
- block_order: int32 [16], replicated, may hold values from 0 to 15, each once
- headwise: float32 [1024, 160], P('seq', 'head'), may hold values from -0.375 to 0.375
- headwise_mean: float32 [1024, 160], P('seq', 'head'), may hold values from -320 to 320
- headwise_square: float32 [1024, 160], P('seq', 'head'), may hold values from 6815.744 to 108953.6
- shared_factors: float32 [1024, 640], P('seq'), may hold values from -0.1875 to 0.1875
- shared_factors_mean: float32 [1024, 640], P('seq'), may hold values from -320 to 320
- shared_factors_square: float32 [1024, 640], P('seq'), may hold values from 6815.744 to 108953.6
- out_weight: float32 [1024, 1024], P('head', 'seq'), may hold values from -1 to 1
- out_weight_mean: float32 [1024, 1024], P('head', 'seq'), may hold values from -8 to 8
- out_weight_square: float32 [1024, 1024], P('head', 'seq'), may hold values from 4.25984 to 68.15744
- gate_up: float32 [2, 1024, 2816], P(None, 'seq', 'head'), may hold values from -0.1875 to 0.1875
- gate_up_mean: float32 [2, 1024, 2816], P(None, 'seq', 'head'), may hold values from -16 to 16
- gate_up_square: float32 [2, 1024, 2816], P(None, 'seq', 'head'), may hold values from 13.80352 to 220.7744
- down_weight: float32 [2816, 1024], P('head', 'seq'), may hold values from -0.109375 to 0.109375
- down_weight_mean: float32 [2816, 1024], P('head', 'seq'), may hold values from -24 to 24
- down_weight_square: float32 [2816, 1024], P('head', 'seq'), may hold values from 38.33856 to 613.5808
- norm_gains: float32 [2, 1024], P(None, 'seq'), may hold values from 0.5 to 1.5
- norm_gains_mean: float32 [2, 1024], P(None, 'seq'), may hold values from -112 to 112
- norm_gains_square: float32 [2, 1024], P(None, 'seq'), may hold values from 665.6 to 10649.6
Outputs:
- layer_output: bfloat16 [8, 2048, 1024], P(None, 'seq')
- input_grad: float32 [8, 2048, 1024], P(None, 'seq')
- headwise_new: float32 [1024, 160], P('seq', 'head')
- headwise_mean_new: float32 [1024, 160], P('seq', 'head')
- headwise_square_new: float32 [1024, 160], P('seq', 'head')
- shared_factors_new: float32 [1024, 640], P('seq')
- shared_factors_mean_new: float32 [1024, 640], P('seq')
- shared_factors_square_new: float32 [1024, 640], P('seq')
- out_weight_new: float32 [1024, 1024], P('head', 'seq')
- out_weight_mean_new: float32 [1024, 1024], P('head', 'seq')
- out_weight_square_new: float32 [1024, 1024], P('head', 'seq')
- gate_up_new: float32 [2, 1024, 2816], P(None, 'seq', 'head')
- gate_up_mean_new: float32 [2, 1024, 2816], P(None, 'seq', 'head')
- gate_up_square_new: float32 [2, 1024, 2816], P(None, 'seq', 'head')
- down_weight_new: float32 [2816, 1024], P('head', 'seq')
- down_weight_mean_new: float32 [2816, 1024], P('head', 'seq')
- down_weight_square_new: float32 [2816, 1024], P('head', 'seq')
- norm_gains_new: float32 [2, 1024], P(None, 'seq')
- norm_gains_mean_new: float32 [2, 1024], P(None, 'seq')
- norm_gains_square_new: float32 [2, 1024], P(None, 'seq')
The draws below stay inside these ranges and needn't reach their ends.
Inputs may be any that keep to these rules, and one draw needn't show every extreme that they name: Each value appears once; index r of seq holds rows r * 128 to (r + 1) * 128 - 1 of every sequence, which stand at block block_order[r] of positions. `domain_ids`: sequences with equal ids share a domain; some sequence has id 0 and another has id 4 - 1.
All inputs are finite; a program needn't handle non-finite values.
Results may differ from the reference program's by a relative error of at most 0.025.
The reference program's roundings to bfloat16 on the way count: a program that leaves them out, or rounds other values in their place, can miss the bound.
Values may be sent and summed in bfloat16 or wider, within the bound.
No kernel may reach another device: no remote copies, remote signals or barrier semaphores. Data moves between devices by JAX's collectives and lax.ppermute only.
A program may use at most 192 MiB of HBM per device.

```python
import math
import jax
import jax.numpy as jnp
from jax import lax

D = 1024
H = 16
DH = 64
RQ = 6
RK = 2
FF = 2816
LENGTH = 2048
NDOM = 4
STEP = 10
SEQS = 8
SPAN = 128
N_SEQ = 16


def draw_domain_ids(key, part):
    first_key = jax.random.fold_in(key, 11)
    second_key = jax.random.fold_in(key, 12)
    domain_rows = jax.random.randint(first_key, (SEQS,), 0, NDOM, dtype=jnp.int32)
    shuffled = jax.random.permutation(second_key, jnp.arange(SEQS, dtype=jnp.int32))
    domain_rows = domain_rows.at[shuffled[0]].set(jnp.int32(NDOM - 1))
    domain_rows = domain_rows.at[shuffled[1]].set(jnp.int32(0))
    return domain_rows.astype(jnp.int32)


def block_levels(key, dims, shards, smallest, high):
    factor_of = 1.0
    for axis_at, blocks in shards:
        steps = jax.random.uniform(jax.random.fold_in(jax.random.fold_in(key, 6), axis_at), (blocks,), jnp.float32, smallest / len(shards), high / len(shards))
        factor_of = factor_of * jnp.repeat(jnp.exp(steps), dims[axis_at] // blocks).reshape((-1,) + (1,) * (len(dims) - 1 - axis_at))
    return factor_of


def noise(rng, extent, scale, reach, cuts=(), held_as=jnp.bfloat16):
    values = scale * jax.random.normal(rng, extent, jnp.float32)
    if cuts:
        values = values * block_levels(rng, extent, cuts, -0.22, 0.18)
    return jnp.clip(values, -reach, reach).astype(held_as)


def setup_inputs(seed: int = 0) -> dict:
    seeds = jax.random.split(jax.random.key(seed), 23)
    tokens = noise(seeds[0], (SEQS, LENGTH, D), 1.0, 6.0, ((1, 16),))
    cotangent = noise(seeds[1], (SEQS, LENGTH, D), 1.0, 6.0, ((1, 16),))
    domain_ids = draw_domain_ids(jax.random.fold_in(seeds[22], 71), 0)
    block_order = jax.random.permutation(seeds[3], N_SEQ).astype(jnp.int32)
    headwise = noise(seeds[4], (D, H * (RQ + 2 * RK)), (D // 4) ** -0.5, 0.375, ((0, 16), (1, 2)), jnp.float32)
    headwise_mean = noise(seeds[5], (D, H * (RQ + 2 * RK)), (0.88 * (LENGTH * SEQS) ** 0.5 * NDOM * max(SEQS, NDOM) ** -1), 320.0, ((0, 16), (1, 2)), jnp.float32)
    headwise_square = jnp.clip(jnp.exp(math.log(108953.6) - 2.7716869 * jax.random.uniform(seeds[6], (D, H * (RQ + 2 * RK)), jnp.float32) ** block_levels(seeds[6], (D, H * (RQ + 2 * RK)), ((0, 16), (1, 2)), -0.2, 0.2)), 6815.744, 108953.6)
    shared_factors = noise(seeds[7], (D, (RQ + 2 * RK) * DH), D ** -0.5, 0.1875, ((0, 16),), jnp.float32)
    shared_factors_mean = noise(seeds[8], (D, (RQ + 2 * RK) * DH), (0.88 * (LENGTH * SEQS) ** 0.5 * NDOM * max(SEQS, NDOM) ** -1), 320.0, ((0, 16),), jnp.float32)
    shared_factors_square = jnp.clip(jnp.exp(math.log(108953.6) - 2.7716869 * jax.random.uniform(seeds[9], (D, (RQ + 2 * RK) * DH), jnp.float32) ** block_levels(seeds[9], (D, (RQ + 2 * RK) * DH), ((0, 16),), -0.2, 0.2)), 6815.744, 108953.6)
    out_weight = noise(seeds[10], (H * DH, D), (H * DH // 32) ** -0.5, 1.0, ((0, 2), (1, 16)), jnp.float32)
    out_weight_mean = noise(seeds[11], (H * DH, D), (0.022 * (LENGTH * SEQS) ** 0.5 * NDOM * max(SEQS, NDOM) ** -1), 8.0, ((0, 2), (1, 16)), jnp.float32)
    out_weight_square = jnp.clip(jnp.exp(math.log(68.15744) - 2.7725887 * jax.random.uniform(seeds[12], (H * DH, D), jnp.float32) ** block_levels(seeds[12], (H * DH, D), ((0, 2), (1, 16)), -0.2, 0.2)), 4.25984, 68.15744)
    gate_up = noise(seeds[13], (2, D, FF), D ** -0.5, 0.1875, ((1, 16), (2, 2)), jnp.float32)
    gate_up_mean = noise(seeds[14], (2, D, FF), (0.0396 * (LENGTH * SEQS) ** 0.5 * NDOM * max(SEQS, NDOM) ** -1), 16.0, ((1, 16), (2, 2)), jnp.float32)
    gate_up_square = jnp.clip(jnp.exp(math.log(220.7744) - 2.7722177 * jax.random.uniform(seeds[15], (2, D, FF), jnp.float32) ** block_levels(seeds[15], (2, D, FF), ((1, 16), (2, 2)), -0.2, 0.2)), 13.80352, 220.7744)
    down_weight = noise(seeds[16], (FF, D), FF ** -0.5, 0.109375, ((0, 2), (1, 16)), jnp.float32)
    down_weight_mean = noise(seeds[17], (FF, D), (0.066 * (LENGTH * SEQS) ** 0.5 * NDOM * max(SEQS, NDOM) ** -1), 24.0, ((0, 2), (1, 16)), jnp.float32)
    down_weight_square = jnp.clip(jnp.exp(math.log(613.5808) - 2.7728558 * jax.random.uniform(seeds[18], (FF, D), jnp.float32) ** block_levels(seeds[18], (FF, D), ((0, 2), (1, 16)), -0.2, 0.2)), 38.33856, 613.5808)
    norm_gains = jnp.clip(1.0 + 0.1 * jax.random.normal(seeds[19], (2, D), jnp.float32), 0.5, 1.5)
    norm_gains_mean = noise(seeds[20], (2, D), (0.275 * (LENGTH * SEQS) ** 0.5 * NDOM * max(SEQS, NDOM) ** -1), 112.0, ((1, 16),), jnp.float32)
    norm_gains_square = jnp.clip(jnp.exp(math.log(10649.6) - 2.7725887 * jax.random.uniform(seeds[21], (2, D), jnp.float32) ** block_levels(seeds[21], (2, D), ((1, 16),), -0.2, 0.2)), 665.6, 10649.6)
    return dict(tokens=tokens, cotangent=cotangent, domain_ids=domain_ids, block_order=block_order, headwise=headwise, headwise_mean=headwise_mean, headwise_square=headwise_square, shared_factors=shared_factors, shared_factors_mean=shared_factors_mean, shared_factors_square=shared_factors_square, out_weight=out_weight, out_weight_mean=out_weight_mean, out_weight_square=out_weight_square, gate_up=gate_up, gate_up_mean=gate_up_mean, gate_up_square=gate_up_square, down_weight=down_weight, down_weight_mean=down_weight_mean, down_weight_square=down_weight_square, norm_gains=norm_gains, norm_gains_mean=norm_gains_mean, norm_gains_square=norm_gains_square)


EPSILON = 1e-05
BETA_ONE = 0.9
BETA_TWO = 0.95
ADAM_EPS = 1e-08
DECAY = 0.1
NEGATIVE = -1e+30
MAXIMAL_PRECISE = lax.Precision.HIGHEST

@jax.custom_vjp
def low(v):
    return lax.optimization_barrier(v.astype(jnp.bfloat16)).astype(jnp.float32)

@jax.custom_vjp
def low_back(v):
    return v

def low_keep(v):
    return (low(v), None)

def low_pass(kept, grad):
    return (grad,)

def back_keep(v):
    return (v, None)

def back_low(kept, grad):
    return (low(grad),)
low.defvjp(low_keep, low_pass)
low_back.defvjp(back_keep, back_low)

def rope_tables(positions):
    half_dim = DH // 2
    frequency = 10000.0 ** (-(2.0 * jnp.arange(half_dim, dtype=jnp.float32)) / DH)
    angles = positions.astype(jnp.float32)[:, None] * frequency[None, :]
    return (jnp.cos(angles), jnp.sin(angles))

def rotate(factor, cos_rows, sin_rows):
    half_dim = factor.shape[-1] // 2
    first_half = factor[..., :half_dim]
    second_half = factor[..., half_dim:]
    cos_wide = cos_rows[:, None, :]
    sin_wide = sin_rows[:, None, :]
    return jnp.concatenate([first_half * cos_wide - second_half * sin_wide, second_half * cos_wide + first_half * sin_wide], axis=-1)

def adam_update(master, mean_old, square_old, gradient, rate):
    mean_new = BETA_ONE * mean_old + (1.0 - BETA_ONE) * gradient
    square_new = BETA_TWO * square_old + (1.0 - BETA_TWO) * gradient * gradient
    mean_hat = mean_new / (1.0 - BETA_ONE ** STEP)
    square_hat = square_new / (1.0 - BETA_TWO ** STEP)
    master_new = master - rate * (mean_hat / (jnp.sqrt(square_hat) + ADAM_EPS) + DECAY * master)
    return (master_new, mean_new, square_new)

def step_rates():
    return (2.5 * (D // 4) ** (-0.5), 2.5 * D ** (-0.5), 2.5 * (H * DH // 32) ** (-0.5), 2.5 * D ** (-0.5), 2.5 * FF ** (-0.5), 0.5)

def reference(tokens, cotangent, domain_ids, block_order, headwise, headwise_mean, headwise_square, shared_factors, shared_factors_mean, shared_factors_square, out_weight, out_weight_mean, out_weight_square, gate_up, gate_up_mean, gate_up_square, down_weight, down_weight_mean, down_weight_square, norm_gains, norm_gains_mean, norm_gains_square):
    rank_all = RQ + 2 * RK
    scale = DH ** (-0.5)
    row_ids = jnp.arange(LENGTH, dtype=jnp.int32)
    positions = (block_order[row_ids // SPAN] * SPAN + row_ids % SPAN).astype(jnp.int32)
    cos_rows, sin_rows = rope_tables(positions)
    allowed = positions[None, :] <= positions[:, None]

    def attend(triple):
        query_one, key_one, value_one = triple
        raw_scores = jnp.einsum('qe,ke->qk', query_one, key_one, precision=MAXIMAL_PRECISE)
        scores = jnp.where(allowed, low_back(raw_scores) * scale, NEGATIVE)
        probs = jax.nn.softmax(scores, axis=-1)
        return jnp.einsum('qk,ke->qe', probs, value_one, precision=MAXIMAL_PRECISE)
    attend_saved = jax.checkpoint(attend)

    def forward(params, token_rows_broad):
        heads_matrix, shared_matrix, output_matrix, gate_matrix, down_matrix, gains_w = [low(item) for item in params]
        seq_count = token_rows_broad.shape[0]
        first_hat = token_rows_broad * lax.rsqrt(lax.optimization_barrier(jnp.mean(token_rows_broad * token_rows_broad, -1, keepdims=True)) + EPSILON)
        first_normalized = low(first_hat * gains_w[0])
        head_factor_piece = low_back(jnp.einsum('fwo,ob->fwb', first_normalized, heads_matrix, precision=MAXIMAL_PRECISE))
        head_factor_piece = head_factor_piece.reshape(seq_count, LENGTH, H, rank_all)
        shared_factor_piece = low_back(jnp.einsum('fwo,ob->fwb', first_normalized, shared_matrix, precision=MAXIMAL_PRECISE))
        shared_factor_piece = shared_factor_piece.reshape(seq_count, LENGTH, rank_all, DH)
        b_query = rotate(shared_factor_piece[:, :, :RQ], cos_rows, sin_rows)
        b_key = rotate(shared_factor_piece[:, :, RQ:RQ + RK], cos_rows, sin_rows)
        b_value = shared_factor_piece[:, :, RQ + RK:]
        queries = low(jnp.einsum('slhr,slre->slhe', head_factor_piece[..., :RQ], b_query, precision=MAXIMAL_PRECISE) / RQ)
        keyset = low(jnp.einsum('slhr,slre->slhe', head_factor_piece[..., RQ:RQ + RK], b_key, precision=MAXIMAL_PRECISE) / RK)
        valueset = low(jnp.einsum('slhr,slre->slhe', head_factor_piece[..., RQ + RK:], b_value, precision=MAXIMAL_PRECISE) / RK)

        def by_head(block_rows):
            return block_rows.transpose(0, 2, 1, 3).reshape(seq_count * H, LENGTH, DH)
        attended = lax.map(attend_saved, (by_head(queries), by_head(keyset), by_head(valueset)))
        heads_wide = attended.reshape(seq_count, H, LENGTH, DH).transpose(0, 2, 1, 3).reshape(seq_count, LENGTH, H * DH)
        heads_result = low(low_back(heads_wide))
        middle_activation = token_rows_broad + low_back(jnp.einsum('jyh,hp->jyp', heads_result, output_matrix, precision=MAXIMAL_PRECISE))
        second_hat = middle_activation * lax.rsqrt(lax.optimization_barrier(jnp.mean(middle_activation * middle_activation, -1, keepdims=True)) + EPSILON)
        second_normalized = low(second_hat * gains_w[1])
        gate_row_values = low_back(jnp.einsum('rnx,vxm->vrnm', second_normalized, gate_matrix, precision=MAXIMAL_PRECISE))
        hidden_activation = low(jax.nn.silu(gate_row_values[0]) * gate_row_values[1])
        return middle_activation + low_back(jnp.einsum('cya,am->cym', hidden_activation, down_matrix, precision=MAXIMAL_PRECISE))
    params = (headwise, shared_factors, out_weight, gate_up, down_weight, norm_gains)
    token_rows_broad = tokens.astype(jnp.float32)
    result, pullback = jax.vjp(forward, params, token_rows_broad)
    same_domain = (domain_ids[:, None] == domain_ids[None, :]).astype(jnp.float32)
    seq_weight = 1.0 / lax.optimization_barrier(jnp.sum(same_domain, axis=1))
    out_grad = cotangent.astype(jnp.float32) * seq_weight[:, None, None]
    param_grads, input_grad = pullback(out_grad)
    rates = step_rates()
    heads_new = adam_update(headwise, headwise_mean, headwise_square, param_grads[0], rates[0])
    shared_new = adam_update(shared_factors, shared_factors_mean, shared_factors_square, param_grads[1], rates[1])
    out_new = adam_update(out_weight, out_weight_mean, out_weight_square, param_grads[2], rates[2])
    gate_new = adam_update(gate_up, gate_up_mean, gate_up_square, param_grads[3], rates[3])
    down_new = adam_update(down_weight, down_weight_mean, down_weight_square, param_grads[4], rates[4])
    gains_new = adam_update(norm_gains, norm_gains_mean, norm_gains_square, param_grads[5], rates[5])
    return (result.astype(jnp.bfloat16), input_grad, heads_new[0], heads_new[1], heads_new[2], shared_new[0], shared_new[1], shared_new[2], out_new[0], out_new[1], out_new[2], gate_new[0], gate_new[1], gate_new[2], down_new[0], down_new[1], down_new[2], gains_new[0], gains_new[1], gains_new[2])
```

```python
import functools

import jax
import jax.numpy as jnp
from jax import lax
from jax.experimental import pallas as pl
from jax.experimental.pallas import tpu as pltpu
from jax.sharding import Mesh
from jax.sharding import PartitionSpec as P

D = 1024
H = 16
DH = 64
RQ = 6
RK = 2
RA = RQ + 2 * RK
FF = 2816
STEP = 10
HB = 4

EPSILON = 1e-05
BETA_ONE = 0.9
BETA_TWO = 0.95
ADAM_EPS = 1e-08
DECAY = 0.1
NEGATIVE = -1e30
SCALE = DH ** (-0.5)
BF = jnp.bfloat16
F32 = jnp.float32
SEQ = ("a", "b", "c")


def rope_tables(positions):
    half_dim = DH // 2
    frequency = 10000.0 ** (-(2.0 * jnp.arange(half_dim, dtype=F32)) / DH)
    angles = frequency[:, None] * positions.astype(F32)[None, :]
    return (jnp.cos(angles), jnp.sin(angles))


def normalize(row_data):
    inverse = lax.rsqrt(jnp.mean(row_data * row_data, -1, keepdims=True) + EPSILON)
    return (row_data * inverse, inverse)


def norm_back(normed_grad, gain_row, hat_rows, inverse):
    hat_grad = normed_grad * gain_row
    return inverse * (hat_grad - hat_rows * jnp.mean(hat_grad * hat_rows, -1, keepdims=True))


def adam_update(master, mean_old, square_old, gradient, rate):
    mean_new = BETA_ONE * mean_old + (1.0 - BETA_ONE) * gradient
    square_new = BETA_TWO * square_old + (1.0 - BETA_TWO) * gradient * gradient
    mean_hat = mean_new / (1.0 - BETA_ONE**STEP)
    square_hat = square_new / (1.0 - BETA_TWO**STEP)
    master_new = master - rate * (mean_hat / (jnp.sqrt(square_hat) + ADAM_EPS) + DECAY * master)
    return (master_new, mean_new, square_new)


def step_rates():
    return (
        2.5 * (D // 4) ** (-0.5),
        2.5 * D ** (-0.5),
        2.5 * (H * DH // 32) ** (-0.5),
        2.5 * D ** (-0.5),
        2.5 * FF ** (-0.5),
        0.5,
    )


def rotated(pair, cos_t, sin_t):
    u = pair[: DH // 2]
    w = pair[DH // 2 :]
    return jnp.concatenate([u * cos_t - w * sin_t, w * cos_t + u * sin_t], axis=0)


def unrotated(pair, cos_t, sin_t):
    u = pair[: DH // 2]
    w = pair[DH // 2 :]
    return jnp.concatenate([u * cos_t + w * sin_t, w * cos_t - u * sin_t], axis=0)


def prologue_body(f_ref, cos_ref, sin_ref, q_ref, fac_ref):
    cos_t = cos_ref[...]
    sin_t = sin_ref[...]
    base = H * RA
    bq = [
        rotated(f_ref[0, base + r * DH : base + (r + 1) * DH, :], cos_t, sin_t) for r in range(RQ)
    ]
    for pair in range(H // 2):
        parts = []
        for h in (2 * pair, 2 * pair + 1):
            acc = f_ref[0, h * RA : h * RA + 1, :] * bq[0]
            for r in range(1, RQ):
                acc = acc + f_ref[0, h * RA + r : h * RA + r + 1, :] * bq[r]
            parts.append(acc)
        both = jnp.concatenate(parts, axis=0) / RQ
        rows = jnp.transpose(both).astype(BF) * SCALE
        q_ref[0, :, pair * 2 * DH : (pair + 1) * 2 * DH] = rows.astype(BF)
    for r in range(RK):
        at = base + (RQ + r) * DH
        fac_ref[0, r * 2 * DH : r * 2 * DH + DH, :] = rotated(
            f_ref[0, at : at + DH, :], cos_t, sin_t
        ).astype(BF)
        at = base + (RQ + RK + r) * DH
        fac_ref[0, r * 2 * DH + DH : (r + 1) * 2 * DH, :] = f_ref[0, at : at + DH, :].astype(BF)
    rows = [f_ref[0, h * RA + RQ : (h + 1) * RA, :] for h in range(H)]
    fac_ref[0, RK * 2 * DH :, :] = (jnp.concatenate(rows, axis=0) * (1.0 / RK)).astype(BF)


FAC = RK * 2 * DH + 2 * RK * H


def prologue(factors, cos_t, sin_t):
    count, width, block = factors.shape
    return pl.pallas_call(
        prologue_body,
        grid=(count,),
        in_specs=[
            pl.BlockSpec((1, width, block), lambda s: (s, 0, 0)),
            pl.BlockSpec((DH // 2, block), lambda s: (0, 0)),
            pl.BlockSpec((DH // 2, block), lambda s: (0, 0)),
        ],
        out_specs=[
            pl.BlockSpec((1, block, H * DH), lambda s: (s, 0, 0)),
            pl.BlockSpec((1, FAC, block), lambda s: (s, 0, 0)),
        ],
        out_shape=[
            jax.ShapeDtypeStruct((count, block, H * DH), BF),
            jax.ShapeDtypeStruct((count, FAC, block), BF),
        ],
        name="factor_prologue",
    )(factors, cos_t, sin_t)


def epilogue_body(dq_ref, df_ref, f_ref, cos_ref, sin_ref, g_ref):
    cos_t = cos_ref[...]
    sin_t = sin_ref[...]
    base = H * RA
    bq = [
        rotated(f_ref[0, base + r * DH : base + (r + 1) * DH, :], cos_t, sin_t) for r in range(RQ)
    ]
    sums = [None] * RQ
    rows = []
    wide = RK * 2 * DH
    for pair in range(H // 2):
        both = jnp.transpose(dq_ref[0, :, pair * 2 * DH : (pair + 1) * 2 * DH])
        for k in range(2):
            h = 2 * pair + k
            dq = both[k * DH : (k + 1) * DH] * (1.0 / RQ)
            for r in range(RQ):
                rows.append(jnp.sum(dq * bq[r], axis=0, keepdims=True))
                term = f_ref[0, h * RA + r : h * RA + r + 1, :] * dq
                sums[r] = term if sums[r] is None else sums[r] + term
            rows.append(df_ref[0, wide + h * 2 * RK : wide + (h + 1) * 2 * RK, :].astype(F32))
    g_ref[0, :base, :] = jnp.concatenate(rows, axis=0).astype(BF)
    for r in range(RQ):
        g_ref[0, base + r * DH : base + (r + 1) * DH, :] = unrotated(sums[r], cos_t, sin_t).astype(BF)
    for r in range(RK):
        at = base + (RQ + r) * DH
        part = df_ref[0, r * 2 * DH : (r + 1) * 2 * DH, :].astype(F32)
        g_ref[0, at : at + DH, :] = unrotated(part[:DH], cos_t, sin_t).astype(BF)
        at = base + (RQ + RK + r) * DH
        g_ref[0, at : at + DH, :] = part[DH:].astype(BF)


def epilogue(query_grad, factor_grad, factors, cos_t, sin_t):
    count, width, block = factors.shape
    return pl.pallas_call(
        epilogue_body,
        grid=(count,),
        in_specs=[
            pl.BlockSpec((1, block, H * DH), lambda s: (s, 0, 0)),
            pl.BlockSpec((1, FAC, block), lambda s: (s, 0, 0)),
            pl.BlockSpec((1, width, block), lambda s: (s, 0, 0)),
            pl.BlockSpec((DH // 2, block), lambda s: (0, 0)),
            pl.BlockSpec((DH // 2, block), lambda s: (0, 0)),
        ],
        out_specs=pl.BlockSpec((1, width, block), lambda s: (s, 0, 0)),
        out_shape=jax.ShapeDtypeStruct((count, width, block), BF),
        name="factor_epilogue",
    )(query_grad, factor_grad, factors, cos_t, sin_t)


def keys_values(a_rows, b_rows, h):
    a = a_rows[4 * h : 4 * h + 4]
    key_t = a[0:1] * b_rows[:DH] + a[1:2] * b_rows[2 * DH : 3 * DH]
    value_t = a[2:3] * b_rows[DH : 2 * DH] + a[3:4] * b_rows[3 * DH :]
    return key_t.astype(BF), value_t.astype(BF)


NT = (((1,), (1,)), ((), ()))
TN = (((0,), (0,)), ((), ()))


def forward_body(q_ref, b_ref, a_ref, kpos_ref, qpos_ref, o_ref, lse_ref):
    allowed = kpos_ref[...] <= qpos_ref[...]
    b_rows = b_ref[0].astype(F32)
    a_rows = a_ref[0].astype(F32)
    outs = []
    stats = []
    for h in range(HB):
        key_t, value_t = keys_values(a_rows, b_rows, h)
        scores = jnp.dot(q_ref[0, :, h * DH : (h + 1) * DH], key_t, preferred_element_type=F32)
        scores = jnp.where(allowed, scores, NEGATIVE)
        best = jnp.max(scores, axis=1, keepdims=True)
        probs = jnp.exp(scores - best)
        total = jnp.sum(probs, axis=1, keepdims=True)
        part = lax.dot_general(probs.astype(BF), value_t, NT, preferred_element_type=F32)
        outs.append(part / total)
        stats.append(best + jnp.log(total))
    o_ref[0] = jnp.concatenate(outs, axis=1)
    lse_ref[0, 0] = jnp.concatenate(stats, axis=1)


def attention_forward(query, gathered, key_pos, query_pos):
    count, block, width = query.shape
    length = gathered.shape[2]
    wide = RK * 2 * DH
    return pl.pallas_call(
        forward_body,
        grid=(count, H // HB),
        in_specs=[
            pl.BlockSpec((1, block, HB * DH), lambda s, g: (s, 0, g)),
            pl.BlockSpec((1, wide, length), lambda s, g: (s, 0, 0)),
            pl.BlockSpec((1, 4 * HB, length), lambda s, g: (s, wide // (4 * HB) + g, 0)),
            pl.BlockSpec((1, length), lambda s, g: (0, 0)),
            pl.BlockSpec((block, 1), lambda s, g: (0, 0)),
        ],
        out_specs=[
            pl.BlockSpec((1, block, HB * DH), lambda s, g: (s, 0, g)),
            pl.BlockSpec((1, 1, block, HB), lambda s, g: (s, g, 0, 0)),
        ],
        out_shape=[
            jax.ShapeDtypeStruct((count, block, width), F32),
            jax.ShapeDtypeStruct((count, H // HB, block, HB), F32),
        ],
        name="attention_forward",
    )(query, gathered, gathered, key_pos, query_pos)


def backward_body(
    q_ref, do_ref, o_ref, lse_ref, b_ref, a_ref, kpos_ref, qpos_ref, dq_ref, db_ref, da_ref, acc_ref
):
    group = pl.program_id(1)

    @pl.when(group == 0)
    def _():
        acc_ref[...] = jnp.zeros_like(acc_ref)

    allowed = kpos_ref[...] <= qpos_ref[...]
    b_rows = b_ref[0].astype(F32)
    a_rows = a_ref[0].astype(F32)
    lse = lse_ref[0, 0]
    dqs = []
    rows = []
    for h in range(HB):
        key_t, value_t = keys_values(a_rows, b_rows, h)
        q = q_ref[0, :, h * DH : (h + 1) * DH]
        do = do_ref[0, :, h * DH : (h + 1) * DH]
        delta = jnp.sum(do.astype(F32) * o_ref[0, :, h * DH : (h + 1) * DH], axis=1, keepdims=True)
        scores = jnp.dot(q, key_t, preferred_element_type=F32)
        probs = jnp.exp(jnp.where(allowed, scores - lse[:, h : h + 1], NEGATIVE))
        prob_grad = jnp.dot(do, value_t, preferred_element_type=F32)
        score_grad = (probs * (prob_grad - delta)).astype(BF)
        dqs.append(lax.dot_general(score_grad, key_t, NT, preferred_element_type=F32) * SCALE)
        dk = lax.dot_general(q, score_grad, TN, preferred_element_type=F32)
        dv = lax.dot_general(do, probs.astype(BF), TN, preferred_element_type=F32)
        a = a_rows[4 * h : 4 * h + 4]
        acc_ref[:DH] += a[0:1] * dk
        acc_ref[DH : 2 * DH] += a[2:3] * dv
        acc_ref[2 * DH : 3 * DH] += a[1:2] * dk
        acc_ref[3 * DH :] += a[3:4] * dv
        rows.append(jnp.sum(dk * b_rows[:DH], axis=0, keepdims=True))
        rows.append(jnp.sum(dk * b_rows[2 * DH : 3 * DH], axis=0, keepdims=True))
        rows.append(jnp.sum(dv * b_rows[DH : 2 * DH], axis=0, keepdims=True))
        rows.append(jnp.sum(dv * b_rows[3 * DH :], axis=0, keepdims=True))
    dq_ref[0] = jnp.concatenate(dqs, axis=1)
    da_ref[0] = (jnp.concatenate(rows, axis=0) * (1.0 / RK)).astype(BF)

    @pl.when(group == pl.num_programs(1) - 1)
    def _():
        db_ref[0] = acc_ref[...].astype(BF)


def attention_backward(query, heads_grad, heads_wide, lse, gathered, key_pos, query_pos):
    count, block, width = query.shape
    length = gathered.shape[2]
    wide = RK * 2 * DH
    return pl.pallas_call(
        backward_body,
        grid=(count, H // HB),
        in_specs=[
            pl.BlockSpec((1, block, HB * DH), lambda s, g: (s, 0, g)),
            pl.BlockSpec((1, block, HB * DH), lambda s, g: (s, 0, g)),
            pl.BlockSpec((1, block, HB * DH), lambda s, g: (s, 0, g)),
            pl.BlockSpec((1, 1, block, HB), lambda s, g: (s, g, 0, 0)),
            pl.BlockSpec((1, wide, length), lambda s, g: (s, 0, 0)),
            pl.BlockSpec((1, 4 * HB, length), lambda s, g: (s, wide // (4 * HB) + g, 0)),
            pl.BlockSpec((1, length), lambda s, g: (0, 0)),
            pl.BlockSpec((block, 1), lambda s, g: (0, 0)),
        ],
        out_specs=[
            pl.BlockSpec((1, block, HB * DH), lambda s, g: (s, 0, g)),
            pl.BlockSpec((1, wide, length), lambda s, g: (s, 0, 0)),
            pl.BlockSpec((1, 4 * HB, length), lambda s, g: (s, g, 0)),
        ],
        out_shape=[
            jax.ShapeDtypeStruct((count, block, width), F32),
            jax.ShapeDtypeStruct((count, wide, length), BF),
            jax.ShapeDtypeStruct((count, 4 * H, length), BF),
        ],
        scratch_shapes=[pltpu.VMEM((wide, length), F32)],
        name="attention_backward",
    )(query, heads_grad, heads_wide, lse, gathered, gathered, key_pos, query_pos)


def swap(block, axis):
    return lax.ppermute(block, axis, [(0, 1), (1, 0)])


def turn_core_head(block):
    return lax.ppermute(block, ("c", "h"), [(0, 0), (1, 2), (2, 1), (3, 3)])


def sum_over_head(block, n_head):
    if n_head == 2:
        return block + swap(block, "h")
    return lax.psum(block, "h")


def share_over_head(block, n_head):
    if n_head == 2:
        other = swap(block, "h")
        mine = lax.axis_index("h") == 0
        first = jnp.where(mine, block, other)
        second = jnp.where(mine, other, block)
        return jnp.concatenate([first, second], axis=0)
    return lax.all_gather(block, "h", axis=0, tiled=True)


def on_device(
    tokens,
    cotangent,
    domain_ids,
    block_order,
    headwise,
    headwise_mean,
    headwise_square,
    shared_factors,
    shared_factors_mean,
    shared_factors_square,
    out_weight,
    out_weight_mean,
    out_weight_square,
    gate_up,
    gate_up_mean,
    gate_up_square,
    down_weight,
    down_weight_mean,
    down_weight_square,
    norm_gains,
    norm_gains_mean,
    norm_gains_square,
):
    n_head = lax.axis_size("h")
    n_seq = lax.axis_size(SEQ)
    paired = n_head == 2
    seq_at = lax.axis_index(SEQ)
    head_at = lax.axis_index("h")
    seq_all, block_len, _ = tokens.shape
    count = seq_all // n_head
    rows = D // n_seq
    o_cols = H * DH // n_head
    h_cols = H * RA // n_head
    s_cols = RA * DH // n_head
    f_cols = FF // n_head

    out_t = out_weight.T.astype(BF)
    shared_part = lax.dynamic_slice_in_dim(shared_factors, head_at * s_cols, s_cols, 1).astype(BF)
    small = jnp.concatenate(
        [out_t, headwise.astype(BF), shared_part, norm_gains.T.astype(BF)], axis=1
    )
    small_all = lax.all_gather(small, SEQ + ("h",), axis=0)
    small_all = small_all.reshape(n_seq, n_head, rows, small.shape[1]).transpose(0, 2, 1, 3)
    small_all = small_all.reshape(D, n_head, small.shape[1])
    w_out_t = small_all[:, :, :o_cols].reshape(D, H * DH)
    w_heads = small_all[:, :, o_cols : o_cols + h_cols].reshape(D, H * RA)
    w_shared = small_all[:, :, o_cols + h_cols : o_cols + h_cols + s_cols].reshape(D, RA * DH)
    w_factors = jnp.concatenate([w_heads, w_shared], axis=1)
    gains_low = small_all[:, 0, o_cols + h_cols + s_cols :].T.astype(F32)
    gain_first = gains_low[0]
    gain_second = gains_low[1]

    wide_part = jnp.concatenate(
        [gate_up[0].astype(BF), gate_up[1].astype(BF), down_weight.T.astype(BF)], axis=1
    )
    if paired:
        wide_part = turn_core_head(wide_part)
        wide_all = lax.all_gather(wide_part, ("a", "b", "h"), axis=0, tiled=True)
        w_gate = wide_all[:, :f_cols]
        w_up = wide_all[:, f_cols : 2 * f_cols]
        w_down_t = wide_all[:, 2 * f_cols :]
    else:
        wide_all = lax.all_gather(wide_part, SEQ + ("h",), axis=0)
        wide_all = wide_all.reshape(n_seq, n_head, rows, 3, f_cols).transpose(3, 0, 2, 1, 4)
        wide_all = wide_all.reshape(3, D, FF)
        w_gate, w_up, w_down_t = wide_all[0], wide_all[1], wide_all[2]

    spots = jnp.arange(n_seq, dtype=jnp.int32)
    own_block = jnp.sum(jnp.where(spots == seq_at, block_order, 0))
    offsets = jnp.arange(block_len, dtype=jnp.int32)
    query_pos = own_block * block_len + offsets
    key_pos = (block_order[:, None] * block_len + offsets[None, :]).reshape(1, n_seq * block_len)
    cos_t, sin_t = rope_tables(query_pos)

    tok = lax.dynamic_slice_in_dim(tokens, head_at * count, count, 0).astype(F32)
    cot = lax.dynamic_slice_in_dim(cotangent, head_at * count, count, 0).astype(F32)
    same_domain = (domain_ids[:, None] == domain_ids[None, :]).astype(F32)
    seq_weight = lax.dynamic_slice_in_dim(1.0 / jnp.sum(same_domain, axis=1), head_at * count, count, 0)
    out_grad = cot * seq_weight[:, None, None]
    out_low = out_grad.astype(BF)

    first_hat, first_inverse = normalize(tok)
    first_normalized = (first_hat * gain_first).astype(BF)
    factors = jnp.einsum("scd,dj->sjc", first_normalized, w_factors, preferred_element_type=F32)
    query, own_factors = prologue(factors, cos_t, sin_t)
    gathered = lax.all_gather(own_factors, SEQ, axis=2, tiled=True)
    heads_wide, lse = attention_forward(query, gathered, key_pos, query_pos[:, None])
    heads_low = heads_wide.astype(BF)
    attn = jnp.einsum("sce,de->scd", heads_low, w_out_t, preferred_element_type=F32)
    middle = tok + attn
    second_hat, second_inverse = normalize(middle)
    second_normalized = (second_hat * gain_second).astype(BF)

    tokens_own = count * block_len

    def both_cores(block):
        flat = block.reshape(tokens_own, D)
        if paired:
            return jnp.concatenate([flat, swap(flat, "c")], axis=0)
        return flat

    def own_sum(partial):
        if paired:
            partial = partial[:tokens_own] + swap(partial[tokens_own:].astype(BF), "c").astype(F32)
        return partial.reshape(count, block_len, D)

    x_low = both_cores(second_normalized)
    y_low = both_cores(out_low)
    gate = jnp.dot(x_low, w_gate, preferred_element_type=F32)
    up = jnp.dot(x_low, w_up, preferred_element_type=F32)
    sigmoid_gate = jax.nn.sigmoid(gate)
    silu_gate = gate * sigmoid_gate
    hidden_low = (silu_gate * up).astype(BF)
    ffn = own_sum(jnp.einsum("tf,df->td", hidden_low, w_down_t, preferred_element_type=F32))
    layer_output = share_over_head((middle + ffn).astype(BF), n_head)

    hidden_grad = jnp.dot(y_low, w_down_t, preferred_element_type=F32)
    up_grad = (hidden_grad * silu_gate).astype(BF)
    gate_grad = (
        hidden_grad * up * (sigmoid_gate * (1.0 + gate * (1.0 - sigmoid_gate)))
    ).astype(BF)
    down_t_grad = jnp.einsum("td,tf->df", y_low, hidden_low, preferred_element_type=F32)
    gate_w_grad = jnp.einsum("td,tf->df", x_low, gate_grad, preferred_element_type=F32)
    up_w_grad = jnp.einsum("td,tf->df", x_low, up_grad, preferred_element_type=F32)
    second_part = jnp.einsum("tf,df->td", gate_grad, w_gate, preferred_element_type=F32)
    second_part = second_part + jnp.einsum("tf,df->td", up_grad, w_up, preferred_element_type=F32)
    second_grad = own_sum(second_part)

    wide_grad = jnp.concatenate(
        [gate_w_grad.astype(BF), up_w_grad.astype(BF), down_t_grad.astype(BF)], axis=1
    )
    if paired:
        wide_sum = lax.psum_scatter(wide_grad, ("a", "b", "h"), scatter_dimension=0, tiled=True)
        wide_sum = turn_core_head(wide_sum).astype(F32).reshape(rows, 3, f_cols)
    else:
        wide_sum = lax.psum_scatter(wide_grad, SEQ, scatter_dimension=0, tiled=True)
        wide_sum = lax.psum(wide_sum, "h").reshape(rows, 3, n_head, f_cols)
        wide_sum = lax.dynamic_index_in_dim(wide_sum, head_at, 2, keepdims=False).astype(F32)

    second_gain_grad = jnp.sum(second_grad * second_hat, axis=(0, 1))
    middle_grad = out_grad + norm_back(second_grad, gain_second, second_hat, second_inverse)
    middle_low = middle_grad.astype(BF)
    out_t_grad = jnp.einsum("scd,sce->de", middle_low, heads_low, preferred_element_type=F32)
    heads_grad = jnp.einsum("scd,de->sce", middle_low, w_out_t, preferred_element_type=F32).astype(BF)

    query_grad, b_grad, a_grad = attention_backward(
        query, heads_grad, heads_wide, lse, gathered, key_pos, query_pos[:, None]
    )
    factor_grad = jnp.concatenate([b_grad, a_grad], axis=1)
    factor_grad = factor_grad.reshape(count, FAC, n_seq, block_len).transpose(2, 0, 1, 3)
    own_grad = lax.psum_scatter(factor_grad, SEQ, scatter_dimension=0, tiled=True)
    own_grad = own_grad.reshape(count, FAC, block_len)
    joint_grad = epilogue(query_grad, own_grad, factors, cos_t, sin_t)

    first_grad = jnp.einsum("sjc,dj->scd", joint_grad, w_factors, preferred_element_type=F32)
    factors_w_grad = jnp.einsum(
        "scd,sjc->dj", first_normalized, joint_grad, preferred_element_type=F32
    )
    first_gain_grad = jnp.sum(first_grad * first_hat, axis=(0, 1))
    input_grad = middle_grad + norm_back(first_grad, gain_first, first_hat, first_inverse)
    input_grad = share_over_head(input_grad.astype(BF), n_head).astype(F32)

    small_grad = jnp.concatenate(
        [
            out_t_grad.astype(BF),
            factors_w_grad.astype(BF),
            first_gain_grad[:, None].astype(BF),
            second_gain_grad[:, None].astype(BF),
        ],
        axis=1,
    )
    small_sum = lax.psum_scatter(small_grad, SEQ, scatter_dimension=0, tiled=True)
    small_sum = sum_over_head(small_sum, n_head).astype(F32)
    out_sum = lax.dynamic_slice_in_dim(small_sum, head_at * o_cols, o_cols, 1).T
    heads_sum = lax.dynamic_slice_in_dim(small_sum, H * DH + head_at * h_cols, h_cols, 1)
    shared_sum = small_sum[:, H * DH + H * RA : H * DH + H * RA + RA * DH]
    gains_sum = small_sum[:, H * DH + H * RA + RA * DH :].T
    gate_up_sum = jnp.stack([wide_sum[:, 0], wide_sum[:, 1]])
    down_sum = wide_sum[:, 2].T

    rates = step_rates()
    heads_new = adam_update(headwise, headwise_mean, headwise_square, heads_sum, rates[0])
    shared_new = adam_update(
        shared_factors, shared_factors_mean, shared_factors_square, shared_sum, rates[1]
    )
    out_new = adam_update(out_weight, out_weight_mean, out_weight_square, out_sum, rates[2])
    gate_new = adam_update(gate_up, gate_up_mean, gate_up_square, gate_up_sum, rates[3])
    down_new = adam_update(down_weight, down_weight_mean, down_weight_square, down_sum, rates[4])
    gains_new = adam_update(norm_gains, norm_gains_mean, norm_gains_square, gains_sum, rates[5])
    return (
        layer_output,
        input_grad,
        *heads_new,
        *shared_new,
        *out_new,
        *gate_new,
        *down_new,
        *gains_new,
    )


def solution(mesh):
    n_seq = mesh.shape["seq"]
    n_head = mesh.shape["head"]
    inner = max(1, n_seq // 8)
    fine = Mesh(mesh.devices.reshape(n_seq // 2 // inner, inner, 2, n_head), ("a", "b", "c", "h"))
    token = P(None, SEQ, None)
    heads = P(SEQ, "h")
    shared = P(SEQ, None)
    turned = P("h", SEQ)
    gates = P(None, SEQ, "h")
    gains = P(None, SEQ)
    weights = sum(([spec] * 3 for spec in (heads, shared, turned, gates, turned, gains)), [])
    return jax.shard_map(
        on_device,
        mesh=fine,
        in_specs=(token, token, P(), P(), *weights),
        out_specs=(token, token, *weights),
        check_vma=False,
    )
```

```python
import functools

import jax
import jax.numpy as jnp
from jax import lax
from jax.experimental import pallas as pl
from jax.experimental.pallas import tpu as pltpu
from jax.sharding import Mesh
from jax.sharding import PartitionSpec as P

D = 1024
H = 16
DH = 64
RQ = 6
RK = 2
RA = RQ + 2 * RK
FF = 2816
STEP = 10
HB = 4

EPSILON = 1e-05
BETA_ONE = 0.9
BETA_TWO = 0.95
ADAM_EPS = 1e-08
DECAY = 0.1
NEGATIVE = -1e30
SCALE = DH ** (-0.5)
BF = jnp.bfloat16
F32 = jnp.float32
SEQ = ("a", "b", "c")


def rope_tables(positions):
    half_dim = DH // 2
    frequency = 10000.0 ** (-(2.0 * jnp.arange(half_dim, dtype=F32)) / DH)
    angles = frequency[:, None] * positions.astype(F32)[None, :]
    return (jnp.cos(angles), jnp.sin(angles))


def normalize(row_data):
    inverse = lax.rsqrt(jnp.mean(row_data * row_data, -1, keepdims=True) + EPSILON)
    return (row_data * inverse, inverse)


def norm_back(normed_grad, gain_row, hat_rows, inverse):
    hat_grad = normed_grad * gain_row
    return inverse * (hat_grad - hat_rows * jnp.mean(hat_grad * hat_rows, -1, keepdims=True))


def adam_update(master, mean_old, square_old, gradient, rate):
    mean_new = BETA_ONE * mean_old + (1.0 - BETA_ONE) * gradient
    square_new = BETA_TWO * square_old + (1.0 - BETA_TWO) * gradient * gradient
    mean_hat = mean_new / (1.0 - BETA_ONE**STEP)
    square_hat = square_new / (1.0 - BETA_TWO**STEP)
    master_new = master - rate * (mean_hat / (jnp.sqrt(square_hat) + ADAM_EPS) + DECAY * master)
    return (master_new, mean_new, square_new)


def step_rates():
    return (
        2.5 * (D // 4) ** (-0.5),
        2.5 * D ** (-0.5),
        2.5 * (H * DH // 32) ** (-0.5),
        2.5 * D ** (-0.5),
        2.5 * FF ** (-0.5),
        0.5,
    )


def rotated(pair, cos_t, sin_t):
    u = pair[: DH // 2]
    w = pair[DH // 2 :]
    return jnp.concatenate([u * cos_t - w * sin_t, w * cos_t + u * sin_t], axis=0)


def unrotated(pair, cos_t, sin_t):
    u = pair[: DH // 2]
    w = pair[DH // 2 :]
    return jnp.concatenate([u * cos_t + w * sin_t, w * cos_t - u * sin_t], axis=0)


def prologue_body(f_ref, cos_ref, sin_ref, q_ref, fac_ref):
    cos_t = cos_ref[...]
    sin_t = sin_ref[...]
    base = H * RA
    bq = [
        rotated(f_ref[0, base + r * DH : base + (r + 1) * DH, :], cos_t, sin_t) for r in range(RQ)
    ]
    for pair in range(H // 2):
        parts = []
        for h in (2 * pair, 2 * pair + 1):
            acc = f_ref[0, h * RA : h * RA + 1, :] * bq[0]
            for r in range(1, RQ):
                acc = acc + f_ref[0, h * RA + r : h * RA + r + 1, :] * bq[r]
            parts.append(acc)
        both = jnp.concatenate(parts, axis=0) / RQ
        rows = jnp.transpose(both).astype(BF) * SCALE
        q_ref[0, :, pair * 2 * DH : (pair + 1) * 2 * DH] = rows.astype(BF)
    for r in range(RK):
        at = base + (RQ + r) * DH
        fac_ref[0, r * 2 * DH : r * 2 * DH + DH, :] = rotated(
            f_ref[0, at : at + DH, :], cos_t, sin_t
        ).astype(BF)
        at = base + (RQ + RK + r) * DH
        fac_ref[0, r * 2 * DH + DH : (r + 1) * 2 * DH, :] = f_ref[0, at : at + DH, :].astype(BF)
    rows = [f_ref[0, h * RA + RQ : (h + 1) * RA, :] for h in range(H)]
    fac_ref[0, RK * 2 * DH :, :] = (jnp.concatenate(rows, axis=0) * (1.0 / RK)).astype(BF)


FAC = RK * 2 * DH + 2 * RK * H


def prologue(factors, cos_t, sin_t):
    count, width, block = factors.shape
    return pl.pallas_call(
        prologue_body,
        grid=(count,),
        in_specs=[
            pl.BlockSpec((1, width, block), lambda s: (s, 0, 0)),
            pl.BlockSpec((DH // 2, block), lambda s: (0, 0)),
            pl.BlockSpec((DH // 2, block), lambda s: (0, 0)),
        ],
        out_specs=[
            pl.BlockSpec((1, block, H * DH), lambda s: (s, 0, 0)),
            pl.BlockSpec((1, FAC, block), lambda s: (s, 0, 0)),
        ],
        out_shape=[
            jax.ShapeDtypeStruct((count, block, H * DH), BF),
            jax.ShapeDtypeStruct((count, FAC, block), BF),
        ],
        name="factor_prologue",
    )(factors, cos_t, sin_t)


def epilogue_body(dq_ref, df_ref, f_ref, cos_ref, sin_ref, g_ref):
    cos_t = cos_ref[...]
    sin_t = sin_ref[...]
    base = H * RA
    bq = [
        rotated(f_ref[0, base + r * DH : base + (r + 1) * DH, :], cos_t, sin_t) for r in range(RQ)
    ]
    sums = [None] * RQ
    rows = []
    wide = RK * 2 * DH
    for pair in range(H // 2):
        both = jnp.transpose(dq_ref[0, :, pair * 2 * DH : (pair + 1) * 2 * DH])
        for k in range(2):
            h = 2 * pair + k
            dq = both[k * DH : (k + 1) * DH] * (1.0 / RQ)
            for r in range(RQ):
                rows.append(jnp.sum(dq * bq[r], axis=0, keepdims=True))
                term = f_ref[0, h * RA + r : h * RA + r + 1, :] * dq
                sums[r] = term if sums[r] is None else sums[r] + term
            rows.append(df_ref[0, wide + h * 2 * RK : wide + (h + 1) * 2 * RK, :].astype(F32))
    g_ref[0, :base, :] = jnp.concatenate(rows, axis=0).astype(BF)
    for r in range(RQ):
        g_ref[0, base + r * DH : base + (r + 1) * DH, :] = unrotated(sums[r], cos_t, sin_t).astype(BF)
    for r in range(RK):
        at = base + (RQ + r) * DH
        part = df_ref[0, r * 2 * DH : (r + 1) * 2 * DH, :].astype(F32)
        g_ref[0, at : at + DH, :] = unrotated(part[:DH], cos_t, sin_t).astype(BF)
        at = base + (RQ + RK + r) * DH
        g_ref[0, at : at + DH, :] = part[DH:].astype(BF)


def epilogue(query_grad, factor_grad, factors, cos_t, sin_t):
    count, width, block = factors.shape
    return pl.pallas_call(
        epilogue_body,
        grid=(count,),
        in_specs=[
            pl.BlockSpec((1, block, H * DH), lambda s: (s, 0, 0)),
            pl.BlockSpec((1, FAC, block), lambda s: (s, 0, 0)),
            pl.BlockSpec((1, width, block), lambda s: (s, 0, 0)),
            pl.BlockSpec((DH // 2, block), lambda s: (0, 0)),
            pl.BlockSpec((DH // 2, block), lambda s: (0, 0)),
        ],
        out_specs=pl.BlockSpec((1, width, block), lambda s: (s, 0, 0)),
        out_shape=jax.ShapeDtypeStruct((count, width, block), BF),
        name="factor_epilogue",
    )(query_grad, factor_grad, factors, cos_t, sin_t)


def keys_values(a_rows, b_rows, h):
    a = a_rows[4 * h : 4 * h + 4]
    key_t = a[0:1] * b_rows[:DH] + a[1:2] * b_rows[2 * DH : 3 * DH]
    value_t = a[2:3] * b_rows[DH : 2 * DH] + a[3:4] * b_rows[3 * DH :]
    return key_t.astype(BF), value_t.astype(BF)


NT = (((1,), (1,)), ((), ()))
TN = (((0,), (0,)), ((), ()))


def forward_body(q_ref, b_ref, a_ref, kpos_ref, qpos_ref, o_ref, lse_ref):
    allowed = kpos_ref[...] <= qpos_ref[...]
    b_rows = b_ref[0].astype(F32)
    a_rows = a_ref[0].astype(F32)
    outs = []
    stats = []
    for h in range(HB):
        key_t, value_t = keys_values(a_rows, b_rows, h)
        scores = jnp.dot(q_ref[0, :, h * DH : (h + 1) * DH], key_t, preferred_element_type=F32)
        scores = jnp.where(allowed, scores, NEGATIVE)
        best = jnp.max(scores, axis=1, keepdims=True)
        probs = jnp.exp(scores - best)
        total = jnp.sum(probs, axis=1, keepdims=True)
        part = lax.dot_general(probs.astype(BF), value_t, NT, preferred_element_type=F32)
        outs.append(part / total)
        stats.append(best + jnp.log(total))
    o_ref[0] = jnp.concatenate(outs, axis=1)
    lse_ref[0, 0] = jnp.concatenate(stats, axis=1)


def attention_forward(query, gathered, key_pos, query_pos):
    count, block, width = query.shape
    length = gathered.shape[2]
    wide = RK * 2 * DH
    return pl.pallas_call(
        forward_body,
        grid=(count, H // HB),
        in_specs=[
            pl.BlockSpec((1, block, HB * DH), lambda s, g: (s, 0, g)),
            pl.BlockSpec((1, wide, length), lambda s, g: (s, 0, 0)),
            pl.BlockSpec((1, 4 * HB, length), lambda s, g: (s, wide // (4 * HB) + g, 0)),
            pl.BlockSpec((1, length), lambda s, g: (0, 0)),
            pl.BlockSpec((block, 1), lambda s, g: (0, 0)),
        ],
        out_specs=[
            pl.BlockSpec((1, block, HB * DH), lambda s, g: (s, 0, g)),
            pl.BlockSpec((1, 1, block, HB), lambda s, g: (s, g, 0, 0)),
        ],
        out_shape=[
            jax.ShapeDtypeStruct((count, block, width), F32),
            jax.ShapeDtypeStruct((count, H // HB, block, HB), F32),
        ],
        name="attention_forward",
    )(query, gathered, gathered, key_pos, query_pos)


def backward_body(
    q_ref, do_ref, o_ref, lse_ref, b_ref, a_ref, kpos_ref, qpos_ref, dq_ref, *refs
):
    piece_refs, acc_ref = refs[:-1], refs[-1]
    group = pl.program_id(1)
    wide = RK * 2 * DH

    @pl.when(group == 0)
    def _():
        acc_ref[...] = jnp.zeros_like(acc_ref)

    allowed = kpos_ref[...] <= qpos_ref[...]
    b_rows = b_ref[0].astype(F32)
    a_rows = a_ref[0].astype(F32)
    lse = lse_ref[0, 0]
    dqs = []
    rows = []
    for h in range(HB):
        key_t, value_t = keys_values(a_rows, b_rows, h)
        q = q_ref[0, :, h * DH : (h + 1) * DH]
        do = do_ref[0, :, h * DH : (h + 1) * DH]
        delta = jnp.sum(do.astype(F32) * o_ref[0, :, h * DH : (h + 1) * DH], axis=1, keepdims=True)
        scores = jnp.dot(q, key_t, preferred_element_type=F32)
        probs = jnp.exp(jnp.where(allowed, scores - lse[:, h : h + 1], NEGATIVE))
        prob_grad = jnp.dot(do, value_t, preferred_element_type=F32)
        score_grad = (probs * (prob_grad - delta)).astype(BF)
        dqs.append(lax.dot_general(score_grad, key_t, NT, preferred_element_type=F32) * SCALE)
        dk = lax.dot_general(q, score_grad, TN, preferred_element_type=F32)
        dv = lax.dot_general(do, probs.astype(BF), TN, preferred_element_type=F32)
        a = a_rows[4 * h : 4 * h + 4]
        acc_ref[:DH] += a[0:1] * dk
        acc_ref[DH : 2 * DH] += a[2:3] * dv
        acc_ref[2 * DH : 3 * DH] += a[1:2] * dk
        acc_ref[3 * DH :] += a[3:4] * dv
        rows.append(jnp.sum(dk * b_rows[:DH], axis=0, keepdims=True))
        rows.append(jnp.sum(dk * b_rows[2 * DH : 3 * DH], axis=0, keepdims=True))
        rows.append(jnp.sum(dv * b_rows[DH : 2 * DH], axis=0, keepdims=True))
        rows.append(jnp.sum(dv * b_rows[3 * DH :], axis=0, keepdims=True))
    dq_ref[0] = jnp.concatenate(dqs, axis=1)
    a_grad = (jnp.concatenate(rows, axis=0) * (1.0 / RK)).astype(BF)
    block = piece_refs[0].shape[3]
    depth = piece_refs[0].shape[0]
    at = pl.multiple_of(wide + group * 4 * HB, 4 * HB)
    for i, ref in enumerate(piece_refs):
        for m in range(depth):
            lanes = (i * depth + m) * block
            ref[m, 0, pl.ds(at, 4 * HB), :] = a_grad[:, lanes : lanes + block]

    @pl.when(group == pl.num_programs(1) - 1)
    def _():
        for i, ref in enumerate(piece_refs):
            for m in range(depth):
                lanes = (i * depth + m) * block
                ref[m, 0, :wide, :] = acc_ref[:, lanes : lanes + block].astype(BF)


def attention_backward(query, heads_grad, heads_wide, lse, gathered, key_pos, query_pos, depth):
    count, block, width = query.shape
    length = gathered.shape[2]
    wide = RK * 2 * DH
    pieces = length // (depth * block)
    return pl.pallas_call(
        backward_body,
        grid=(count, H // HB),
        in_specs=[
            pl.BlockSpec((1, block, HB * DH), lambda s, g: (s, 0, g)),
            pl.BlockSpec((1, block, HB * DH), lambda s, g: (s, 0, g)),
            pl.BlockSpec((1, block, HB * DH), lambda s, g: (s, 0, g)),
            pl.BlockSpec((1, 1, block, HB), lambda s, g: (s, g, 0, 0)),
            pl.BlockSpec((1, wide, length), lambda s, g: (s, 0, 0)),
            pl.BlockSpec((1, 4 * HB, length), lambda s, g: (s, wide // (4 * HB) + g, 0)),
            pl.BlockSpec((1, length), lambda s, g: (0, 0)),
            pl.BlockSpec((block, 1), lambda s, g: (0, 0)),
        ],
        out_specs=[pl.BlockSpec((1, block, HB * DH), lambda s, g: (s, 0, g))]
        + [pl.BlockSpec((depth, 1, FAC, block), lambda s, g: (0, s, 0, 0))] * pieces,
        out_shape=[jax.ShapeDtypeStruct((count, block, width), F32)]
        + [jax.ShapeDtypeStruct((depth, count, FAC, block), BF)] * pieces,
        scratch_shapes=[pltpu.VMEM((wide, length), F32)],
        name="attention_backward",
    )(query, heads_grad, heads_wide, lse, gathered, gathered, key_pos, query_pos)


def swap(block, axis):
    return lax.ppermute(block, axis, [(0, 1), (1, 0)])


def turn_core_head(block):
    return lax.ppermute(block, ("c", "h"), [(0, 0), (1, 2), (2, 1), (3, 3)])


def from_ahead(block, axis, distance):
    size = lax.axis_size(axis)
    return lax.ppermute(block, axis, [((i + distance) % size, i) for i in range(size)])


def to_ahead(block, axis, distance):
    size = lax.axis_size(axis)
    return lax.ppermute(block, axis, [(i, (i + distance) % size) for i in range(size)])


def ordered_gather(block, axis):
    size = lax.axis_size(axis)
    spot = lax.axis_index(axis)
    if size == 2:
        other = swap(block, axis)
        mine = spot == 0
        return jnp.stack([jnp.where(mine, block, other), jnp.where(mine, other, block)])
    parts = [block] + [from_ahead(block, axis, m) for m in range(1, size)]
    twice = jnp.stack(parts + parts[:-1])
    return lax.dynamic_slice_in_dim(twice, jnp.mod(size - spot, size), size, 0)


def ordered_scatter(block, axis, dim):
    size = lax.axis_size(axis)
    spot = lax.axis_index(axis)

    def part(m):
        return lax.dynamic_index_in_dim(block, jnp.mod(spot + m, size), dim, keepdims=False)

    total = part(0).astype(F32)
    for m in range(1, size):
        total = total + to_ahead(part(m), axis, m).astype(F32)
    return total.astype(BF)


def gather_blocks(block):
    order = {}
    for ma in range(lax.axis_size("a")):
        at_a = from_ahead(block, "a", ma) if ma else block
        for mb in range(lax.axis_size("b")):
            at_b = from_ahead(at_a, "b", mb) if mb else at_a
            order[0, mb, ma] = at_b
            order[1, mb, ma] = swap(at_b, "c")
    return [order[key] for key in sorted(order)]


def blocks_ahead():
    na, nb = lax.axis_size("a"), lax.axis_size("b")
    at = [lax.axis_index(name) for name in SEQ]
    spots = []
    for mc in range(2):
        for mb in range(nb):
            for ma in range(na):
                a = jnp.mod(at[0] + ma, na)
                b = jnp.mod(at[1] + mb, nb)
                spots.append((a * nb + b) * 2 + jnp.mod(at[2] + mc, 2))
    return jnp.stack(spots)


def scatter_blocks(pieces):
    na, nb = lax.axis_size("a"), lax.axis_size("b")
    after_core = []
    for mb in range(nb):
        other = swap(pieces[nb + mb], "c")
        after_core.append((pieces[mb].astype(F32) + other.astype(F32)).astype(BF))
    moved = [to_ahead(after_core[mb], "b", mb) for mb in range(1, nb)]
    total = None
    for ma in range(na):
        part = after_core[0][ma].astype(F32)
        for block in moved:
            part = part + block[ma].astype(F32)
        if ma:
            part = to_ahead(part.astype(BF), "a", ma).astype(F32)
        total = part if total is None else total + part
    return total


def place_body(at_ref, t1, r1, t2, r2, out_ref, sems):
    depth = t1.shape[1]
    copies = []
    for m in range(depth):
        z = lax.rem(at_ref[0] + m, depth)
        for i in range(2):
            for j in range(2):
                x = lax.rem(at_ref[1] + i, 2)
                y = lax.rem(at_ref[2] + j, 2)
                first = (r1 if j else t1).at[i, m]
                second = (r2 if i else t2).at[j, m]
                copies.append((first, out_ref.at[z, x, y, 0]))
                copies.append((second, out_ref.at[z, x, y, 1]))
    copies = [pltpu.make_async_copy(a, b, sems.at[n]) for n, (a, b) in enumerate(copies)]
    for copy in copies:
        copy.start()
    for copy in copies:
        copy.wait()


def place(t1, r1, t2, r2):
    _, depth, part, cols = t1.shape
    at = jnp.stack([lax.axis_index(name) for name in ("a", "b", "h")]).astype(jnp.int32)
    out = pl.pallas_call(
        place_body,
        grid_spec=pltpu.PrefetchScalarGridSpec(
            num_scalar_prefetch=1,
            grid=(1,),
            in_specs=[pl.BlockSpec(memory_space=pl.ANY)] * 4,
            out_specs=pl.BlockSpec(memory_space=pl.ANY),
            scratch_shapes=[pltpu.SemaphoreType.DMA((8 * depth,))],
        ),
        out_shape=jax.ShapeDtypeStruct((depth, 2, 2, 2, part, cols), t1.dtype),
        name="place_rows",
    )(at, t1, r1, t2, r2)
    return out.reshape(depth * 8 * part, cols)


def bulk_gather(block):
    part = block.shape[0] // 2
    parts = [block] + [from_ahead(block, "a", m) for m in range(1, lax.axis_size("a"))]
    low = jnp.stack([p[:part] for p in parts])
    high = jnp.stack([p[part:] for p in parts])
    t1 = jnp.stack([low, swap(low, "b")])
    t2 = jnp.stack([high, swap(high, "h")])
    return place(t1, swap(t1, "h"), t2, swap(t2, "b"))


def bulk_scatter(grad):
    na = lax.axis_size("a")
    part = grad.shape[0] // (8 * na)
    cols = grad.shape[1]
    a, b, h = (lax.axis_index(name) for name in ("a", "b", "h"))
    grad = grad.reshape(na, 2, 2, 2, part, cols)

    def take(block, spot, dim):
        return lax.dynamic_index_in_dim(block, spot, dim, keepdims=False)

    def fold(block, axis, spot, dim):
        other = swap(take(block, 1 - spot, dim), axis)
        return (take(block, spot, dim).astype(F32) + other.astype(F32)).astype(BF)

    low = fold(fold(grad[:, :, :, 0], "h", h, 2), "b", b, 1)
    high = fold(fold(grad[:, :, :, 1], "b", b, 1), "h", h, 1)
    both = jnp.concatenate([low, high], axis=1)
    total = take(both, a, 0).astype(F32)
    for m in range(1, na):
        total = total + to_ahead(take(both, jnp.mod(a + m, na), 0), "a", m).astype(F32)
    return turn_core_head(total.astype(BF)).astype(F32)


def sum_over_head(block, n_head):
    if n_head == 2:
        return block + swap(block, "h")
    return lax.psum(block, "h")


def in_core_order(own, other, axis):
    first = lax.axis_index("c") == 0
    return jnp.concatenate([jnp.where(first, own, other), jnp.where(first, other, own)], axis=axis)


def share_over_head(block, n_head):
    if n_head == 2:
        other = swap(block, "h")
        mine = lax.axis_index("h") == 0
        first = jnp.where(mine, block, other)
        second = jnp.where(mine, other, block)
        return jnp.concatenate([first, second], axis=0)
    return lax.all_gather(block, "h", axis=0, tiled=True)


def on_device(
    tokens,
    cotangent,
    domain_ids,
    block_order,
    headwise,
    headwise_mean,
    headwise_square,
    shared_factors,
    shared_factors_mean,
    shared_factors_square,
    out_weight,
    out_weight_mean,
    out_weight_square,
    gate_up,
    gate_up_mean,
    gate_up_square,
    down_weight,
    down_weight_mean,
    down_weight_square,
    norm_gains,
    norm_gains_mean,
    norm_gains_square,
):
    n_head = lax.axis_size("h")
    n_seq = lax.axis_size(SEQ)
    paired = n_head == 2 and lax.axis_size("b") == 2
    seq_at = lax.axis_index(SEQ)
    head_at = lax.axis_index("h")
    seq_all, block_len, _ = tokens.shape
    count = seq_all // n_head
    rows = D // n_seq
    o_cols = H * DH // n_head
    h_cols = H * RA // n_head
    s_cols = RA * DH // n_head
    f_cols = FF // n_head

    shared_part = lax.dynamic_slice_in_dim(shared_factors, head_at * s_cols, s_cols, 1)
    small = jnp.concatenate([headwise, shared_part, norm_gains.T], axis=1).astype(BF)
    for name in ("a", "b", "c"):
        small = ordered_gather(small, name)
    if paired:
        small = ordered_gather(small, "h")
    else:
        small = lax.all_gather(small, "h", axis=0)
    small = small.transpose(3, 2, 1, 4, 0, 5).reshape(D, n_head, h_cols + s_cols + 2)
    w_heads = small[:, :, :h_cols].reshape(D, H * RA)
    w_shared = small[:, :, h_cols : h_cols + s_cols].reshape(D, RA * DH)
    w_factors = jnp.concatenate([w_heads, w_shared], axis=1)
    gains_low = small[:, 0, h_cols + s_cols :].T.astype(F32)
    gain_first = gains_low[0]
    gain_second = gains_low[1]

    wide_parts = [
        part.astype(BF) for part in (out_weight.T, gate_up[0], gate_up[1], down_weight.T)
    ]
    if paired:
        wide_parts = [turn_core_head(part) for part in wide_parts]
        own_out, w_gate, w_up, w_down_t = [bulk_gather(part) for part in wide_parts]
        w_out_t = in_core_order(own_out, swap(own_out, "c"), 1)
    else:
        wide_part = jnp.concatenate(wide_parts, axis=1)
        wide_all = lax.all_gather(wide_part, SEQ + ("h",), axis=0)
        wide_all = wide_all.reshape(n_seq, n_head, rows, 3 * f_cols + o_cols)
        w_out_t = wide_all[..., :o_cols].transpose(0, 2, 1, 3).reshape(D, H * DH)
        wide_all = wide_all[..., o_cols:].reshape(n_seq, n_head, rows, 3, f_cols)
        wide_all = wide_all.transpose(3, 0, 2, 1, 4).reshape(3, D, FF)
        w_gate, w_up, w_down_t = wide_all[0], wide_all[1], wide_all[2]

    spots = jnp.arange(n_seq, dtype=jnp.int32)
    own_block = jnp.sum(jnp.where(spots == seq_at, block_order, 0))
    offsets = jnp.arange(block_len, dtype=jnp.int32)
    query_pos = own_block * block_len + offsets
    ahead = blocks_ahead()
    ahead_block = jnp.sum(jnp.where(spots[None, :] == ahead[:, None], block_order[None, :], 0), axis=1)
    key_pos = (ahead_block[:, None] * block_len + offsets[None, :]).reshape(1, n_seq * block_len)
    cos_t, sin_t = rope_tables(query_pos)

    tok = lax.dynamic_slice_in_dim(tokens, head_at * count, count, 0).astype(F32)
    cot = lax.dynamic_slice_in_dim(cotangent, head_at * count, count, 0).astype(F32)
    same_domain = (domain_ids[:, None] == domain_ids[None, :]).astype(F32)
    seq_weight = lax.dynamic_slice_in_dim(1.0 / jnp.sum(same_domain, axis=1), head_at * count, count, 0)
    out_grad = cot * seq_weight[:, None, None]
    out_low = out_grad.astype(BF)

    first_hat, first_inverse = normalize(tok)
    first_normalized = (first_hat * gain_first).astype(BF)
    factors = jnp.einsum("scd,dj->sjc", first_normalized, w_factors, preferred_element_type=F32)
    query, own_factors = prologue(factors, cos_t, sin_t)
    half = max(1, count // 2)
    groups = [slice(at, at + half) for at in range(0, count, half)]
    gathered = [jnp.concatenate(gather_blocks(own_factors[g]), axis=2) for g in groups]
    forward = [
        attention_forward(query[g], keys, key_pos, query_pos[:, None])
        for g, keys in zip(groups, gathered)
    ]
    heads_wide = jnp.concatenate([part[0] for part in forward], axis=0)
    heads_low = heads_wide.astype(BF)
    attn = jnp.einsum("sce,de->scd", heads_low, w_out_t, preferred_element_type=F32)
    middle = tok + attn
    second_hat, second_inverse = normalize(middle)
    second_normalized = (second_hat * gain_second).astype(BF)

    tokens_own = count * block_len

    def both_cores(block):
        flat = block.reshape(tokens_own, D)
        if paired:
            return jnp.concatenate([flat, swap(flat, "c")], axis=0)
        return flat

    def own_sum(partial):
        if paired:
            partial = partial[:tokens_own] + swap(partial[tokens_own:].astype(BF), "c").astype(F32)
        return partial.reshape(count, block_len, D)

    x_low = both_cores(second_normalized)
    y_low = both_cores(out_low)
    gate = jnp.dot(x_low, w_gate, preferred_element_type=F32)
    up = jnp.dot(x_low, w_up, preferred_element_type=F32)
    sigmoid_gate = jax.nn.sigmoid(gate)
    silu_gate = gate * sigmoid_gate
    hidden_low = (silu_gate * up).astype(BF)
    ffn = own_sum(jnp.einsum("tf,df->td", hidden_low, w_down_t, preferred_element_type=F32))
    layer_output = share_over_head((middle + ffn).astype(BF), n_head)

    hidden_grad = jnp.dot(y_low, w_down_t, preferred_element_type=F32)
    up_grad = (hidden_grad * silu_gate).astype(BF)
    gate_grad = (
        hidden_grad * up * (sigmoid_gate * (1.0 + gate * (1.0 - sigmoid_gate)))
    ).astype(BF)
    down_t_grad = jnp.einsum("td,tf->df", y_low, hidden_low, preferred_element_type=F32)
    gate_w_grad = jnp.einsum("td,tf->df", x_low, gate_grad, preferred_element_type=F32)
    up_w_grad = jnp.einsum("td,tf->df", x_low, up_grad, preferred_element_type=F32)
    second_part = jnp.einsum("tf,df->td", gate_grad, w_gate, preferred_element_type=F32)
    second_part = second_part + jnp.einsum("tf,df->td", up_grad, w_up, preferred_element_type=F32)
    second_grad = own_sum(second_part)

    second_gain_grad = jnp.sum(second_grad * second_hat, axis=(0, 1))
    middle_grad = out_grad + norm_back(second_grad, gain_second, second_hat, second_inverse)
    middle_low = middle_grad.astype(BF)
    heads_grad = jnp.einsum("scd,de->sce", middle_low, w_out_t, preferred_element_type=F32).astype(BF)

    def out_grad_of(columns):
        return jnp.einsum("scd,sce->de", middle_low, columns, preferred_element_type=F32)

    if paired:
        core_at = lax.axis_index("c")
        mine = lax.dynamic_slice_in_dim(heads_low, core_at * o_cols, o_cols, 2)
        theirs = lax.dynamic_slice_in_dim(heads_low, (1 - core_at) * o_cols, o_cols, 2)
        sent = swap(out_grad_of(theirs).astype(BF), "c")
        out_t_grad = out_grad_of(mine) + sent.astype(F32)
    else:
        out_t_grad = out_grad_of(heads_low)
    wide_grads = [
        grad.astype(BF) for grad in (down_t_grad, gate_w_grad, up_w_grad, out_t_grad)
    ]
    wide_grads, heads_grad = lax.optimization_barrier((wide_grads, heads_grad))
    if paired:
        down_sum, gate_sum, up_sum, out_sum = [bulk_scatter(grad) for grad in wide_grads]
    else:
        wide_sum = jnp.concatenate(wide_grads, axis=1)
        wide_sum = lax.psum_scatter(wide_sum, SEQ, scatter_dimension=0, tiled=True)
        wide_sum = lax.psum(wide_sum, "h").astype(F32)
        out_sum = lax.dynamic_slice_in_dim(wide_sum, 3 * FF + head_at * o_cols, o_cols, 1)
        wide_sum = wide_sum[:, : 3 * FF].reshape(rows, 3, n_head, f_cols)
        wide_sum = lax.dynamic_index_in_dim(wide_sum, head_at, 2, keepdims=False)
        down_sum, gate_sum, up_sum = wide_sum[:, 0], wide_sum[:, 1], wide_sum[:, 2]

    joint = []
    for at, g in enumerate(groups):
        query_grad, *pieces = attention_backward(
            query[g],
            heads_grad[g],
            forward[at][0],
            forward[at][1],
            gathered[at],
            key_pos,
            query_pos[:, None],
            lax.axis_size("a"),
        )
        own_grad = scatter_blocks(pieces)
        joint.append(epilogue(query_grad, own_grad, factors[g], cos_t, sin_t))
    joint_grad = jnp.concatenate(joint, axis=0)

    first_grad = jnp.einsum("sjc,dj->scd", joint_grad, w_factors, preferred_element_type=F32)
    factors_w_grad = jnp.einsum(
        "scd,sjc->dj", first_normalized, joint_grad, preferred_element_type=F32
    )
    first_gain_grad = jnp.sum(first_grad * first_hat, axis=(0, 1))
    input_grad = middle_grad + norm_back(first_grad, gain_first, first_hat, first_inverse)
    input_grad = share_over_head(input_grad.astype(BF), n_head).astype(F32)

    gain_cols = jnp.stack([first_gain_grad, second_gain_grad]).T
    small_grad = jnp.concatenate([factors_w_grad, gain_cols], axis=1).astype(BF)
    small_sum = small_grad.reshape(
        lax.axis_size("a"), lax.axis_size("b"), 2, rows, small_grad.shape[1]
    )
    small_sum = ordered_scatter(small_sum, "c", 2)
    small_sum = ordered_scatter(small_sum, "b", 1)
    small_sum = ordered_scatter(small_sum, "a", 0)
    small_sum = sum_over_head(small_sum, n_head).astype(F32)
    heads_sum = lax.dynamic_slice_in_dim(small_sum, head_at * h_cols, h_cols, 1)
    shared_sum = small_sum[:, H * RA : H * RA + RA * DH]
    gains_sum = small_sum[:, H * RA + RA * DH :].T
    out_sum = out_sum.T
    gate_up_sum = jnp.stack([gate_sum, up_sum])
    down_sum = down_sum.T

    rates = step_rates()
    heads_new = adam_update(headwise, headwise_mean, headwise_square, heads_sum, rates[0])
    shared_new = adam_update(
        shared_factors, shared_factors_mean, shared_factors_square, shared_sum, rates[1]
    )
    out_new = adam_update(out_weight, out_weight_mean, out_weight_square, out_sum, rates[2])
    gate_new = adam_update(gate_up, gate_up_mean, gate_up_square, gate_up_sum, rates[3])
    down_new = adam_update(down_weight, down_weight_mean, down_weight_square, down_sum, rates[4])
    gains_new = adam_update(norm_gains, norm_gains_mean, norm_gains_square, gains_sum, rates[5])
    return (
        layer_output,
        input_grad,
        *heads_new,
        *shared_new,
        *out_new,
        *gate_new,
        *down_new,
        *gains_new,
    )


def solution(mesh):
    n_seq = mesh.shape["seq"]
    n_head = mesh.shape["head"]
    inner = max(1, n_seq // 8)
    fine = Mesh(mesh.devices.reshape(n_seq // 2 // inner, inner, 2, n_head), ("a", "b", "c", "h"))
    token = P(None, SEQ, None)
    heads = P(SEQ, "h")
    shared = P(SEQ, None)
    turned = P("h", SEQ)
    gates = P(None, SEQ, "h")
    gains = P(None, SEQ)
    weights = sum(([spec] * 3 for spec in (heads, shared, turned, gates, turned, gains)), [])
    return jax.shard_map(
        on_device,
        mesh=fine,
        in_specs=(token, token, P(), P(), *weights),
        out_specs=(token, token, *weights),
        check_vma=False,
    )
```

```python
import functools

import jax
import jax.numpy as jnp
from jax import lax
from jax.experimental import pallas as pl
from jax.experimental.pallas import tpu as pltpu
from jax.sharding import Mesh
from jax.sharding import PartitionSpec as P

D = 1024
H = 16
DH = 64
RQ = 6
RK = 2
RA = RQ + 2 * RK
FF = 2816
STEP = 10
HB = 4

EPSILON = 1e-05
BETA_ONE = 0.9
BETA_TWO = 0.95
ADAM_EPS = 1e-08
DECAY = 0.1
NEGATIVE = -1e30
SCALE = DH ** (-0.5)
BF = jnp.bfloat16
F32 = jnp.float32
SEQ = ("a", "b", "c")


def rope_tables(positions):
    half_dim = DH // 2
    frequency = 10000.0 ** (-(2.0 * jnp.arange(half_dim, dtype=F32)) / DH)
    angles = frequency[:, None] * positions.astype(F32)[None, :]
    return (jnp.cos(angles), jnp.sin(angles))


def normalize(row_data):
    inverse = lax.rsqrt(jnp.mean(row_data * row_data, -1, keepdims=True) + EPSILON)
    return (row_data * inverse, inverse)


def norm_back(normed_grad, gain_row, hat_rows, inverse):
    hat_grad = normed_grad * gain_row
    return inverse * (hat_grad - hat_rows * jnp.mean(hat_grad * hat_rows, -1, keepdims=True))


def adam_update(master, mean_old, square_old, gradient, rate):
    mean_new = BETA_ONE * mean_old + (1.0 - BETA_ONE) * gradient
    square_new = BETA_TWO * square_old + (1.0 - BETA_TWO) * gradient * gradient
    mean_hat = mean_new / (1.0 - BETA_ONE**STEP)
    square_hat = square_new / (1.0 - BETA_TWO**STEP)
    master_new = master - rate * (mean_hat / (jnp.sqrt(square_hat) + ADAM_EPS) + DECAY * master)
    return (master_new, mean_new, square_new)


def step_rates():
    return (
        2.5 * (D // 4) ** (-0.5),
        2.5 * D ** (-0.5),
        2.5 * (H * DH // 32) ** (-0.5),
        2.5 * D ** (-0.5),
        2.5 * FF ** (-0.5),
        0.5,
    )


def rotated(pair, cos_t, sin_t):
    u = pair[: DH // 2]
    w = pair[DH // 2 :]
    return jnp.concatenate([u * cos_t - w * sin_t, w * cos_t + u * sin_t], axis=0)


def unrotated(pair, cos_t, sin_t):
    u = pair[: DH // 2]
    w = pair[DH // 2 :]
    return jnp.concatenate([u * cos_t + w * sin_t, w * cos_t - u * sin_t], axis=0)


def prologue_body(f_ref, cos_ref, sin_ref, q_ref, fac_ref):
    cos_t = cos_ref[...]
    sin_t = sin_ref[...]
    base = H * RA
    bq = [
        rotated(f_ref[0, base + r * DH : base + (r + 1) * DH, :], cos_t, sin_t) for r in range(RQ)
    ]
    for pair in range(H // 2):
        parts = []
        for h in (2 * pair, 2 * pair + 1):
            acc = f_ref[0, h * RA : h * RA + 1, :] * bq[0]
            for r in range(1, RQ):
                acc = acc + f_ref[0, h * RA + r : h * RA + r + 1, :] * bq[r]
            parts.append(acc)
        both = jnp.concatenate(parts, axis=0) / RQ
        rows = jnp.transpose(both).astype(BF) * SCALE
        q_ref[0, :, pair * 2 * DH : (pair + 1) * 2 * DH] = rows.astype(BF)
    for r in range(RK):
        at = base + (RQ + r) * DH
        fac_ref[0, r * 2 * DH : r * 2 * DH + DH, :] = rotated(
            f_ref[0, at : at + DH, :], cos_t, sin_t
        ).astype(BF)
        at = base + (RQ + RK + r) * DH
        fac_ref[0, r * 2 * DH + DH : (r + 1) * 2 * DH, :] = f_ref[0, at : at + DH, :].astype(BF)
    rows = [f_ref[0, h * RA + RQ : (h + 1) * RA, :] for h in range(H)]
    fac_ref[0, RK * 2 * DH :, :] = (jnp.concatenate(rows, axis=0) * (1.0 / RK)).astype(BF)


FAC = RK * 2 * DH + 2 * RK * H


def prologue(factors, cos_t, sin_t):
    count, width, block = factors.shape
    return pl.pallas_call(
        prologue_body,
        grid=(count,),
        in_specs=[
            pl.BlockSpec((1, width, block), lambda s: (s, 0, 0)),
            pl.BlockSpec((DH // 2, block), lambda s: (0, 0)),
            pl.BlockSpec((DH // 2, block), lambda s: (0, 0)),
        ],
        out_specs=[
            pl.BlockSpec((1, block, H * DH), lambda s: (s, 0, 0)),
            pl.BlockSpec((1, FAC, block), lambda s: (s, 0, 0)),
        ],
        out_shape=[
            jax.ShapeDtypeStruct((count, block, H * DH), BF),
            jax.ShapeDtypeStruct((count, FAC, block), BF),
        ],
        name="factor_prologue",
    )(factors, cos_t, sin_t)


def epilogue_body(dq_ref, df_ref, f_ref, cos_ref, sin_ref, g_ref):
    cos_t = cos_ref[...]
    sin_t = sin_ref[...]
    base = H * RA
    bq = [
        rotated(f_ref[0, base + r * DH : base + (r + 1) * DH, :], cos_t, sin_t) for r in range(RQ)
    ]
    sums = [None] * RQ
    rows = []
    wide = RK * 2 * DH
    for pair in range(H // 2):
        both = jnp.transpose(dq_ref[0, :, pair * 2 * DH : (pair + 1) * 2 * DH])
        for k in range(2):
            h = 2 * pair + k
            dq = both[k * DH : (k + 1) * DH] * (1.0 / RQ)
            for r in range(RQ):
                rows.append(jnp.sum(dq * bq[r], axis=0, keepdims=True))
                term = f_ref[0, h * RA + r : h * RA + r + 1, :] * dq
                sums[r] = term if sums[r] is None else sums[r] + term
            rows.append(df_ref[0, wide + h * 2 * RK : wide + (h + 1) * 2 * RK, :].astype(F32))
    for r in range(RQ):
        rows.append(unrotated(sums[r], cos_t, sin_t))
    for r in range(RK):
        part = df_ref[0, r * 2 * DH : r * 2 * DH + DH, :].astype(F32)
        rows.append(unrotated(part, cos_t, sin_t))
    for r in range(RK):
        rows.append(df_ref[0, r * 2 * DH + DH : (r + 1) * 2 * DH, :].astype(F32))
    g_ref[0] = jnp.transpose(jnp.concatenate(rows, axis=0)).astype(BF)


def epilogue(query_grad, factor_grad, factors, cos_t, sin_t):
    count, width, block = factors.shape
    return pl.pallas_call(
        epilogue_body,
        grid=(count,),
        in_specs=[
            pl.BlockSpec((1, block, H * DH), lambda s: (s, 0, 0)),
            pl.BlockSpec((1, FAC, block), lambda s: (s, 0, 0)),
            pl.BlockSpec((1, width, block), lambda s: (s, 0, 0)),
            pl.BlockSpec((DH // 2, block), lambda s: (0, 0)),
            pl.BlockSpec((DH // 2, block), lambda s: (0, 0)),
        ],
        out_specs=pl.BlockSpec((1, block, width), lambda s: (s, 0, 0)),
        out_shape=jax.ShapeDtypeStruct((count, block, width), BF),
        name="factor_epilogue",
    )(query_grad, factor_grad, factors, cos_t, sin_t)


def keys_values(a_rows, b_rows, h):
    a = a_rows[4 * h : 4 * h + 4]
    key_t = a[0:1] * b_rows[:DH] + a[1:2] * b_rows[2 * DH : 3 * DH]
    value_t = a[2:3] * b_rows[DH : 2 * DH] + a[3:4] * b_rows[3 * DH :]
    return key_t.astype(BF), value_t.astype(BF)


NT = (((1,), (1,)), ((), ()))
TN = (((0,), (0,)), ((), ()))


def forward_body(q_ref, b_ref, a_ref, kpos_ref, qpos_ref, o_ref, lse_ref):
    allowed = kpos_ref[...] <= qpos_ref[...]
    b_rows = b_ref[0].astype(F32)
    a_rows = a_ref[0].astype(F32)
    outs = []
    stats = []
    for h in range(HB):
        key_t, value_t = keys_values(a_rows, b_rows, h)
        scores = jnp.dot(q_ref[0, :, h * DH : (h + 1) * DH], key_t, preferred_element_type=F32)
        scores = jnp.where(allowed, scores, NEGATIVE)
        best = jnp.max(scores, axis=1, keepdims=True)
        probs = jnp.exp(scores - best)
        total = jnp.sum(probs, axis=1, keepdims=True)
        part = lax.dot_general(probs.astype(BF), value_t, NT, preferred_element_type=F32)
        outs.append(part / total)
        stats.append(best + jnp.log(total))
    o_ref[0] = jnp.concatenate(outs, axis=1)
    lse_ref[0, 0] = jnp.concatenate(stats, axis=1)


def attention_forward(query, gathered, key_pos, query_pos):
    count, block, width = query.shape
    length = gathered.shape[2]
    wide = RK * 2 * DH
    return pl.pallas_call(
        forward_body,
        grid=(count, H // HB),
        in_specs=[
            pl.BlockSpec((1, block, HB * DH), lambda s, g: (s, 0, g)),
            pl.BlockSpec((1, wide, length), lambda s, g: (s, 0, 0)),
            pl.BlockSpec((1, 4 * HB, length), lambda s, g: (s, wide // (4 * HB) + g, 0)),
            pl.BlockSpec((1, length), lambda s, g: (0, 0)),
            pl.BlockSpec((block, 1), lambda s, g: (0, 0)),
        ],
        out_specs=[
            pl.BlockSpec((1, block, HB * DH), lambda s, g: (s, 0, g)),
            pl.BlockSpec((1, 1, block, HB), lambda s, g: (s, g, 0, 0)),
        ],
        out_shape=[
            jax.ShapeDtypeStruct((count, block, width), F32),
            jax.ShapeDtypeStruct((count, H // HB, block, HB), F32),
        ],
        cost_estimate=pl.CostEstimate(
            flops=4 * count * H * block * length * DH,
            bytes_accessed=2 * count * length * FAC,
            transcendentals=count * H * block * length,
        ),
        name="attention_forward",
    )(query, gathered, gathered, key_pos, query_pos)


def backward_body(
    q_ref, do_ref, o_ref, lse_ref, b_ref, a_ref, kpos_ref, qpos_ref, dq_ref, *refs
):
    piece_refs, acc_ref = refs[:-1], refs[-1]
    group = pl.program_id(1)
    wide = RK * 2 * DH

    @pl.when(group == 0)
    def _():
        acc_ref[...] = jnp.zeros_like(acc_ref)

    allowed = kpos_ref[...] <= qpos_ref[...]
    b_rows = b_ref[0].astype(F32)
    a_rows = a_ref[0].astype(F32)
    lse = lse_ref[0, 0]
    dqs = []
    rows = []
    for h in range(HB):
        key_t, value_t = keys_values(a_rows, b_rows, h)
        q = q_ref[0, :, h * DH : (h + 1) * DH]
        do = do_ref[0, :, h * DH : (h + 1) * DH]
        delta = jnp.sum(do.astype(F32) * o_ref[0, :, h * DH : (h + 1) * DH], axis=1, keepdims=True)
        scores = jnp.dot(q, key_t, preferred_element_type=F32)
        probs = jnp.exp(jnp.where(allowed, scores - lse[:, h : h + 1], NEGATIVE))
        prob_grad = jnp.dot(do, value_t, preferred_element_type=F32)
        score_grad = (probs * (prob_grad - delta)).astype(BF)
        dqs.append(lax.dot_general(score_grad, key_t, NT, preferred_element_type=F32) * SCALE)
        dk = lax.dot_general(q, score_grad, TN, preferred_element_type=F32)
        dv = lax.dot_general(do, probs.astype(BF), TN, preferred_element_type=F32)
        a = a_rows[4 * h : 4 * h + 4]
        acc_ref[:DH] += a[0:1] * dk
        acc_ref[DH : 2 * DH] += a[2:3] * dv
        acc_ref[2 * DH : 3 * DH] += a[1:2] * dk
        acc_ref[3 * DH :] += a[3:4] * dv
        rows.append(jnp.sum(dk * b_rows[:DH], axis=0, keepdims=True))
        rows.append(jnp.sum(dk * b_rows[2 * DH : 3 * DH], axis=0, keepdims=True))
        rows.append(jnp.sum(dv * b_rows[DH : 2 * DH], axis=0, keepdims=True))
        rows.append(jnp.sum(dv * b_rows[3 * DH :], axis=0, keepdims=True))
    dq_ref[0] = jnp.concatenate(dqs, axis=1)
    a_grad = (jnp.concatenate(rows, axis=0) * (1.0 / RK)).astype(BF)
    block = piece_refs[0].shape[3]
    depth = piece_refs[0].shape[0]
    at = pl.multiple_of(wide + group * 4 * HB, 4 * HB)
    for i, ref in enumerate(piece_refs):
        for m in range(depth):
            lanes = (i * depth + m) * block
            ref[m, 0, pl.ds(at, 4 * HB), :] = a_grad[:, lanes : lanes + block]

    @pl.when(group == pl.num_programs(1) - 1)
    def _():
        for i, ref in enumerate(piece_refs):
            for m in range(depth):
                lanes = (i * depth + m) * block
                ref[m, 0, :wide, :] = acc_ref[:, lanes : lanes + block].astype(BF)


def attention_backward(query, heads_grad, heads_wide, lse, gathered, key_pos, query_pos, depth):
    count, block, width = query.shape
    length = gathered.shape[2]
    wide = RK * 2 * DH
    pieces = length // (depth * block)
    return pl.pallas_call(
        backward_body,
        grid=(count, H // HB),
        in_specs=[
            pl.BlockSpec((1, block, HB * DH), lambda s, g: (s, 0, g)),
            pl.BlockSpec((1, block, HB * DH), lambda s, g: (s, 0, g)),
            pl.BlockSpec((1, block, HB * DH), lambda s, g: (s, 0, g)),
            pl.BlockSpec((1, 1, block, HB), lambda s, g: (s, g, 0, 0)),
            pl.BlockSpec((1, wide, length), lambda s, g: (s, 0, 0)),
            pl.BlockSpec((1, 4 * HB, length), lambda s, g: (s, wide // (4 * HB) + g, 0)),
            pl.BlockSpec((1, length), lambda s, g: (0, 0)),
            pl.BlockSpec((block, 1), lambda s, g: (0, 0)),
        ],
        out_specs=[pl.BlockSpec((1, block, HB * DH), lambda s, g: (s, 0, g))]
        + [pl.BlockSpec((depth, 1, FAC, block), lambda s, g: (0, s, 0, 0))] * pieces,
        out_shape=[jax.ShapeDtypeStruct((count, block, width), F32)]
        + [jax.ShapeDtypeStruct((depth, count, FAC, block), BF)] * pieces,
        scratch_shapes=[pltpu.VMEM((wide, length), F32)],
        cost_estimate=pl.CostEstimate(
            flops=10 * count * H * block * length * DH,
            bytes_accessed=4 * count * length * FAC,
            transcendentals=count * H * block * length,
        ),
        name="attention_backward",
    )(query, heads_grad, heads_wide, lse, gathered, gathered, key_pos, query_pos)


def swap(block, axis):
    return lax.ppermute(block, axis, [(0, 1), (1, 0)])


def turn_core_head(block):
    return lax.ppermute(block, ("c", "h"), [(0, 0), (1, 2), (2, 1), (3, 3)])


def from_ahead(block, axis, distance):
    size = lax.axis_size(axis)
    return lax.ppermute(block, axis, [((i + distance) % size, i) for i in range(size)])


def to_ahead(block, axis, distance):
    size = lax.axis_size(axis)
    return lax.ppermute(block, axis, [(i, (i + distance) % size) for i in range(size)])


def ordered_gather(block, axis):
    size = lax.axis_size(axis)
    spot = lax.axis_index(axis)
    if size == 2:
        other = swap(block, axis)
        mine = spot == 0
        return jnp.stack([jnp.where(mine, block, other), jnp.where(mine, other, block)])
    parts = [block] + [from_ahead(block, axis, m) for m in range(1, size)]
    twice = jnp.stack(parts + parts[:-1])
    return lax.dynamic_slice_in_dim(twice, jnp.mod(size - spot, size), size, 0)


def ordered_scatter(block, axis, dim):
    size = lax.axis_size(axis)
    spot = lax.axis_index(axis)

    def part(m):
        return lax.dynamic_index_in_dim(block, jnp.mod(spot + m, size), dim, keepdims=False)

    total = part(0).astype(F32)
    for m in range(1, size):
        total = total + to_ahead(part(m), axis, m).astype(F32)
    return total.astype(BF)


def gather_blocks(block):
    for name in ("a", "b"):
        ahead = [from_ahead(block, name, m) for m in range(1, lax.axis_size(name))]
        block = jnp.concatenate([block] + ahead, axis=2)
    return jnp.concatenate([block, swap(block, "c")], axis=2)


def blocks_ahead():
    na, nb = lax.axis_size("a"), lax.axis_size("b")
    at = [lax.axis_index(name) for name in SEQ]
    spots = []
    for mc in range(2):
        for mb in range(nb):
            for ma in range(na):
                a = jnp.mod(at[0] + ma, na)
                b = jnp.mod(at[1] + mb, nb)
                spots.append((a * nb + b) * 2 + jnp.mod(at[2] + mc, 2))
    return jnp.stack(spots)


def scatter_core(own, theirs):
    return (own.astype(F32) + swap(theirs, "c").astype(F32)).astype(BF)


def scatter_chips(total):
    for name in ("b", "a"):
        size = lax.axis_size(name)
        total = total.reshape(size, total.shape[0] // size, *total.shape[1:])
        part = total[0].astype(F32)
        for m in range(1, size):
            part = part + to_ahead(total[m], name, m).astype(F32)
        total = part.astype(BF)
    return total[0]


def sum_over_head(block, n_head):
    if n_head == 2:
        return block + swap(block, "h")
    return lax.psum(block, "h")


def in_core_order(own, other, axis):
    first = lax.axis_index("c") == 0
    return jnp.concatenate([jnp.where(first, own, other), jnp.where(first, other, own)], axis=axis)


def every_head(block, n_head):
    if n_head == 2:
        return ordered_gather(block, "h")
    return lax.all_gather(block, "h", axis=0)


def on_device(
    tokens,
    cotangent,
    domain_ids,
    block_order,
    headwise,
    headwise_mean,
    headwise_square,
    shared_factors,
    shared_factors_mean,
    shared_factors_square,
    out_weight,
    out_weight_mean,
    out_weight_square,
    gate_up,
    gate_up_mean,
    gate_up_square,
    down_weight,
    down_weight_mean,
    down_weight_square,
    norm_gains,
    norm_gains_mean,
    norm_gains_square,
):
    n_head = lax.axis_size("h")
    n_seq = lax.axis_size(SEQ)
    paired = n_head == 2
    seq_at = lax.axis_index(SEQ)
    head_at = lax.axis_index("h")
    seq_all, block_len, _ = tokens.shape
    count = seq_all // n_head
    rows = D // n_seq
    o_cols = H * DH // n_head
    h_cols = H * RA // n_head
    s_cols = RA * DH // n_head
    f_cols = FF // n_head

    shared_part = lax.dynamic_slice_in_dim(shared_factors, head_at * s_cols, s_cols, 1)
    small = jnp.concatenate([headwise, shared_part, norm_gains.T], axis=1).astype(BF)
    if n_head == 2:
        halves = ordered_gather(small, "h")
    else:
        halves = lax.all_gather(small, "h", axis=0)
    small = jnp.concatenate(
        [halves[k, :, :h_cols] for k in range(n_head)]
        + [halves[k, :, h_cols : h_cols + s_cols] for k in range(n_head)]
        + [halves[0, :, h_cols + s_cols :]],
        axis=1,
    )
    for name in ("a", "b", "c"):
        small = ordered_gather(small, name)
    small = small.transpose(2, 1, 0, 3, 4).reshape(D, H * RA + RA * DH + 2)
    w_factors = small[:, : H * RA + RA * DH]
    gains_low = small[:, H * RA + RA * DH :].T.astype(F32)
    gain_first = gains_low[0]
    gain_second = gains_low[1]

    wide_parts = (gate_up[0], gate_up[1], down_weight.T, out_weight.T)
    wide_part = jnp.concatenate([part.astype(BF) for part in wide_parts], axis=1)
    if paired:
        wide_all = lax.all_gather(turn_core_head(wide_part), ("a", "b", "h"), axis=0, tiled=True)
    else:
        wide_all = lax.all_gather(wide_part, SEQ + ("h",), axis=0)

    spots = jnp.arange(n_seq, dtype=jnp.int32)
    own_block = jnp.sum(jnp.where(spots == seq_at, block_order, 0))
    offsets = jnp.arange(block_len, dtype=jnp.int32)
    query_pos = own_block * block_len + offsets
    ahead = blocks_ahead()
    ahead_block = jnp.sum(jnp.where(spots[None, :] == ahead[:, None], block_order[None, :], 0), axis=1)
    key_pos = (ahead_block[:, None] * block_len + offsets[None, :]).reshape(1, n_seq * block_len)
    cos_t, sin_t = rope_tables(query_pos)

    tok = lax.dynamic_slice_in_dim(tokens, head_at * count, count, 0).astype(F32)
    cot = lax.dynamic_slice_in_dim(cotangent, head_at * count, count, 0).astype(F32)
    same_domain = (domain_ids[:, None] == domain_ids[None, :]).astype(F32)
    seq_weight = lax.dynamic_slice_in_dim(1.0 / jnp.sum(same_domain, axis=1), head_at * count, count, 0)
    out_grad = cot * seq_weight[:, None, None]
    out_low = out_grad.astype(BF)

    first_hat, first_inverse = normalize(tok)
    first_normalized = (first_hat * gain_first).astype(BF)
    factors = jnp.einsum("scd,dj->sjc", first_normalized, w_factors, preferred_element_type=F32)
    query, own_factors = prologue(factors, cos_t, sin_t)
    half = max(1, count // 2)
    groups = [slice(at, at + half) for at in range(0, count, half)]
    gathered = [gather_blocks(own_factors[g]) for g in groups]
    forward = []
    for at, g in enumerate(groups):
        wide, stats = attention_forward(query[g], gathered[at], key_pos, query_pos[:, None])
        if at == 0:
            wide, wide_all = lax.optimization_barrier((wide, wide_all))
        forward.append((wide, stats))
    if paired:
        w_gate = wide_all[:, :f_cols]
        w_up = wide_all[:, f_cols : 2 * f_cols]
        w_down_t = wide_all[:, 2 * f_cols : 3 * f_cols]
        own_out = wide_all[:, 3 * f_cols :]
        w_out_t = in_core_order(own_out, swap(own_out, "c"), 1)
    else:
        wide_all = wide_all.reshape(n_seq, n_head, rows, 3 * f_cols + o_cols)
        w_out_t = wide_all[..., 3 * f_cols :].transpose(0, 2, 1, 3).reshape(D, H * DH)
        wide_all = wide_all[..., : 3 * f_cols].reshape(n_seq, n_head, rows, 3, f_cols)
        wide_all = wide_all.transpose(3, 0, 2, 1, 4).reshape(3, D, FF)
        w_gate, w_up, w_down_t = wide_all[0], wide_all[1], wide_all[2]
    heads_wide = jnp.concatenate([part[0] for part in forward], axis=0)
    heads_low = heads_wide.astype(BF)
    attn = jnp.einsum("sce,de->scd", heads_low, w_out_t, preferred_element_type=F32)
    middle = tok + attn
    second_hat, second_inverse = normalize(middle)
    second_normalized = (second_hat * gain_second).astype(BF)

    tokens_own = count * block_len

    def both_cores(block):
        flat = block.reshape(tokens_own, D)
        if paired:
            return jnp.concatenate([flat, swap(flat, "c")], axis=0)
        return flat

    def own_sum(partial):
        if paired:
            partial = partial[:tokens_own] + swap(partial[tokens_own:].astype(BF), "c").astype(F32)
        return partial.reshape(count, block_len, D)

    x_low = both_cores(second_normalized)
    y_low = both_cores(out_low)
    gate = jnp.dot(x_low, w_gate, preferred_element_type=F32)
    up = jnp.dot(x_low, w_up, preferred_element_type=F32)
    sigmoid_gate = jax.nn.sigmoid(gate)
    silu_gate = gate * sigmoid_gate
    hidden_low = (silu_gate * up).astype(BF)
    ffn = own_sum(jnp.einsum("tf,df->td", hidden_low, w_down_t, preferred_element_type=F32))
    layer_low = (middle + ffn).astype(BF)
    down_low = jnp.einsum("td,tf->df", y_low, hidden_low, preferred_element_type=F32).astype(BF)
    layer_all = every_head(layer_low, n_head)

    hidden_grad = jnp.dot(y_low, w_down_t, preferred_element_type=F32)
    up_grad = (hidden_grad * silu_gate).astype(BF)
    gate_grad = (
        hidden_grad * up * (sigmoid_gate * (1.0 + gate * (1.0 - sigmoid_gate)))
    ).astype(BF)
    gate_w_grad = jnp.einsum("td,tf->df", x_low, gate_grad, preferred_element_type=F32)
    up_w_grad = jnp.einsum("td,tf->df", x_low, up_grad, preferred_element_type=F32)
    second_part = jnp.einsum("tf,df->td", gate_grad, w_gate, preferred_element_type=F32)
    second_part = second_part + jnp.einsum("tf,df->td", up_grad, w_up, preferred_element_type=F32)
    second_grad = own_sum(second_part)

    second_gain_grad = jnp.sum(second_grad * second_hat, axis=(0, 1))
    middle_grad = out_grad + norm_back(second_grad, gain_second, second_hat, second_inverse)
    middle_low = middle_grad.astype(BF)
    heads_grad = jnp.einsum("scd,de->sce", middle_low, w_out_t, preferred_element_type=F32).astype(BF)

    def out_grad_of(columns):
        return jnp.einsum("scd,sce->de", middle_low, columns, preferred_element_type=F32)

    if paired:
        core_at = lax.axis_index("c")
        mine = lax.dynamic_slice_in_dim(heads_low, core_at * o_cols, o_cols, 2)
        theirs = lax.dynamic_slice_in_dim(heads_low, (1 - core_at) * o_cols, o_cols, 2)
        sent = swap(out_grad_of(theirs).astype(BF), "c")
        out_t_grad = out_grad_of(mine) + sent.astype(F32)
    else:
        out_t_grad = out_grad_of(heads_low)
    if paired:
        wide_grads = (gate_w_grad, up_w_grad, down_low, out_t_grad)
        wide_grad = jnp.concatenate([grad.astype(BF) for grad in wide_grads], axis=1)
        wide_grad, heads_grad = lax.optimization_barrier((wide_grad, heads_grad))
        wide_sum = lax.psum_scatter(wide_grad, ("a", "b", "h"), scatter_dimension=0, tiled=True)
        wide_sum = turn_core_head(wide_sum).astype(F32)
        gate_sum = wide_sum[:, :f_cols]
        up_sum = wide_sum[:, f_cols : 2 * f_cols]
        down_sum = wide_sum[:, 2 * f_cols : 3 * f_cols]
        out_sum = wide_sum[:, 3 * f_cols :]
    else:
        wide_grads = (gate_w_grad, up_w_grad, down_low, out_t_grad)
        wide_sum = jnp.concatenate([grad.astype(BF) for grad in wide_grads], axis=1)
        wide_sum = lax.psum_scatter(wide_sum, SEQ, scatter_dimension=0, tiled=True)
        wide_sum = lax.psum(wide_sum, "h").astype(F32)
        out_sum = lax.dynamic_slice_in_dim(wide_sum, 3 * FF + head_at * o_cols, o_cols, 1)
        wide_sum = wide_sum[:, : 3 * FF].reshape(rows, 3, n_head, f_cols)
        wide_sum = lax.dynamic_index_in_dim(wide_sum, head_at, 2, keepdims=False)
        gate_sum, up_sum, down_sum = wide_sum[:, 0], wide_sum[:, 1], wide_sum[:, 2]

    query_grads = []
    core_sums = []
    for at, g in enumerate(groups):
        backed = heads_grad[g]
        if at == 1:
            backed, core_sums[0] = lax.optimization_barrier((backed, core_sums[0]))
        query_grad, *pieces = attention_backward(
            query[g],
            backed,
            forward[at][0],
            forward[at][1],
            gathered[at],
            key_pos,
            query_pos[:, None],
            n_seq // 2,
        )
        query_grads.append(query_grad)
        core_sums.append(scatter_core(*pieces))
    layer_output = layer_all.reshape(seq_all, block_len, D)

    factors_w_grad = 0.0
    first_gain_grad = 0.0
    input_parts = []
    own_grads = [scatter_chips(total) for total in core_sums]
    for at, g in enumerate(groups):
        joint_grad = epilogue(query_grads[at], own_grads[at], factors[g], cos_t, sin_t)
        first_grad = jnp.einsum("scj,dj->scd", joint_grad, w_factors, preferred_element_type=F32)
        factors_w_grad = factors_w_grad + jnp.einsum(
            "scd,scj->dj", first_normalized[g], joint_grad, preferred_element_type=F32
        )
        first_gain_grad = first_gain_grad + jnp.sum(first_grad * first_hat[g], axis=(0, 1))
        part = middle_grad[g] + norm_back(first_grad, gain_first, first_hat[g], first_inverse[g])
        part = part.astype(BF)
        if at + 1 < len(groups):
            part, own_grads[at + 1] = lax.optimization_barrier((part, own_grads[at + 1]))
        input_parts.append(every_head(part, n_head))
    input_grad = jnp.concatenate(input_parts, axis=1).reshape(seq_all, block_len, D).astype(F32)

    gain_cols = jnp.stack([first_gain_grad, second_gain_grad]).T
    small_grad = jnp.concatenate([factors_w_grad, gain_cols], axis=1).astype(BF)
    small_sum = small_grad.reshape(
        lax.axis_size("a"), lax.axis_size("b"), 2, rows, small_grad.shape[1]
    )
    small_sum = ordered_scatter(small_sum, "c", 2)
    small_sum = ordered_scatter(small_sum, "b", 1)
    small_sum = ordered_scatter(small_sum, "a", 0)
    small_sum = sum_over_head(small_sum, n_head).astype(F32)
    heads_sum = lax.dynamic_slice_in_dim(small_sum, head_at * h_cols, h_cols, 1)
    shared_sum = small_sum[:, H * RA : H * RA + RA * DH]
    gains_sum = small_sum[:, H * RA + RA * DH :].T
    out_sum = out_sum.T
    gate_up_sum = jnp.stack([gate_sum, up_sum])
    down_sum = down_sum.T

    rates = step_rates()
    heads_new = adam_update(headwise, headwise_mean, headwise_square, heads_sum, rates[0])
    shared_new = adam_update(
        shared_factors, shared_factors_mean, shared_factors_square, shared_sum, rates[1]
    )
    out_new = adam_update(out_weight, out_weight_mean, out_weight_square, out_sum, rates[2])
    gate_new = adam_update(gate_up, gate_up_mean, gate_up_square, gate_up_sum, rates[3])
    down_new = adam_update(down_weight, down_weight_mean, down_weight_square, down_sum, rates[4])
    gains_new = adam_update(norm_gains, norm_gains_mean, norm_gains_square, gains_sum, rates[5])
    return (
        layer_output,
        input_grad,
        *heads_new,
        *shared_new,
        *out_new,
        *gate_new,
        *down_new,
        *gains_new,
    )


def solution(mesh):
    n_seq = mesh.shape["seq"]
    n_head = mesh.shape["head"]
    inner = max(1, n_seq // 8)
    fine = Mesh(mesh.devices.reshape(n_seq // 2 // inner, inner, 2, n_head), ("a", "b", "c", "h"))
    token = P(None, SEQ, None)
    heads = P(SEQ, "h")
    shared = P(SEQ, None)
    turned = P("h", SEQ)
    gates = P(None, SEQ, "h")
    gains = P(None, SEQ)
    weights = sum(([spec] * 3 for spec in (heads, shared, turned, gates, turned, gains)), [])
    return jax.shard_map(
        on_device,
        mesh=fine,
        in_specs=(token, token, P(), P(), *weights),
        out_specs=(token, token, *weights),
        check_vma=False,
    )
```

```python
import functools

import jax
import jax.numpy as jnp
from jax import lax
from jax.experimental import pallas as pl
from jax.experimental.pallas import tpu as pltpu
from jax.sharding import Mesh
from jax.sharding import PartitionSpec as P

D = 1024
H = 16
DH = 64
RQ = 6
RK = 2
RA = RQ + 2 * RK
FF = 2816
STEP = 10
HB = 4

EPSILON = 1e-05
BETA_ONE = 0.9
BETA_TWO = 0.95
ADAM_EPS = 1e-08
DECAY = 0.1
NEGATIVE = -1e30
SCALE = DH ** (-0.5)
BF = jnp.bfloat16
F32 = jnp.float32
SEQ = ("a", "b", "c")


def rope_tables(positions):
    half_dim = DH // 2
    frequency = 10000.0 ** (-(2.0 * jnp.arange(half_dim, dtype=F32)) / DH)
    angles = frequency[:, None] * positions.astype(F32)[None, :]
    return (jnp.cos(angles), jnp.sin(angles))


def normalize(row_data):
    inverse = lax.rsqrt(jnp.mean(row_data * row_data, -1, keepdims=True) + EPSILON)
    return (row_data * inverse, inverse)


def norm_back(normed_grad, gain_row, hat_rows, inverse):
    hat_grad = normed_grad * gain_row
    return inverse * (hat_grad - hat_rows * jnp.mean(hat_grad * hat_rows, -1, keepdims=True))


def adam_update(master, mean_old, square_old, gradient, rate):
    mean_new = BETA_ONE * mean_old + (1.0 - BETA_ONE) * gradient
    square_new = BETA_TWO * square_old + (1.0 - BETA_TWO) * gradient * gradient
    mean_hat = mean_new / (1.0 - BETA_ONE**STEP)
    square_hat = square_new / (1.0 - BETA_TWO**STEP)
    master_new = master - rate * (mean_hat / (jnp.sqrt(square_hat) + ADAM_EPS) + DECAY * master)
    return (master_new, mean_new, square_new)


def step_rates():
    return (
        2.5 * (D // 4) ** (-0.5),
        2.5 * D ** (-0.5),
        2.5 * (H * DH // 32) ** (-0.5),
        2.5 * D ** (-0.5),
        2.5 * FF ** (-0.5),
        0.5,
    )


def rotated(pair, cos_t, sin_t):
    u = pair[: DH // 2]
    w = pair[DH // 2 :]
    return jnp.concatenate([u * cos_t - w * sin_t, w * cos_t + u * sin_t], axis=0)


def unrotated(pair, cos_t, sin_t):
    u = pair[: DH // 2]
    w = pair[DH // 2 :]
    return jnp.concatenate([u * cos_t + w * sin_t, w * cos_t - u * sin_t], axis=0)


def prologue_body(f_ref, cos_ref, sin_ref, q_ref, fac_ref):
    cos_t = cos_ref[...]
    sin_t = sin_ref[...]
    base = H * RA
    bq = [
        rotated(f_ref[0, base + r * DH : base + (r + 1) * DH, :], cos_t, sin_t) for r in range(RQ)
    ]
    for pair in range(H // 2):
        parts = []
        for h in (2 * pair, 2 * pair + 1):
            acc = f_ref[0, h * RA : h * RA + 1, :] * bq[0]
            for r in range(1, RQ):
                acc = acc + f_ref[0, h * RA + r : h * RA + r + 1, :] * bq[r]
            parts.append(acc)
        both = jnp.concatenate(parts, axis=0) / RQ
        rows = jnp.transpose(both).astype(BF) * SCALE
        q_ref[0, :, pair * 2 * DH : (pair + 1) * 2 * DH] = rows.astype(BF)
    for r in range(RK):
        at = base + (RQ + r) * DH
        fac_ref[0, r * 2 * DH : r * 2 * DH + DH, :] = rotated(
            f_ref[0, at : at + DH, :], cos_t, sin_t
        ).astype(BF)
        at = base + (RQ + RK + r) * DH
        fac_ref[0, r * 2 * DH + DH : (r + 1) * 2 * DH, :] = f_ref[0, at : at + DH, :].astype(BF)
    rows = [f_ref[0, h * RA + RQ : (h + 1) * RA, :] for h in range(H)]
    fac_ref[0, RK * 2 * DH :, :] = (jnp.concatenate(rows, axis=0) * (1.0 / RK)).astype(BF)


FAC = RK * 2 * DH + 2 * RK * H


def prologue(factors, cos_t, sin_t):
    count, width, block = factors.shape
    return pl.pallas_call(
        prologue_body,
        grid=(count,),
        in_specs=[
            pl.BlockSpec((1, width, block), lambda s: (s, 0, 0)),
            pl.BlockSpec((DH // 2, block), lambda s: (0, 0)),
            pl.BlockSpec((DH // 2, block), lambda s: (0, 0)),
        ],
        out_specs=[
            pl.BlockSpec((1, block, H * DH), lambda s: (s, 0, 0)),
            pl.BlockSpec((1, FAC, block), lambda s: (s, 0, 0)),
        ],
        out_shape=[
            jax.ShapeDtypeStruct((count, block, H * DH), BF),
            jax.ShapeDtypeStruct((count, FAC, block), BF),
        ],
        name="factor_prologue",
    )(factors, cos_t, sin_t)


def epilogue_body(dq_ref, df_ref, f_ref, cos_ref, sin_ref, g_ref):
    cos_t = cos_ref[...]
    sin_t = sin_ref[...]
    base = H * RA
    bq = [
        rotated(f_ref[0, base + r * DH : base + (r + 1) * DH, :], cos_t, sin_t) for r in range(RQ)
    ]
    sums = [None] * RQ
    rows = []
    wide = RK * 2 * DH
    for pair in range(H // 2):
        both = jnp.transpose(dq_ref[0, :, pair * 2 * DH : (pair + 1) * 2 * DH])
        for k in range(2):
            h = 2 * pair + k
            dq = both[k * DH : (k + 1) * DH] * (1.0 / RQ)
            for r in range(RQ):
                rows.append(jnp.sum(dq * bq[r], axis=0, keepdims=True))
                term = f_ref[0, h * RA + r : h * RA + r + 1, :] * dq
                sums[r] = term if sums[r] is None else sums[r] + term
            rows.append(df_ref[0, wide + h * 2 * RK : wide + (h + 1) * 2 * RK, :].astype(F32))
    for r in range(RQ):
        rows.append(unrotated(sums[r], cos_t, sin_t))
    for r in range(RK):
        part = df_ref[0, r * 2 * DH : r * 2 * DH + DH, :].astype(F32)
        rows.append(unrotated(part, cos_t, sin_t))
    for r in range(RK):
        rows.append(df_ref[0, r * 2 * DH + DH : (r + 1) * 2 * DH, :].astype(F32))
    g_ref[0] = jnp.transpose(jnp.concatenate(rows, axis=0)).astype(BF)


def epilogue(query_grad, factor_grad, factors, cos_t, sin_t):
    count, width, block = factors.shape
    return pl.pallas_call(
        epilogue_body,
        grid=(count,),
        in_specs=[
            pl.BlockSpec((1, block, H * DH), lambda s: (s, 0, 0)),
            pl.BlockSpec((1, FAC, block), lambda s: (s, 0, 0)),
            pl.BlockSpec((1, width, block), lambda s: (s, 0, 0)),
            pl.BlockSpec((DH // 2, block), lambda s: (0, 0)),
            pl.BlockSpec((DH // 2, block), lambda s: (0, 0)),
        ],
        out_specs=pl.BlockSpec((1, block, width), lambda s: (s, 0, 0)),
        out_shape=jax.ShapeDtypeStruct((count, block, width), BF),
        name="factor_epilogue",
    )(query_grad, factor_grad, factors, cos_t, sin_t)


def keys_values(a_rows, b_rows, h):
    a = a_rows[4 * h : 4 * h + 4]
    key_t = a[0:1] * b_rows[:DH] + a[1:2] * b_rows[2 * DH : 3 * DH]
    value_t = a[2:3] * b_rows[DH : 2 * DH] + a[3:4] * b_rows[3 * DH :]
    return key_t.astype(BF), value_t.astype(BF)


NT = (((1,), (1,)), ((), ()))
TN = (((0,), (0,)), ((), ()))


def forward_body(q_ref, b_ref, a_ref, kpos_ref, qpos_ref, o_ref, lse_ref):
    allowed = kpos_ref[...] <= qpos_ref[...]
    b_rows = b_ref[0].astype(F32)
    a_rows = a_ref[0].astype(F32)
    outs = []
    stats = []
    for h in range(HB):
        key_t, value_t = keys_values(a_rows, b_rows, h)
        scores = jnp.dot(q_ref[0, :, h * DH : (h + 1) * DH], key_t, preferred_element_type=F32)
        scores = jnp.where(allowed, scores, NEGATIVE)
        best = jnp.max(scores, axis=1, keepdims=True)
        probs = jnp.exp(scores - best)
        total = jnp.sum(probs, axis=1, keepdims=True)
        part = lax.dot_general(probs.astype(BF), value_t, NT, preferred_element_type=F32)
        outs.append(part / total)
        stats.append(best + jnp.log(total))
    o_ref[0] = jnp.concatenate(outs, axis=1)
    lse_ref[0, 0] = jnp.concatenate(stats, axis=1)


def attention_forward(query, gathered, key_pos, query_pos):
    count, block, width = query.shape
    length = gathered.shape[2]
    wide = RK * 2 * DH
    return pl.pallas_call(
        forward_body,
        grid=(count, H // HB),
        in_specs=[
            pl.BlockSpec((1, block, HB * DH), lambda s, g: (s, 0, g)),
            pl.BlockSpec((1, wide, length), lambda s, g: (s, 0, 0)),
            pl.BlockSpec((1, 4 * HB, length), lambda s, g: (s, wide // (4 * HB) + g, 0)),
            pl.BlockSpec((1, length), lambda s, g: (0, 0)),
            pl.BlockSpec((block, 1), lambda s, g: (0, 0)),
        ],
        out_specs=[
            pl.BlockSpec((1, block, HB * DH), lambda s, g: (s, 0, g)),
            pl.BlockSpec((1, 1, block, HB), lambda s, g: (s, g, 0, 0)),
        ],
        out_shape=[
            jax.ShapeDtypeStruct((count, block, width), F32),
            jax.ShapeDtypeStruct((count, H // HB, block, HB), F32),
        ],
        cost_estimate=pl.CostEstimate(
            flops=4 * count * H * block * length * DH,
            bytes_accessed=2 * count * length * FAC,
            transcendentals=count * H * block * length,
        ),
        name="attention_forward",
    )(query, gathered, gathered, key_pos, query_pos)


def backward_body(
    q_ref, do_ref, o_ref, lse_ref, b_ref, a_ref, kpos_ref, qpos_ref, dq_ref, *refs
):
    piece_refs, acc_ref = refs[:-1], refs[-1]
    group = pl.program_id(1)
    wide = RK * 2 * DH

    @pl.when(group == 0)
    def _():
        acc_ref[...] = jnp.zeros_like(acc_ref)

    allowed = kpos_ref[...] <= qpos_ref[...]
    b_rows = b_ref[0].astype(F32)
    a_rows = a_ref[0].astype(F32)
    lse = lse_ref[0, 0]
    dqs = []
    rows = []
    for h in range(HB):
        key_t, value_t = keys_values(a_rows, b_rows, h)
        q = q_ref[0, :, h * DH : (h + 1) * DH]
        do = do_ref[0, :, h * DH : (h + 1) * DH]
        delta = jnp.sum(do.astype(F32) * o_ref[0, :, h * DH : (h + 1) * DH], axis=1, keepdims=True)
        scores = jnp.dot(q, key_t, preferred_element_type=F32)
        probs = jnp.exp(jnp.where(allowed, scores - lse[:, h : h + 1], NEGATIVE))
        prob_grad = jnp.dot(do, value_t, preferred_element_type=F32)
        score_grad = (probs * (prob_grad - delta)).astype(BF)
        dqs.append(lax.dot_general(score_grad, key_t, NT, preferred_element_type=F32) * SCALE)
        dk = lax.dot_general(q, score_grad, TN, preferred_element_type=F32)
        dv = lax.dot_general(do, probs.astype(BF), TN, preferred_element_type=F32)
        a = a_rows[4 * h : 4 * h + 4]
        acc_ref[:DH] += a[0:1] * dk
        acc_ref[DH : 2 * DH] += a[2:3] * dv
        acc_ref[2 * DH : 3 * DH] += a[1:2] * dk
        acc_ref[3 * DH :] += a[3:4] * dv
        rows.append(jnp.sum(dk * b_rows[:DH], axis=0, keepdims=True))
        rows.append(jnp.sum(dk * b_rows[2 * DH : 3 * DH], axis=0, keepdims=True))
        rows.append(jnp.sum(dv * b_rows[DH : 2 * DH], axis=0, keepdims=True))
        rows.append(jnp.sum(dv * b_rows[3 * DH :], axis=0, keepdims=True))
    dq_ref[0] = jnp.concatenate(dqs, axis=1)
    a_grad = (jnp.concatenate(rows, axis=0) * (1.0 / RK)).astype(BF)
    block = piece_refs[0].shape[3]
    depth = piece_refs[0].shape[0]
    at = pl.multiple_of(wide + group * 4 * HB, 4 * HB)
    for i, ref in enumerate(piece_refs):
        for m in range(depth):
            lanes = (i * depth + m) * block
            ref[m, 0, pl.ds(at, 4 * HB), :] = a_grad[:, lanes : lanes + block]

    @pl.when(group == pl.num_programs(1) - 1)
    def _():
        for i, ref in enumerate(piece_refs):
            for m in range(depth):
                lanes = (i * depth + m) * block
                ref[m, 0, :wide, :] = acc_ref[:, lanes : lanes + block].astype(BF)


def attention_backward(query, heads_grad, heads_wide, lse, gathered, key_pos, query_pos, depth):
    count, block, width = query.shape
    length = gathered.shape[2]
    wide = RK * 2 * DH
    pieces = length // (depth * block)
    return pl.pallas_call(
        backward_body,
        grid=(count, H // HB),
        in_specs=[
            pl.BlockSpec((1, block, HB * DH), lambda s, g: (s, 0, g)),
            pl.BlockSpec((1, block, HB * DH), lambda s, g: (s, 0, g)),
            pl.BlockSpec((1, block, HB * DH), lambda s, g: (s, 0, g)),
            pl.BlockSpec((1, 1, block, HB), lambda s, g: (s, g, 0, 0)),
            pl.BlockSpec((1, wide, length), lambda s, g: (s, 0, 0)),
            pl.BlockSpec((1, 4 * HB, length), lambda s, g: (s, wide // (4 * HB) + g, 0)),
            pl.BlockSpec((1, length), lambda s, g: (0, 0)),
            pl.BlockSpec((block, 1), lambda s, g: (0, 0)),
        ],
        out_specs=[pl.BlockSpec((1, block, HB * DH), lambda s, g: (s, 0, g))]
        + [pl.BlockSpec((depth, 1, FAC, block), lambda s, g: (0, s, 0, 0))] * pieces,
        out_shape=[jax.ShapeDtypeStruct((count, block, width), F32)]
        + [jax.ShapeDtypeStruct((depth, count, FAC, block), BF)] * pieces,
        scratch_shapes=[pltpu.VMEM((wide, length), F32)],
        cost_estimate=pl.CostEstimate(
            flops=10 * count * H * block * length * DH,
            bytes_accessed=4 * count * length * FAC,
            transcendentals=count * H * block * length,
        ),
        name="attention_backward",
    )(query, heads_grad, heads_wide, lse, gathered, gathered, key_pos, query_pos)


def swap(block, axis):
    return lax.ppermute(block, axis, [(0, 1), (1, 0)])


def turn_core_head(block):
    return lax.ppermute(block, ("c", "h"), [(0, 0), (1, 2), (2, 1), (3, 3)])


def from_ahead(block, axis, distance):
    size = lax.axis_size(axis)
    return lax.ppermute(block, axis, [((i + distance) % size, i) for i in range(size)])


def to_ahead(block, axis, distance):
    size = lax.axis_size(axis)
    return lax.ppermute(block, axis, [(i, (i + distance) % size) for i in range(size)])


def ordered_gather(block, axis):
    size = lax.axis_size(axis)
    spot = lax.axis_index(axis)
    if size == 2:
        other = swap(block, axis)
        mine = spot == 0
        return jnp.stack([jnp.where(mine, block, other), jnp.where(mine, other, block)])
    parts = [block] + [from_ahead(block, axis, m) for m in range(1, size)]
    twice = jnp.stack(parts + parts[:-1])
    return lax.dynamic_slice_in_dim(twice, jnp.mod(size - spot, size), size, 0)


def ordered_scatter(block, axis, dim):
    size = lax.axis_size(axis)
    spot = lax.axis_index(axis)

    def part(m):
        return lax.dynamic_index_in_dim(block, jnp.mod(spot + m, size), dim, keepdims=False)

    total = part(0).astype(F32)
    for m in range(1, size):
        total = total + to_ahead(part(m), axis, m).astype(F32)
    return total.astype(BF)


def gather_blocks(block):
    for name in ("a", "b"):
        ahead = [from_ahead(block, name, m) for m in range(1, lax.axis_size(name))]
        block = jnp.concatenate([block] + ahead, axis=2)
    return jnp.concatenate([block, swap(block, "c")], axis=2)


def blocks_ahead():
    na, nb = lax.axis_size("a"), lax.axis_size("b")
    at = [lax.axis_index(name) for name in SEQ]
    spots = []
    for mc in range(2):
        for mb in range(nb):
            for ma in range(na):
                a = jnp.mod(at[0] + ma, na)
                b = jnp.mod(at[1] + mb, nb)
                spots.append((a * nb + b) * 2 + jnp.mod(at[2] + mc, 2))
    return jnp.stack(spots)


def scatter_core(own, theirs):
    return (own.astype(F32) + swap(theirs, "c").astype(F32)).astype(BF)


def scatter_chips(total):
    for name in ("b", "a"):
        size = lax.axis_size(name)
        total = total.reshape(size, total.shape[0] // size, *total.shape[1:])
        part = total[0].astype(F32)
        for m in range(1, size):
            part = part + to_ahead(total[m], name, m).astype(F32)
        total = part.astype(BF)
    return total[0]


def sum_over_head(block, n_head):
    if n_head == 2:
        return block + swap(block, "h")
    return lax.psum(block, "h")


def in_core_order(own, other, axis):
    first = lax.axis_index("c") == 0
    return jnp.concatenate([jnp.where(first, own, other), jnp.where(first, other, own)], axis=axis)


def after(block, gate):
    return lax.optimization_barrier((block, gate))[0]


def every_head(block, n_head):
    if n_head == 2:
        other = swap(block, "h")
        mine = lax.axis_index("h") == 0
        return jnp.stack([jnp.where(mine, block, other), jnp.where(mine, other, block)])
    return lax.all_gather(block, "h", axis=0)


def take(block, spot, dim):
    return lax.dynamic_index_in_dim(block, spot, dim, keepdims=False)


def fold_send(block, axis, dim):
    spot = lax.axis_index(axis)
    return take(block, spot, dim), swap(take(block, 1 - spot, dim), axis)


def fold_add(pair, gate):
    own, other = pair
    return (after(own, gate).astype(F32) + other.astype(F32)).astype(BF)


def depth_send(block):
    size = lax.axis_size("a")
    spot = lax.axis_index("a")
    sent = [to_ahead(take(block, jnp.mod(spot + m, size), 0), "a", m) for m in range(1, size)]
    return take(block, spot, 0), sent


def factor_grads_body(core_ref, x_ref, gain_ref, *refs):
    joint_refs, own_ref, sent_ref = refs[:-2], refs[-2], refs[-1]
    total = None
    at = 0
    for ref in joint_refs:
        size = ref.shape[0]
        part = lax.dot_general(x_ref[at : at + size, :], ref[...], TN, preferred_element_type=F32)
        total = part if total is None else total + part
        at += size
    na, nb, rows, _ = own_ref.shape
    width = total.shape[1]
    first = core_ref[0] == 0
    gains = jnp.transpose(gain_ref[...])[:, :2]
    for i in range(na * nb):
        low = slice(2 * i * rows, (2 * i + 1) * rows)
        high = slice((2 * i + 1) * rows, (2 * i + 2) * rows)
        for block, lanes in ((total, slice(0, width)), (gains, slice(width, width + 2))):
            own = jnp.where(first, block[low], block[high])
            sent = jnp.where(first, block[high], block[low])
            own_ref[i // nb, i % nb, :, lanes] = own.astype(BF)
            sent_ref[i // nb, i % nb, :, lanes] = sent.astype(BF)


def factor_grads(rows_of, joints, gains):
    na, nb = lax.axis_size("a"), lax.axis_size("b")
    shape = (na, nb, D // (2 * na * nb), H * RA + RA * DH + 2)
    core = lax.axis_index("c").astype(jnp.int32).reshape(1)
    vmem = pl.BlockSpec(memory_space=pltpu.VMEM)
    return pl.pallas_call(
        factor_grads_body,
        in_specs=[pl.BlockSpec(memory_space=pltpu.SMEM)] + [vmem] * (2 + len(joints)),
        out_specs=[vmem, vmem],
        out_shape=[jax.ShapeDtypeStruct(shape, BF)] * 2,
        name="factor_grads",
    )(core, rows_of, gains, *joints)


def on_device(
    tokens,
    cotangent,
    domain_ids,
    block_order,
    headwise,
    headwise_mean,
    headwise_square,
    shared_factors,
    shared_factors_mean,
    shared_factors_square,
    out_weight,
    out_weight_mean,
    out_weight_square,
    gate_up,
    gate_up_mean,
    gate_up_square,
    down_weight,
    down_weight_mean,
    down_weight_square,
    norm_gains,
    norm_gains_mean,
    norm_gains_square,
):
    n_head = lax.axis_size("h")
    n_seq = lax.axis_size(SEQ)
    paired = n_head == 2
    seq_at = lax.axis_index(SEQ)
    head_at = lax.axis_index("h")
    seq_all, block_len, _ = tokens.shape
    count = seq_all // n_head
    rows = D // n_seq
    o_cols = H * DH // n_head
    h_cols = H * RA // n_head
    s_cols = RA * DH // n_head
    f_cols = FF // n_head

    shared_part = lax.dynamic_slice_in_dim(shared_factors, head_at * s_cols, s_cols, 1)
    small = jnp.concatenate([headwise, shared_part, norm_gains.T], axis=1).astype(BF)
    if n_head == 2:
        halves = ordered_gather(small, "h")
    else:
        halves = lax.all_gather(small, "h", axis=0)
    small = jnp.concatenate(
        [halves[k, :, :h_cols] for k in range(n_head)]
        + [halves[k, :, h_cols : h_cols + s_cols] for k in range(n_head)]
        + [halves[0, :, h_cols + s_cols :]],
        axis=1,
    )
    for name in ("a", "b", "c"):
        small = ordered_gather(small, name)
    small = small.transpose(2, 1, 0, 3, 4).reshape(D, H * RA + RA * DH + 2)
    w_factors = small[:, : H * RA + RA * DH]
    gains_low = small[:, H * RA + RA * DH :].T.astype(F32)
    gain_first = gains_low[0]
    gain_second = gains_low[1]

    wide_parts = (gate_up[0], gate_up[1], down_weight.T, out_weight.T)
    wide_part = jnp.concatenate([part.astype(BF) for part in wide_parts], axis=1)
    if paired:
        wide_all = lax.all_gather(turn_core_head(wide_part), ("a", "b", "h"), axis=0, tiled=True)
    else:
        wide_all = lax.all_gather(wide_part, SEQ + ("h",), axis=0)

    spots = jnp.arange(n_seq, dtype=jnp.int32)
    own_block = jnp.sum(jnp.where(spots == seq_at, block_order, 0))
    offsets = jnp.arange(block_len, dtype=jnp.int32)
    query_pos = own_block * block_len + offsets
    ahead = blocks_ahead()
    ahead_block = jnp.sum(jnp.where(spots[None, :] == ahead[:, None], block_order[None, :], 0), axis=1)
    key_pos = (ahead_block[:, None] * block_len + offsets[None, :]).reshape(1, n_seq * block_len)
    cos_t, sin_t = rope_tables(query_pos)

    tok = lax.dynamic_slice_in_dim(tokens, head_at * count, count, 0).astype(F32)
    cot = lax.dynamic_slice_in_dim(cotangent, head_at * count, count, 0).astype(F32)
    same_domain = (domain_ids[:, None] == domain_ids[None, :]).astype(F32)
    seq_weight = lax.dynamic_slice_in_dim(1.0 / jnp.sum(same_domain, axis=1), head_at * count, count, 0)
    out_grad = cot * seq_weight[:, None, None]
    out_low = out_grad.astype(BF)

    first_hat, first_inverse = normalize(tok)
    first_normalized = (first_hat * gain_first).astype(BF)
    factors = jnp.einsum("scd,dj->sjc", first_normalized, w_factors, preferred_element_type=F32)
    query, own_factors = prologue(factors, cos_t, sin_t)
    half = max(1, count // 2)
    groups = [slice(at, at + half) for at in range(0, count, half)]
    gathered = [gather_blocks(own_factors[g]) for g in groups]
    forward = []
    for at, g in enumerate(groups):
        wide, stats = attention_forward(query[g], gathered[at], key_pos, query_pos[:, None])
        if at == 0:
            wide, wide_all = lax.optimization_barrier((wide, wide_all))
        forward.append((wide, stats))
    if paired:
        w_gate = wide_all[:, :f_cols]
        w_up = wide_all[:, f_cols : 2 * f_cols]
        w_down_t = wide_all[:, 2 * f_cols : 3 * f_cols]
        own_out = wide_all[:, 3 * f_cols :]
        w_out_t = in_core_order(own_out, swap(own_out, "c"), 1)
    else:
        wide_all = wide_all.reshape(n_seq, n_head, rows, 3 * f_cols + o_cols)
        w_out_t = wide_all[..., 3 * f_cols :].transpose(0, 2, 1, 3).reshape(D, H * DH)
        wide_all = wide_all[..., : 3 * f_cols].reshape(n_seq, n_head, rows, 3, f_cols)
        wide_all = wide_all.transpose(3, 0, 2, 1, 4).reshape(3, D, FF)
        w_gate, w_up, w_down_t = wide_all[0], wide_all[1], wide_all[2]
    heads_wide = jnp.concatenate([part[0] for part in forward], axis=0)
    heads_low = heads_wide.astype(BF)
    attn = jnp.einsum("sce,de->scd", heads_low, w_out_t, preferred_element_type=F32)
    middle = tok + attn
    second_hat, second_inverse = normalize(middle)
    second_normalized = (second_hat * gain_second).astype(BF)

    tokens_own = count * block_len

    def both_cores(block):
        flat = block.reshape(tokens_own, D)
        if paired:
            return jnp.concatenate([flat, swap(flat, "c")], axis=0)
        return flat

    def own_sum(partial):
        if paired:
            partial = partial[:tokens_own] + swap(partial[tokens_own:].astype(BF), "c").astype(F32)
        return partial.reshape(count, block_len, D)

    x_low = both_cores(second_normalized)
    y_low = both_cores(out_low)
    gate = jnp.dot(x_low, w_gate, preferred_element_type=F32)
    up = jnp.dot(x_low, w_up, preferred_element_type=F32)
    sigmoid_gate = jax.nn.sigmoid(gate)
    silu_gate = gate * sigmoid_gate
    hidden_low = (silu_gate * up).astype(BF)
    ffn = own_sum(jnp.einsum("tf,df->td", hidden_low, w_down_t, preferred_element_type=F32))
    layer_low = (middle + ffn).astype(BF)
    down_low = jnp.einsum("td,tf->df", y_low, hidden_low, preferred_element_type=F32).astype(BF)
    y_low, down_low, layer_low = lax.optimization_barrier((y_low, down_low, layer_low))
    layer_all = every_head(layer_low, n_head)
    if paired:
        parts = down_low.reshape(lax.axis_size("a"), 2, 2, 2, rows // 2, f_cols)
        down_pairs = (fold_send(parts[:, :, :, 0], "h", 2), fold_send(parts[:, :, :, 1], "b", 1))

    hidden_grad = jnp.dot(y_low, w_down_t, preferred_element_type=F32)
    up_grad = (hidden_grad * silu_gate).astype(BF)
    gate_grad = (
        hidden_grad * up * (sigmoid_gate * (1.0 + gate * (1.0 - sigmoid_gate)))
    ).astype(BF)
    gate_w_grad = jnp.einsum("td,tf->df", x_low, gate_grad, preferred_element_type=F32)
    up_w_grad = jnp.einsum("td,tf->df", x_low, up_grad, preferred_element_type=F32)
    second_part = jnp.einsum("tf,df->td", gate_grad, w_gate, preferred_element_type=F32)
    second_part = second_part + jnp.einsum("tf,df->td", up_grad, w_up, preferred_element_type=F32)
    second_grad = own_sum(second_part)

    second_gain_grad = jnp.sum(second_grad * second_hat, axis=(0, 1))
    middle_grad = out_grad + norm_back(second_grad, gain_second, second_hat, second_inverse)
    middle_low = middle_grad.astype(BF)
    heads_grad = jnp.einsum("scd,de->sce", middle_low, w_out_t, preferred_element_type=F32).astype(BF)

    def out_grad_of(columns):
        return jnp.einsum("scd,sce->de", middle_low, columns, preferred_element_type=F32)

    if paired:
        core_at = lax.axis_index("c")
        mine = lax.dynamic_slice_in_dim(heads_low, core_at * o_cols, o_cols, 2)
        theirs = lax.dynamic_slice_in_dim(heads_low, (1 - core_at) * o_cols, o_cols, 2)
        sent = swap(out_grad_of(theirs).astype(BF), "c")
        out_t_grad = out_grad_of(mine) + sent.astype(F32)
    else:
        out_t_grad = out_grad_of(heads_low)
    if paired:
        wide_grads = (gate_w_grad, up_w_grad, out_t_grad)
        wide_grad = jnp.concatenate([grad.astype(BF) for grad in wide_grads], axis=1)
        wide_grad, heads_grad, layer_all = lax.optimization_barrier(
            (wide_grad, heads_grad, layer_all)
        )
        wide_sum = lax.psum_scatter(wide_grad, ("a", "b", "h"), scatter_dimension=0, tiled=True)
        wide_sum = turn_core_head(wide_sum).astype(F32)
        gate_sum = wide_sum[:, :f_cols]
        up_sum = wide_sum[:, f_cols : 2 * f_cols]
        out_sum = wide_sum[:, 2 * f_cols :]
    else:
        wide_grads = (gate_w_grad, up_w_grad, down_low, out_t_grad)
        wide_sum = jnp.concatenate([grad.astype(BF) for grad in wide_grads], axis=1)
        wide_sum = lax.psum_scatter(wide_sum, SEQ, scatter_dimension=0, tiled=True)
        wide_sum = lax.psum(wide_sum, "h").astype(F32)
        out_sum = lax.dynamic_slice_in_dim(wide_sum, 3 * FF + head_at * o_cols, o_cols, 1)
        wide_sum = wide_sum[:, : 3 * FF].reshape(rows, 3, n_head, f_cols)
        wide_sum = lax.dynamic_index_in_dim(wide_sum, head_at, 2, keepdims=False)
        gate_sum, up_sum, down_sum = wide_sum[:, 0], wide_sum[:, 1], wide_sum[:, 2]

    query_grads = []
    core_sums = []
    for at, g in enumerate(groups):
        backed = heads_grad[g]
        if at == 1:
            backed, core_sums[0] = lax.optimization_barrier((backed, core_sums[0]))
        query_grad, *pieces = attention_backward(
            query[g],
            backed,
            forward[at][0],
            forward[at][1],
            gathered[at],
            key_pos,
            query_pos[:, None],
            n_seq // 2,
        )
        query_grads.append(query_grad)
        if paired and at == 0:
            low = fold_send(fold_add(down_pairs[0], query_grad), "b", 1)
            high = fold_send(fold_add(down_pairs[1], query_grad), "h", 1)
        core_sums.append(scatter_core(*pieces))
    layer_output = layer_all.reshape(seq_all, block_len, D)
    if paired:
        low = fold_add(low, query_grads[-1])
        high = fold_add(high, query_grads[-1])
        down_own, down_sent = depth_send(jnp.concatenate([low, high], axis=1))

    first_gain_grad = 0.0
    joints = []
    input_parts = []
    own_grads = [scatter_chips(total) for total in core_sums]
    if paired:
        down_sent, own_grads[1] = lax.optimization_barrier((down_sent, own_grads[1]))
    for at, g in enumerate(groups):
        joint_grad = epilogue(query_grads[at], own_grads[at], factors[g], cos_t, sin_t)
        first_grad = jnp.einsum("scj,dj->scd", joint_grad, w_factors, preferred_element_type=F32)
        joints.append(joint_grad.reshape(-1, joint_grad.shape[2]))
        first_gain_grad = first_gain_grad + jnp.sum(first_grad * first_hat[g], axis=(0, 1))
        part = middle_grad[g] + norm_back(first_grad, gain_first, first_hat[g], first_inverse[g])
        part = part.astype(BF)
        if at + 1 < len(groups):
            part, own_grads[at + 1] = lax.optimization_barrier((part, own_grads[at + 1]))
        input_parts.append(part)

    gain_rows = jnp.stack([first_gain_grad, second_gain_grad] + [jnp.zeros(D, F32)] * 6)
    input_parts = [every_head(part, n_head) for part in input_parts]
    if len(groups) > 1:
        joints[-1] = after(joints[-1], input_parts[0])
    small_own, small_sent = factor_grads(first_normalized.reshape(-1, D), joints, gain_rows)
    small_sum = scatter_core(small_own, small_sent)
    small_sum = ordered_scatter(small_sum, "b", 1)
    small_sum = ordered_scatter(small_sum, "a", 0)
    small_sum = after(small_sum, input_parts[-1])
    small_sum = sum_over_head(small_sum, n_head).astype(F32)
    input_grad = jnp.concatenate(input_parts, axis=1).reshape(seq_all, block_len, D).astype(F32)
    if paired:
        down_sum = down_own.astype(F32)
        for part in down_sent:
            down_sum = down_sum + part.astype(F32)
        down_sum = turn_core_head(down_sum.astype(BF)).astype(F32)
    heads_sum = lax.dynamic_slice_in_dim(small_sum, head_at * h_cols, h_cols, 1)
    shared_sum = small_sum[:, H * RA : H * RA + RA * DH]
    gains_sum = small_sum[:, H * RA + RA * DH :].T
    out_sum = out_sum.T
    gate_up_sum = jnp.stack([gate_sum, up_sum])
    down_sum = down_sum.T

    rates = step_rates()
    heads_new = adam_update(headwise, headwise_mean, headwise_square, heads_sum, rates[0])
    shared_new = adam_update(
        shared_factors, shared_factors_mean, shared_factors_square, shared_sum, rates[1]
    )
    out_new = adam_update(out_weight, out_weight_mean, out_weight_square, out_sum, rates[2])
    gate_new = adam_update(gate_up, gate_up_mean, gate_up_square, gate_up_sum, rates[3])
    down_new = adam_update(down_weight, down_weight_mean, down_weight_square, down_sum, rates[4])
    gains_new = adam_update(norm_gains, norm_gains_mean, norm_gains_square, gains_sum, rates[5])
    return (
        layer_output,
        input_grad,
        *heads_new,
        *shared_new,
        *out_new,
        *gate_new,
        *down_new,
        *gains_new,
    )


def solution(mesh):
    n_seq = mesh.shape["seq"]
    n_head = mesh.shape["head"]
    inner = max(1, n_seq // 8)
    fine = Mesh(mesh.devices.reshape(n_seq // 2 // inner, inner, 2, n_head), ("a", "b", "c", "h"))
    token = P(None, SEQ, None)
    heads = P(SEQ, "h")
    shared = P(SEQ, None)
    turned = P("h", SEQ)
    gates = P(None, SEQ, "h")
    gains = P(None, SEQ)
    weights = sum(([spec] * 3 for spec in (heads, shared, turned, gates, turned, gains)), [])
    return jax.shard_map(
        on_device,
        mesh=fine,
        in_specs=(token, token, P(), P(), *weights),
        out_specs=(token, token, *weights),
        check_vma=False,
    )
```

```python
import functools

import jax
import jax.numpy as jnp
from jax import lax
from jax.experimental import pallas as pl
from jax.experimental.pallas import tpu as pltpu
from jax.sharding import Mesh
from jax.sharding import PartitionSpec as P

D = 1024
H = 16
DH = 64
RQ = 6
RK = 2
RA = RQ + 2 * RK
FF = 2816
STEP = 10
HB = 4

EPSILON = 1e-05
BETA_ONE = 0.9
BETA_TWO = 0.95
ADAM_EPS = 1e-08
DECAY = 0.1
NEGATIVE = -1e30
SCALE = DH ** (-0.5)
BF = jnp.bfloat16
F32 = jnp.float32
SEQ = ("a", "b", "c")


def rope_tables(positions):
    half_dim = DH // 2
    frequency = 10000.0 ** (-(2.0 * jnp.arange(half_dim, dtype=F32)) / DH)
    angles = frequency[:, None] * positions.astype(F32)[None, :]
    return (jnp.cos(angles), jnp.sin(angles))


def normalize(row_data):
    inverse = lax.rsqrt(jnp.mean(row_data * row_data, -1, keepdims=True) + EPSILON)
    return (row_data * inverse, inverse)


def norm_back(normed_grad, gain_row, hat_rows, inverse):
    hat_grad = normed_grad * gain_row
    return inverse * (hat_grad - hat_rows * jnp.mean(hat_grad * hat_rows, -1, keepdims=True))


def adam_update(master, mean_old, square_old, gradient, rate):
    mean_new = BETA_ONE * mean_old + (1.0 - BETA_ONE) * gradient
    square_new = BETA_TWO * square_old + (1.0 - BETA_TWO) * gradient * gradient
    mean_hat = mean_new / (1.0 - BETA_ONE**STEP)
    square_hat = square_new / (1.0 - BETA_TWO**STEP)
    master_new = master - rate * (mean_hat / (jnp.sqrt(square_hat) + ADAM_EPS) + DECAY * master)
    return (master_new, mean_new, square_new)


def step_rates():
    return (
        2.5 * (D // 4) ** (-0.5),
        2.5 * D ** (-0.5),
        2.5 * (H * DH // 32) ** (-0.5),
        2.5 * D ** (-0.5),
        2.5 * FF ** (-0.5),
        0.5,
    )


def rotated(pair, cos_t, sin_t):
    u = pair[: DH // 2]
    w = pair[DH // 2 :]
    return jnp.concatenate([u * cos_t - w * sin_t, w * cos_t + u * sin_t], axis=0)


def unrotated(pair, cos_t, sin_t):
    u = pair[: DH // 2]
    w = pair[DH // 2 :]
    return jnp.concatenate([u * cos_t + w * sin_t, w * cos_t - u * sin_t], axis=0)


def prologue_body(f_ref, cos_ref, sin_ref, q_ref, fac_ref):
    cos_t = cos_ref[...]
    sin_t = sin_ref[...]
    base = H * RA
    bq = [
        rotated(f_ref[0, base + r * DH : base + (r + 1) * DH, :], cos_t, sin_t) for r in range(RQ)
    ]
    for pair in range(H // 2):
        parts = []
        for h in (2 * pair, 2 * pair + 1):
            acc = f_ref[0, h * RA : h * RA + 1, :] * bq[0]
            for r in range(1, RQ):
                acc = acc + f_ref[0, h * RA + r : h * RA + r + 1, :] * bq[r]
            parts.append(acc)
        both = jnp.concatenate(parts, axis=0) / RQ
        rows = jnp.transpose(both).astype(BF) * SCALE
        q_ref[0, :, pair * 2 * DH : (pair + 1) * 2 * DH] = rows.astype(BF)
    for r in range(RK):
        at = base + (RQ + r) * DH
        fac_ref[0, r * 2 * DH : r * 2 * DH + DH, :] = rotated(
            f_ref[0, at : at + DH, :], cos_t, sin_t
        ).astype(BF)
        at = base + (RQ + RK + r) * DH
        fac_ref[0, r * 2 * DH + DH : (r + 1) * 2 * DH, :] = f_ref[0, at : at + DH, :].astype(BF)
    rows = [f_ref[0, h * RA + RQ : (h + 1) * RA, :] for h in range(H)]
    fac_ref[0, RK * 2 * DH :, :] = (jnp.concatenate(rows, axis=0) * (1.0 / RK)).astype(BF)


FAC = RK * 2 * DH + 2 * RK * H


def prologue(factors, cos_t, sin_t):
    count, width, block = factors.shape
    return pl.pallas_call(
        prologue_body,
        grid=(count,),
        in_specs=[
            pl.BlockSpec((1, width, block), lambda s: (s, 0, 0)),
            pl.BlockSpec((DH // 2, block), lambda s: (0, 0)),
            pl.BlockSpec((DH // 2, block), lambda s: (0, 0)),
        ],
        out_specs=[
            pl.BlockSpec((1, block, H * DH), lambda s: (s, 0, 0)),
            pl.BlockSpec((1, FAC, block), lambda s: (s, 0, 0)),
        ],
        out_shape=[
            jax.ShapeDtypeStruct((count, block, H * DH), BF),
            jax.ShapeDtypeStruct((count, FAC, block), BF),
        ],
        name="factor_prologue",
    )(factors, cos_t, sin_t)


def epilogue_body(dq_ref, df_ref, f_ref, cos_ref, sin_ref, g_ref):
    cos_t = cos_ref[...]
    sin_t = sin_ref[...]
    base = H * RA
    bq = [
        rotated(f_ref[0, base + r * DH : base + (r + 1) * DH, :], cos_t, sin_t) for r in range(RQ)
    ]
    sums = [None] * RQ
    rows = []
    wide = RK * 2 * DH
    for pair in range(H // 2):
        both = jnp.transpose(dq_ref[0, :, pair * 2 * DH : (pair + 1) * 2 * DH])
        for k in range(2):
            h = 2 * pair + k
            dq = both[k * DH : (k + 1) * DH] * (1.0 / RQ)
            for r in range(RQ):
                rows.append(jnp.sum(dq * bq[r], axis=0, keepdims=True))
                term = f_ref[0, h * RA + r : h * RA + r + 1, :] * dq
                sums[r] = term if sums[r] is None else sums[r] + term
            rows.append(df_ref[0, wide + h * 2 * RK : wide + (h + 1) * 2 * RK, :].astype(F32))
    for r in range(RQ):
        rows.append(unrotated(sums[r], cos_t, sin_t))
    for r in range(RK):
        part = df_ref[0, r * 2 * DH : r * 2 * DH + DH, :].astype(F32)
        rows.append(unrotated(part, cos_t, sin_t))
    for r in range(RK):
        rows.append(df_ref[0, r * 2 * DH + DH : (r + 1) * 2 * DH, :].astype(F32))
    g_ref[0] = jnp.transpose(jnp.concatenate(rows, axis=0)).astype(BF)


def epilogue(query_grad, factor_grad, factors, cos_t, sin_t, first, inner):
    count = query_grad.shape[0]
    _, width, block = factors.shape
    return pl.pallas_call(
        epilogue_body,
        grid=(count,),
        in_specs=[
            pl.BlockSpec((1, block, H * DH), lambda s: (s, 0, 0)),
            pl.BlockSpec((1, FAC, block), lambda s: (s + inner, 0, 0)),
            pl.BlockSpec((1, width, block), lambda s: (s + first, 0, 0)),
            pl.BlockSpec((DH // 2, block), lambda s: (0, 0)),
            pl.BlockSpec((DH // 2, block), lambda s: (0, 0)),
        ],
        out_specs=pl.BlockSpec((1, block, width), lambda s: (s, 0, 0)),
        out_shape=jax.ShapeDtypeStruct((count, block, width), BF),
        name="factor_epilogue",
    )(query_grad, factor_grad, factors, cos_t, sin_t)


def keys_values(a_rows, b_rows, h):
    a = a_rows[4 * h : 4 * h + 4]
    key_t = a[0:1] * b_rows[:DH] + a[1:2] * b_rows[2 * DH : 3 * DH]
    value_t = a[2:3] * b_rows[DH : 2 * DH] + a[3:4] * b_rows[3 * DH :]
    return key_t.astype(BF), value_t.astype(BF)


NT = (((1,), (1,)), ((), ()))
TN = (((0,), (0,)), ((), ()))


def forward_body(q_ref, b_ref, a_ref, kpos_ref, qpos_ref, o_ref, lse_ref):
    allowed = kpos_ref[...] <= qpos_ref[...]
    b_rows = b_ref[0].astype(F32)
    a_rows = a_ref[0].astype(F32)
    outs = []
    stats = []
    for h in range(HB):
        key_t, value_t = keys_values(a_rows, b_rows, h)
        scores = jnp.dot(q_ref[0, :, h * DH : (h + 1) * DH], key_t, preferred_element_type=F32)
        scores = jnp.where(allowed, scores, NEGATIVE)
        best = jnp.max(scores, axis=1, keepdims=True)
        probs = jnp.exp(scores - best)
        total = jnp.sum(probs, axis=1, keepdims=True)
        part = lax.dot_general(probs.astype(BF), value_t, NT, preferred_element_type=F32)
        outs.append(part / total)
        stats.append(best + jnp.log(total))
    o_ref[0] = jnp.concatenate(outs, axis=1)
    lse_ref[0, 0] = jnp.concatenate(stats, axis=1)


def attention_forward(query, first, gathered, key_pos, query_pos):
    _, block, width = query.shape
    count, _, length = gathered.shape
    wide = RK * 2 * DH
    return pl.pallas_call(
        forward_body,
        grid=(count, H // HB),
        in_specs=[
            pl.BlockSpec((1, block, HB * DH), lambda s, g: (s + first, 0, g)),
            pl.BlockSpec((1, wide, length), lambda s, g: (s, 0, 0)),
            pl.BlockSpec((1, 4 * HB, length), lambda s, g: (s, wide // (4 * HB) + g, 0)),
            pl.BlockSpec((1, length), lambda s, g: (0, 0)),
            pl.BlockSpec((block, 1), lambda s, g: (0, 0)),
        ],
        out_specs=[
            pl.BlockSpec((1, block, HB * DH), lambda s, g: (s, 0, g)),
            pl.BlockSpec((1, 1, block, HB), lambda s, g: (s, g, 0, 0)),
        ],
        out_shape=[
            jax.ShapeDtypeStruct((count, block, width), F32),
            jax.ShapeDtypeStruct((count, H // HB, block, HB), F32),
        ],
        cost_estimate=pl.CostEstimate(
            flops=4 * count * H * block * length * DH,
            bytes_accessed=2 * count * length * FAC,
            transcendentals=count * H * block * length,
        ),
        name="attention_forward",
    )(query, gathered, gathered, key_pos, query_pos)


def backward_body(
    q_ref, do_ref, o_ref, lse_ref, b_ref, a_ref, kpos_ref, qpos_ref, dq_ref, *refs
):
    piece_refs, acc_ref = refs[:-1], refs[-1]
    group = pl.program_id(1)
    wide = RK * 2 * DH

    @pl.when(group == 0)
    def _():
        acc_ref[...] = jnp.zeros_like(acc_ref)

    allowed = kpos_ref[...] <= qpos_ref[...]
    b_rows = b_ref[0].astype(F32)
    a_rows = a_ref[0].astype(F32)
    lse = lse_ref[0, 0]
    dqs = []
    rows = []
    for h in range(HB):
        key_t, value_t = keys_values(a_rows, b_rows, h)
        q = q_ref[0, :, h * DH : (h + 1) * DH]
        do = do_ref[0, :, h * DH : (h + 1) * DH]
        delta = jnp.sum(do.astype(F32) * o_ref[0, :, h * DH : (h + 1) * DH], axis=1, keepdims=True)
        scores = jnp.dot(q, key_t, preferred_element_type=F32)
        probs = jnp.exp(jnp.where(allowed, scores - lse[:, h : h + 1], NEGATIVE))
        prob_grad = jnp.dot(do, value_t, preferred_element_type=F32)
        score_grad = (probs * (prob_grad - delta)).astype(BF)
        dqs.append(lax.dot_general(score_grad, key_t, NT, preferred_element_type=F32) * SCALE)
        dk = lax.dot_general(q, score_grad, TN, preferred_element_type=F32)
        dv = lax.dot_general(do, probs.astype(BF), TN, preferred_element_type=F32)
        a = a_rows[4 * h : 4 * h + 4]
        acc_ref[:DH] += a[0:1] * dk
        acc_ref[DH : 2 * DH] += a[2:3] * dv
        acc_ref[2 * DH : 3 * DH] += a[1:2] * dk
        acc_ref[3 * DH :] += a[3:4] * dv
        rows.append(jnp.sum(dk * b_rows[:DH], axis=0, keepdims=True))
        rows.append(jnp.sum(dk * b_rows[2 * DH : 3 * DH], axis=0, keepdims=True))
        rows.append(jnp.sum(dv * b_rows[DH : 2 * DH], axis=0, keepdims=True))
        rows.append(jnp.sum(dv * b_rows[3 * DH :], axis=0, keepdims=True))
    dq_ref[0] = jnp.concatenate(dqs, axis=1)
    a_grad = (jnp.concatenate(rows, axis=0) * (1.0 / RK)).astype(BF)
    block = piece_refs[0].shape[3]
    depth = piece_refs[0].shape[0]
    at = pl.multiple_of(wide + group * 4 * HB, 4 * HB)
    for i, ref in enumerate(piece_refs):
        for m in range(depth):
            lanes = (i * depth + m) * block
            ref[m, 0, pl.ds(at, 4 * HB), :] = a_grad[:, lanes : lanes + block]

    @pl.when(group == pl.num_programs(1) - 1)
    def _():
        for i, ref in enumerate(piece_refs):
            for m in range(depth):
                lanes = (i * depth + m) * block
                ref[m, 0, :wide, :] = acc_ref[:, lanes : lanes + block].astype(BF)


def attention_backward(
    query, heads_grad, heads_wide, lse, gathered, key_pos, query_pos, depth, first, inner, count
):
    _, block, width = query.shape
    length = gathered.shape[2]
    wide = RK * 2 * DH
    pieces = length // (depth * block)
    return pl.pallas_call(
        backward_body,
        grid=(count, H // HB),
        in_specs=[
            pl.BlockSpec((1, block, HB * DH), lambda s, g: (s + first, 0, g)),
            pl.BlockSpec((1, block, HB * DH), lambda s, g: (s + first, 0, g)),
            pl.BlockSpec((1, block, HB * DH), lambda s, g: (s + inner, 0, g)),
            pl.BlockSpec((1, 1, block, HB), lambda s, g: (s + inner, g, 0, 0)),
            pl.BlockSpec((1, wide, length), lambda s, g: (s + inner, 0, 0)),
            pl.BlockSpec((1, 4 * HB, length), lambda s, g: (s + inner, wide // (4 * HB) + g, 0)),
            pl.BlockSpec((1, length), lambda s, g: (0, 0)),
            pl.BlockSpec((block, 1), lambda s, g: (0, 0)),
        ],
        out_specs=[pl.BlockSpec((1, block, HB * DH), lambda s, g: (s, 0, g))]
        + [pl.BlockSpec((depth, 1, FAC, block), lambda s, g: (0, s, 0, 0))] * pieces,
        out_shape=[jax.ShapeDtypeStruct((count, block, width), F32)]
        + [jax.ShapeDtypeStruct((depth, count, FAC, block), BF)] * pieces,
        scratch_shapes=[pltpu.VMEM((wide, length), F32)],
        cost_estimate=pl.CostEstimate(
            flops=10 * count * H * block * length * DH,
            bytes_accessed=4 * count * length * FAC,
            transcendentals=count * H * block * length,
        ),
        name="attention_backward",
    )(query, heads_grad, heads_wide, lse, gathered, gathered, key_pos, query_pos)


def swap(block, axis):
    return lax.ppermute(block, axis, [(0, 1), (1, 0)])


def turn_core_head(block):
    return lax.ppermute(block, ("c", "h"), [(0, 0), (1, 2), (2, 1), (3, 3)])


def from_ahead(block, axis, distance):
    size = lax.axis_size(axis)
    return lax.ppermute(block, axis, [((i + distance) % size, i) for i in range(size)])


def to_ahead(block, axis, distance):
    size = lax.axis_size(axis)
    return lax.ppermute(block, axis, [(i, (i + distance) % size) for i in range(size)])


def ordered_gather(block, axis):
    size = lax.axis_size(axis)
    spot = lax.axis_index(axis)
    if size == 2:
        other = swap(block, axis)
        mine = spot == 0
        return jnp.stack([jnp.where(mine, block, other), jnp.where(mine, other, block)])
    parts = [block] + [from_ahead(block, axis, m) for m in range(1, size)]
    twice = jnp.stack(parts + parts[:-1])
    return lax.dynamic_slice_in_dim(twice, jnp.mod(size - spot, size), size, 0)


def ordered_scatter(block, axis, dim):
    size = lax.axis_size(axis)
    spot = lax.axis_index(axis)

    def part(m):
        return lax.dynamic_index_in_dim(block, jnp.mod(spot + m, size), dim, keepdims=False)

    total = part(0).astype(F32)
    for m in range(1, size):
        total = total + to_ahead(part(m), axis, m).astype(F32)
    return total.astype(BF)


def gather_blocks(block):
    for name in ("a", "b"):
        ahead = [from_ahead(block, name, m) for m in range(1, lax.axis_size(name))]
        block = jnp.concatenate([block] + ahead, axis=2)
    return jnp.concatenate([block, swap(block, "c")], axis=2)


def blocks_ahead():
    na, nb = lax.axis_size("a"), lax.axis_size("b")
    at = [lax.axis_index(name) for name in SEQ]
    spots = []
    for mc in range(2):
        for mb in range(nb):
            for ma in range(na):
                a = jnp.mod(at[0] + ma, na)
                b = jnp.mod(at[1] + mb, nb)
                spots.append((a * nb + b) * 2 + jnp.mod(at[2] + mc, 2))
    return jnp.stack(spots)


def scatter_core(own, theirs):
    return (own.astype(F32) + swap(theirs, "c").astype(F32)).astype(BF)


def scatter_axis(total, name):
    size = lax.axis_size(name)
    total = total.reshape(size, total.shape[0] // size, *total.shape[1:])
    part = total[0].astype(F32)
    for m in range(1, size):
        part = part + to_ahead(total[m], name, m).astype(F32)
    return part.astype(BF)


def sum_over_head(block, n_head):
    if n_head == 2:
        return block + swap(block, "h")
    return lax.psum(block, "h")


def in_core_order(own, other, axis):
    first = lax.axis_index("c") == 0
    return jnp.concatenate([jnp.where(first, own, other), jnp.where(first, other, own)], axis=axis)


def every_head(block, n_head):
    if n_head == 2:
        other = swap(block, "h")
        mine = lax.axis_index("h") == 0
        return jnp.stack([jnp.where(mine, block, other), jnp.where(mine, other, block)])
    return lax.all_gather(block, "h", axis=0)


def factor_grads_body(core_ref, x_ref, gain_ref, *refs):
    joint_refs, own_ref, sent_ref = refs[:-2], refs[-2], refs[-1]
    total = None
    at = 0
    for ref in joint_refs:
        size = ref.shape[0]
        part = lax.dot_general(x_ref[at : at + size, :], ref[...], TN, preferred_element_type=F32)
        total = part if total is None else total + part
        at += size
    na, nb, rows, _ = own_ref.shape
    width = total.shape[1]
    first = core_ref[0] == 0
    gains = jnp.transpose(gain_ref[...])[:, :2]
    for i in range(na * nb):
        low = slice(2 * i * rows, (2 * i + 1) * rows)
        high = slice((2 * i + 1) * rows, (2 * i + 2) * rows)
        for block, lanes in ((total, slice(0, width)), (gains, slice(width, width + 2))):
            own = jnp.where(first, block[low], block[high])
            sent = jnp.where(first, block[high], block[low])
            own_ref[i // nb, i % nb, :, lanes] = own.astype(BF)
            sent_ref[i // nb, i % nb, :, lanes] = sent.astype(BF)


def factor_grads(rows_of, joints, gains):
    na, nb = lax.axis_size("a"), lax.axis_size("b")
    shape = (na, nb, D // (2 * na * nb), H * RA + RA * DH + 2)
    core = lax.axis_index("c").astype(jnp.int32).reshape(1)
    vmem = pl.BlockSpec(memory_space=pltpu.VMEM)
    return pl.pallas_call(
        factor_grads_body,
        in_specs=[pl.BlockSpec(memory_space=pltpu.SMEM)] + [vmem] * (2 + len(joints)),
        out_specs=[vmem, vmem],
        out_shape=[jax.ShapeDtypeStruct(shape, BF)] * 2,
        name="factor_grads",
    )(core, rows_of, gains, *joints)


def on_device(
    tokens,
    cotangent,
    domain_ids,
    block_order,
    headwise,
    headwise_mean,
    headwise_square,
    shared_factors,
    shared_factors_mean,
    shared_factors_square,
    out_weight,
    out_weight_mean,
    out_weight_square,
    gate_up,
    gate_up_mean,
    gate_up_square,
    down_weight,
    down_weight_mean,
    down_weight_square,
    norm_gains,
    norm_gains_mean,
    norm_gains_square,
):
    n_head = lax.axis_size("h")
    n_seq = lax.axis_size(SEQ)
    paired = n_head == 2
    seq_at = lax.axis_index(SEQ)
    head_at = lax.axis_index("h")
    seq_all, block_len, _ = tokens.shape
    count = seq_all // n_head
    rows = D // n_seq
    o_cols = H * DH // n_head
    h_cols = H * RA // n_head
    s_cols = RA * DH // n_head
    f_cols = FF // n_head

    shared_part = lax.dynamic_slice_in_dim(shared_factors, head_at * s_cols, s_cols, 1)
    small = jnp.concatenate([headwise, shared_part, norm_gains.T], axis=1).astype(BF)
    if n_head == 2:
        halves = ordered_gather(small, "h")
    else:
        halves = lax.all_gather(small, "h", axis=0)
    small = jnp.concatenate(
        [halves[k, :, :h_cols] for k in range(n_head)]
        + [halves[k, :, h_cols : h_cols + s_cols] for k in range(n_head)]
        + [halves[0, :, h_cols + s_cols :]],
        axis=1,
    )
    for name in ("a", "b", "c"):
        small = ordered_gather(small, name)
    small = small.transpose(2, 1, 0, 3, 4).reshape(D, H * RA + RA * DH + 2)
    w_factors = small[:, : H * RA + RA * DH]
    gains_low = small[:, H * RA + RA * DH :].T.astype(F32)
    gain_first = gains_low[0]
    gain_second = gains_low[1]

    wide_parts = (gate_up[0], gate_up[1], down_weight.T, out_weight.T)
    wide_part = jnp.concatenate([part.astype(BF) for part in wide_parts], axis=1)
    if paired:
        wide_all = lax.all_gather(turn_core_head(wide_part), ("a", "b", "h"), axis=0, tiled=True)
    else:
        wide_all = lax.all_gather(wide_part, SEQ + ("h",), axis=0)

    spots = jnp.arange(n_seq, dtype=jnp.int32)
    own_block = jnp.sum(jnp.where(spots == seq_at, block_order, 0))
    offsets = jnp.arange(block_len, dtype=jnp.int32)
    query_pos = own_block * block_len + offsets
    ahead = blocks_ahead()
    ahead_block = jnp.sum(jnp.where(spots[None, :] == ahead[:, None], block_order[None, :], 0), axis=1)
    key_pos = (ahead_block[:, None] * block_len + offsets[None, :]).reshape(1, n_seq * block_len)
    cos_t, sin_t = rope_tables(query_pos)

    tok = lax.dynamic_slice_in_dim(tokens, head_at * count, count, 0).astype(F32)
    cot = lax.dynamic_slice_in_dim(cotangent, head_at * count, count, 0).astype(F32)
    same_domain = (domain_ids[:, None] == domain_ids[None, :]).astype(F32)
    seq_weight = lax.dynamic_slice_in_dim(1.0 / jnp.sum(same_domain, axis=1), head_at * count, count, 0)
    out_grad = cot * seq_weight[:, None, None]
    out_low = out_grad.astype(BF)

    first_hat, first_inverse = normalize(tok)
    first_normalized = (first_hat * gain_first).astype(BF)
    factors = jnp.einsum("scd,dj->sjc", first_normalized, w_factors, preferred_element_type=F32)
    query, own_factors = prologue(factors, cos_t, sin_t)
    half = max(1, count // 2)
    groups = [slice(at, at + half) for at in range(0, count, half)]
    gathered = [gather_blocks(own_factors[g]) for g in groups]
    forward = []
    for at, g in enumerate(groups):
        wide, stats = attention_forward(query, g.start, gathered[at], key_pos, query_pos[:, None])
        if at == 0:
            wide, wide_all = lax.optimization_barrier((wide, wide_all))
        forward.append((wide, stats))
    if paired:
        w_gate = wide_all[:, :f_cols]
        w_up = wide_all[:, f_cols : 2 * f_cols]
        w_down_t = wide_all[:, 2 * f_cols : 3 * f_cols]
        own_out = wide_all[:, 3 * f_cols :]
        w_out_t = in_core_order(own_out, swap(own_out, "c"), 1)
    else:
        wide_all = wide_all.reshape(n_seq, n_head, rows, 3 * f_cols + o_cols)
        w_out_t = wide_all[..., 3 * f_cols :].transpose(0, 2, 1, 3).reshape(D, H * DH)
        wide_all = wide_all[..., : 3 * f_cols].reshape(n_seq, n_head, rows, 3, f_cols)
        wide_all = wide_all.transpose(3, 0, 2, 1, 4).reshape(3, D, FF)
        w_gate, w_up, w_down_t = wide_all[0], wide_all[1], wide_all[2]
    heads_wide = jnp.concatenate([part[0] for part in forward], axis=0)
    heads_low = heads_wide.astype(BF)
    attn = jnp.einsum("sce,de->scd", heads_low, w_out_t, preferred_element_type=F32)
    middle = tok + attn
    second_hat, second_inverse = normalize(middle)
    second_normalized = (second_hat * gain_second).astype(BF)

    tokens_own = count * block_len

    def both_cores(block):
        flat = block.reshape(tokens_own, D)
        if paired:
            return jnp.concatenate([flat, swap(flat, "c")], axis=0)
        return flat

    def own_sum(partial):
        if paired:
            partial = partial[:tokens_own] + swap(partial[tokens_own:].astype(BF), "c").astype(F32)
        return partial.reshape(count, block_len, D)

    x_low = both_cores(second_normalized)
    y_low = both_cores(out_low)
    gate = jnp.dot(x_low, w_gate, preferred_element_type=F32)
    up = jnp.dot(x_low, w_up, preferred_element_type=F32)
    sigmoid_gate = jax.nn.sigmoid(gate)
    silu_gate = gate * sigmoid_gate
    hidden_low = (silu_gate * up).astype(BF)
    ffn = own_sum(jnp.einsum("tf,df->td", hidden_low, w_down_t, preferred_element_type=F32))
    layer_low = (middle + ffn).astype(BF)
    down_low = jnp.einsum("td,tf->df", y_low, hidden_low, preferred_element_type=F32).astype(BF)
    layer_all = every_head(layer_low, n_head)
    hidden_grad = jnp.dot(y_low, w_down_t, preferred_element_type=F32)
    up_grad = (hidden_grad * silu_gate).astype(BF)
    gate_grad = (
        hidden_grad * up * (sigmoid_gate * (1.0 + gate * (1.0 - sigmoid_gate)))
    ).astype(BF)
    gate_w_grad = jnp.einsum("td,tf->df", x_low, gate_grad, preferred_element_type=F32)
    up_w_grad = jnp.einsum("td,tf->df", x_low, up_grad, preferred_element_type=F32)
    second_part = jnp.einsum("tf,df->td", gate_grad, w_gate, preferred_element_type=F32)
    second_part = second_part + jnp.einsum("tf,df->td", up_grad, w_up, preferred_element_type=F32)
    second_grad = own_sum(second_part)

    second_gain_grad = jnp.sum(second_grad * second_hat, axis=(0, 1))
    middle_grad = out_grad + norm_back(second_grad, gain_second, second_hat, second_inverse)
    middle_low = middle_grad.astype(BF)
    heads_grad = jnp.einsum("scd,de->sce", middle_low, w_out_t, preferred_element_type=F32).astype(BF)

    def out_grad_of(columns):
        return jnp.einsum("scd,sce->de", middle_low, columns, preferred_element_type=F32)

    if paired:
        core_at = lax.axis_index("c")
        mine = lax.dynamic_slice_in_dim(heads_low, core_at * o_cols, o_cols, 2)
        theirs = lax.dynamic_slice_in_dim(heads_low, (1 - core_at) * o_cols, o_cols, 2)
        sent = swap(out_grad_of(theirs).astype(BF), "c")
        out_t_grad = out_grad_of(mine) + sent.astype(F32)
    else:
        out_t_grad = out_grad_of(heads_low)
    if paired:
        wide_grads = (gate_w_grad, up_w_grad, down_low, out_t_grad)
        wide_grad = jnp.concatenate([grad.astype(BF) for grad in wide_grads], axis=1)
        wide_grad, heads_grad, layer_all = lax.optimization_barrier(
            (wide_grad, heads_grad, layer_all)
        )
        wide_sum = lax.psum_scatter(wide_grad, ("a", "b", "h"), scatter_dimension=0, tiled=True)
        wide_sum = turn_core_head(wide_sum).astype(F32)
        gate_sum = wide_sum[:, :f_cols]
        up_sum = wide_sum[:, f_cols : 2 * f_cols]
        down_sum = wide_sum[:, 2 * f_cols : 3 * f_cols]
        out_sum = wide_sum[:, 3 * f_cols :]
    else:
        wide_grads = (gate_w_grad, up_w_grad, down_low, out_t_grad)
        wide_sum = jnp.concatenate([grad.astype(BF) for grad in wide_grads], axis=1)
        wide_sum = lax.psum_scatter(wide_sum, SEQ, scatter_dimension=0, tiled=True)
        wide_sum = lax.psum(wide_sum, "h").astype(F32)
        out_sum = lax.dynamic_slice_in_dim(wide_sum, 3 * FF + head_at * o_cols, o_cols, 1)
        wide_sum = wide_sum[:, : 3 * FF].reshape(rows, 3, n_head, f_cols)
        wide_sum = lax.dynamic_index_in_dim(wide_sum, head_at, 2, keepdims=False)
        gate_sum, up_sum, down_sum = wide_sum[:, 0], wide_sum[:, 1], wide_sum[:, 2]

    def backward_call(at, inner, size, backed):
        query_grad, *pieces = attention_backward(
            query,
            backed,
            forward[at][0],
            forward[at][1],
            gathered[at],
            key_pos,
            query_pos[:, None],
            n_seq // 2,
            groups[at].start + inner,
            inner,
            size,
        )
        return query_grad, scatter_core(*pieces)

    query_grads = []
    own_grads = []
    if len(groups) > 1:
        query_grad, total = backward_call(0, 0, half, heads_grad)
        heads_grad, total = lax.optimization_barrier((heads_grad, total))
        query_grads.append([query_grad])
        total = scatter_axis(total, "b")
        own_grads.append(total)
    last = len(groups) - 1
    sizes = [half // 2, half - half // 2] if half > 1 else [half]
    inner = 0
    calls = []
    for i, size in enumerate(sizes):
        if i and last:
            heads_grad, own_grads[0] = lax.optimization_barrier((heads_grad, own_grads[0]))
        calls.append(backward_call(last, inner, size, heads_grad))
        inner += size
    query_grads.append([call[0] for call in calls])
    own_grads.append(scatter_axis(jnp.concatenate([call[1] for call in calls], axis=1), "b"))
    own_grads = [scatter_axis(total, "a")[0] for total in own_grads]
    layer_output = layer_all.reshape(seq_all, block_len, D)
    first_gain_grad = 0.0
    joints = []
    input_parts = []
    for at, g in enumerate(groups):
        inner = 0
        parts = []
        for query_grad in query_grads[at]:
            parts.append(
                epilogue(query_grad, own_grads[at], factors, cos_t, sin_t, g.start + inner, inner)
            )
            inner += query_grad.shape[0]
        joint_grad = jnp.concatenate(parts, axis=0)
        first_grad = jnp.einsum("scj,dj->scd", joint_grad, w_factors, preferred_element_type=F32)
        joints.append(joint_grad.reshape(-1, joint_grad.shape[2]))
        first_gain_grad = first_gain_grad + jnp.sum(first_grad * first_hat[g], axis=(0, 1))
        part = middle_grad[g] + norm_back(first_grad, gain_first, first_hat[g], first_inverse[g])
        part = part.astype(BF)
        if at + 1 < len(groups):
            part, own_grads[at + 1] = lax.optimization_barrier((part, own_grads[at + 1]))
        input_parts.append(part)

    gain_rows = jnp.stack([first_gain_grad, second_gain_grad] + [jnp.zeros(D, F32)] * 6)
    input_parts = [every_head(part, n_head) for part in input_parts]
    if len(groups) > 1:
        joints[-1], input_parts[0] = lax.optimization_barrier((joints[-1], input_parts[0]))
    small_own, small_sent = factor_grads(first_normalized.reshape(-1, D), joints, gain_rows)
    small_sum = scatter_core(small_own, small_sent)
    small_sum = ordered_scatter(small_sum, "b", 1)
    small_sum = ordered_scatter(small_sum, "a", 0)
    small_sum, input_parts[-1] = lax.optimization_barrier((small_sum, input_parts[-1]))
    small_sum = sum_over_head(small_sum, n_head).astype(F32)
    input_grad = jnp.concatenate(input_parts, axis=1).reshape(seq_all, block_len, D).astype(F32)
    heads_sum = lax.dynamic_slice_in_dim(small_sum, head_at * h_cols, h_cols, 1)
    shared_sum = small_sum[:, H * RA : H * RA + RA * DH]
    gains_sum = small_sum[:, H * RA + RA * DH :].T
    out_sum = out_sum.T
    gate_up_sum = jnp.stack([gate_sum, up_sum])
    down_sum = down_sum.T

    rates = step_rates()
    heads_new = adam_update(headwise, headwise_mean, headwise_square, heads_sum, rates[0])
    shared_new = adam_update(
        shared_factors, shared_factors_mean, shared_factors_square, shared_sum, rates[1]
    )
    out_new = adam_update(out_weight, out_weight_mean, out_weight_square, out_sum, rates[2])
    gate_new = adam_update(gate_up, gate_up_mean, gate_up_square, gate_up_sum, rates[3])
    down_new = adam_update(down_weight, down_weight_mean, down_weight_square, down_sum, rates[4])
    gains_new = adam_update(norm_gains, norm_gains_mean, norm_gains_square, gains_sum, rates[5])
    return (
        layer_output,
        input_grad,
        *heads_new,
        *shared_new,
        *out_new,
        *gate_new,
        *down_new,
        *gains_new,
    )


def solution(mesh):
    n_seq = mesh.shape["seq"]
    n_head = mesh.shape["head"]
    inner = max(1, n_seq // 8)
    fine = Mesh(mesh.devices.reshape(n_seq // 2 // inner, inner, 2, n_head), ("a", "b", "c", "h"))
    token = P(None, SEQ, None)
    heads = P(SEQ, "h")
    shared = P(SEQ, None)
    turned = P("h", SEQ)
    gates = P(None, SEQ, "h")
    gains = P(None, SEQ)
    weights = sum(([spec] * 3 for spec in (heads, shared, turned, gates, turned, gains)), [])
    return jax.shard_map(
        on_device,
        mesh=fine,
        in_specs=(token, token, P(), P(), *weights),
        out_specs=(token, token, *weights),
        check_vma=False,
    )
```

```python
import functools

import jax
import jax.numpy as jnp
from jax import lax
from jax.experimental import pallas as pl
from jax.experimental.pallas import tpu as pltpu
from jax.sharding import Mesh
from jax.sharding import PartitionSpec as P

D = 1024
H = 16
DH = 64
RQ = 6
RK = 2
RA = RQ + 2 * RK
FF = 2816
STEP = 10
HB = 4

EPSILON = 1e-05
BETA_ONE = 0.9
BETA_TWO = 0.95
ADAM_EPS = 1e-08
DECAY = 0.1
NEGATIVE = -1e30
SCALE = DH ** (-0.5)
BF = jnp.bfloat16
F32 = jnp.float32
SEQ = ("a", "b", "c")


def rope_tables(positions):
    half_dim = DH // 2
    frequency = 10000.0 ** (-(2.0 * jnp.arange(half_dim, dtype=F32)) / DH)
    angles = frequency[:, None] * positions.astype(F32)[None, :]
    return (jnp.cos(angles), jnp.sin(angles))


def normalize(row_data):
    inverse = lax.rsqrt(jnp.mean(row_data * row_data, -1, keepdims=True) + EPSILON)
    return (row_data * inverse, inverse)


def norm_back(normed_grad, gain_row, hat_rows, inverse):
    hat_grad = normed_grad * gain_row
    return inverse * (hat_grad - hat_rows * jnp.mean(hat_grad * hat_rows, -1, keepdims=True))


def adam_update(master, mean_old, square_old, gradient, rate):
    mean_new = BETA_ONE * mean_old + (1.0 - BETA_ONE) * gradient
    square_new = BETA_TWO * square_old + (1.0 - BETA_TWO) * gradient * gradient
    mean_hat = mean_new / (1.0 - BETA_ONE**STEP)
    square_hat = square_new / (1.0 - BETA_TWO**STEP)
    master_new = master - rate * (mean_hat / (jnp.sqrt(square_hat) + ADAM_EPS) + DECAY * master)
    return (master_new, mean_new, square_new)


def step_rates():
    return (
        2.5 * (D // 4) ** (-0.5),
        2.5 * D ** (-0.5),
        2.5 * (H * DH // 32) ** (-0.5),
        2.5 * D ** (-0.5),
        2.5 * FF ** (-0.5),
        0.5,
    )


def rotated(pair, cos_t, sin_t):
    u = pair[: DH // 2]
    w = pair[DH // 2 :]
    return jnp.concatenate([u * cos_t - w * sin_t, w * cos_t + u * sin_t], axis=0)


def unrotated(pair, cos_t, sin_t):
    u = pair[: DH // 2]
    w = pair[DH // 2 :]
    return jnp.concatenate([u * cos_t + w * sin_t, w * cos_t - u * sin_t], axis=0)


def prologue_body(f_ref, cos_ref, sin_ref, q_ref, fac_ref):
    cos_t = cos_ref[...]
    sin_t = sin_ref[...]
    base = H * RA
    bq = [
        rotated(f_ref[0, base + r * DH : base + (r + 1) * DH, :], cos_t, sin_t) for r in range(RQ)
    ]
    for pair in range(H // 2):
        parts = []
        for h in (2 * pair, 2 * pair + 1):
            acc = f_ref[0, h * RA : h * RA + 1, :] * bq[0]
            for r in range(1, RQ):
                acc = acc + f_ref[0, h * RA + r : h * RA + r + 1, :] * bq[r]
            parts.append(acc)
        both = jnp.concatenate(parts, axis=0) / RQ
        rows = jnp.transpose(both).astype(BF) * SCALE
        q_ref[0, :, pair * 2 * DH : (pair + 1) * 2 * DH] = rows.astype(BF)
    for r in range(RK):
        at = base + (RQ + r) * DH
        fac_ref[0, r * 2 * DH : r * 2 * DH + DH, :] = rotated(
            f_ref[0, at : at + DH, :], cos_t, sin_t
        ).astype(BF)
        at = base + (RQ + RK + r) * DH
        fac_ref[0, r * 2 * DH + DH : (r + 1) * 2 * DH, :] = f_ref[0, at : at + DH, :].astype(BF)
    rows = [f_ref[0, h * RA + RQ : (h + 1) * RA, :] for h in range(H)]
    fac_ref[0, RK * 2 * DH :, :] = (jnp.concatenate(rows, axis=0) * (1.0 / RK)).astype(BF)


FAC = RK * 2 * DH + 2 * RK * H


def prologue(factors, cos_t, sin_t):
    count, width, block = factors.shape
    return pl.pallas_call(
        prologue_body,
        grid=(count,),
        in_specs=[
            pl.BlockSpec((1, width, block), lambda s: (s, 0, 0)),
            pl.BlockSpec((DH // 2, block), lambda s: (0, 0)),
            pl.BlockSpec((DH // 2, block), lambda s: (0, 0)),
        ],
        out_specs=[
            pl.BlockSpec((1, block, H * DH), lambda s: (s, 0, 0)),
            pl.BlockSpec((1, FAC, block), lambda s: (s, 0, 0)),
        ],
        out_shape=[
            jax.ShapeDtypeStruct((count, block, H * DH), BF),
            jax.ShapeDtypeStruct((count, FAC, block), BF),
        ],
        name="factor_prologue",
    )(factors, cos_t, sin_t)


def epilogue_body(dq_ref, df_ref, f_ref, cos_ref, sin_ref, g_ref):
    cos_t = cos_ref[...]
    sin_t = sin_ref[...]
    base = H * RA
    bq = [
        rotated(f_ref[0, base + r * DH : base + (r + 1) * DH, :], cos_t, sin_t) for r in range(RQ)
    ]
    sums = [None] * RQ
    rows = []
    wide = RK * 2 * DH
    for pair in range(H // 2):
        both = jnp.transpose(dq_ref[0, :, pair * 2 * DH : (pair + 1) * 2 * DH])
        for k in range(2):
            h = 2 * pair + k
            dq = both[k * DH : (k + 1) * DH] * (1.0 / RQ)
            for r in range(RQ):
                rows.append(jnp.sum(dq * bq[r], axis=0, keepdims=True))
                term = f_ref[0, h * RA + r : h * RA + r + 1, :] * dq
                sums[r] = term if sums[r] is None else sums[r] + term
            rows.append(df_ref[0, wide + h * 2 * RK : wide + (h + 1) * 2 * RK, :].astype(F32))
    for r in range(RQ):
        rows.append(unrotated(sums[r], cos_t, sin_t))
    for r in range(RK):
        part = df_ref[0, r * 2 * DH : r * 2 * DH + DH, :].astype(F32)
        rows.append(unrotated(part, cos_t, sin_t))
    for r in range(RK):
        rows.append(df_ref[0, r * 2 * DH + DH : (r + 1) * 2 * DH, :].astype(F32))
    g_ref[0] = jnp.transpose(jnp.concatenate(rows, axis=0)).astype(BF)


def epilogue(query_grad, factor_grad, factors, cos_t, sin_t, first, inner):
    count = query_grad.shape[0]
    _, width, block = factors.shape
    return pl.pallas_call(
        epilogue_body,
        grid=(count,),
        in_specs=[
            pl.BlockSpec((1, block, H * DH), lambda s: (s, 0, 0)),
            pl.BlockSpec((1, FAC, block), lambda s: (s + inner, 0, 0)),
            pl.BlockSpec((1, width, block), lambda s: (s + first, 0, 0)),
            pl.BlockSpec((DH // 2, block), lambda s: (0, 0)),
            pl.BlockSpec((DH // 2, block), lambda s: (0, 0)),
        ],
        out_specs=pl.BlockSpec((1, block, width), lambda s: (s, 0, 0)),
        out_shape=jax.ShapeDtypeStruct((count, block, width), BF),
        name="factor_epilogue",
    )(query_grad, factor_grad, factors, cos_t, sin_t)


def keys_values(a_rows, b_rows, h):
    a = a_rows[4 * h : 4 * h + 4]
    key_t = a[0:1] * b_rows[:DH] + a[1:2] * b_rows[2 * DH : 3 * DH]
    value_t = a[2:3] * b_rows[DH : 2 * DH] + a[3:4] * b_rows[3 * DH :]
    return key_t.astype(BF), value_t.astype(BF)


NT = (((1,), (1,)), ((), ()))
TN = (((0,), (0,)), ((), ()))


def forward_body(q_ref, b_ref, a_ref, kpos_ref, qpos_ref, o_ref, lse_ref):
    allowed = kpos_ref[...] <= qpos_ref[...]
    b_rows = b_ref[0].astype(F32)
    a_rows = a_ref[0].astype(F32)
    outs = []
    stats = []
    for h in range(HB):
        key_t, value_t = keys_values(a_rows, b_rows, h)
        scores = jnp.dot(q_ref[0, :, h * DH : (h + 1) * DH], key_t, preferred_element_type=F32)
        scores = jnp.where(allowed, scores, NEGATIVE)
        best = jnp.max(scores, axis=1, keepdims=True)
        probs = jnp.exp(scores - best)
        total = jnp.sum(probs, axis=1, keepdims=True)
        part = lax.dot_general(probs.astype(BF), value_t, NT, preferred_element_type=F32)
        outs.append(part / total)
        stats.append(best + jnp.log(total))
    o_ref[0] = jnp.concatenate(outs, axis=1)
    lse_ref[0, 0] = jnp.concatenate(stats, axis=1)


def attention_forward(query, first, gathered, key_pos, query_pos):
    _, block, width = query.shape
    count, _, length = gathered.shape
    wide = RK * 2 * DH
    return pl.pallas_call(
        forward_body,
        grid=(count, H // HB),
        in_specs=[
            pl.BlockSpec((1, block, HB * DH), lambda s, g: (s + first, 0, g)),
            pl.BlockSpec((1, wide, length), lambda s, g: (s, 0, 0)),
            pl.BlockSpec((1, 4 * HB, length), lambda s, g: (s, wide // (4 * HB) + g, 0)),
            pl.BlockSpec((1, length), lambda s, g: (0, 0)),
            pl.BlockSpec((block, 1), lambda s, g: (0, 0)),
        ],
        out_specs=[
            pl.BlockSpec((1, block, HB * DH), lambda s, g: (s, 0, g)),
            pl.BlockSpec((1, 1, block, HB), lambda s, g: (s, g, 0, 0)),
        ],
        out_shape=[
            jax.ShapeDtypeStruct((count, block, width), F32),
            jax.ShapeDtypeStruct((count, H // HB, block, HB), F32),
        ],
        cost_estimate=pl.CostEstimate(
            flops=4 * count * H * block * length * DH,
            bytes_accessed=2 * count * length * FAC,
            transcendentals=count * H * block * length,
        ),
        name="attention_forward",
    )(query, gathered, gathered, key_pos, query_pos)


def backward_body(
    q_ref, do_ref, o_ref, lse_ref, b_ref, a_ref, kpos_ref, qpos_ref, dq_ref, *refs
):
    piece_refs, acc_ref = refs[:-1], refs[-1]
    group = pl.program_id(1)
    wide = RK * 2 * DH

    @pl.when(group == 0)
    def _():
        acc_ref[...] = jnp.zeros_like(acc_ref)

    allowed = kpos_ref[...] <= qpos_ref[...]
    b_rows = b_ref[0].astype(F32)
    a_rows = a_ref[0].astype(F32)
    lse = lse_ref[0, 0]
    dqs = []
    rows = []
    for h in range(HB):
        key_t, value_t = keys_values(a_rows, b_rows, h)
        q = q_ref[0, :, h * DH : (h + 1) * DH]
        do = do_ref[0, :, h * DH : (h + 1) * DH]
        delta = jnp.sum(do.astype(F32) * o_ref[0, :, h * DH : (h + 1) * DH], axis=1, keepdims=True)
        scores = jnp.dot(q, key_t, preferred_element_type=F32)
        probs = jnp.exp(jnp.where(allowed, scores - lse[:, h : h + 1], NEGATIVE))
        prob_grad = jnp.dot(do, value_t, preferred_element_type=F32)
        score_grad = (probs * (prob_grad - delta)).astype(BF)
        dqs.append(lax.dot_general(score_grad, key_t, NT, preferred_element_type=F32) * SCALE)
        dk = lax.dot_general(q, score_grad, TN, preferred_element_type=F32)
        dv = lax.dot_general(do, probs.astype(BF), TN, preferred_element_type=F32)
        a = a_rows[4 * h : 4 * h + 4]
        acc_ref[:DH] += a[0:1] * dk
        acc_ref[DH : 2 * DH] += a[2:3] * dv
        acc_ref[2 * DH : 3 * DH] += a[1:2] * dk
        acc_ref[3 * DH :] += a[3:4] * dv
        rows.append(jnp.sum(dk * b_rows[:DH], axis=0, keepdims=True))
        rows.append(jnp.sum(dk * b_rows[2 * DH : 3 * DH], axis=0, keepdims=True))
        rows.append(jnp.sum(dv * b_rows[DH : 2 * DH], axis=0, keepdims=True))
        rows.append(jnp.sum(dv * b_rows[3 * DH :], axis=0, keepdims=True))
    dq_ref[0] = jnp.concatenate(dqs, axis=1)
    a_grad = (jnp.concatenate(rows, axis=0) * (1.0 / RK)).astype(BF)
    block = piece_refs[0].shape[3]
    depth = piece_refs[0].shape[0]
    at = pl.multiple_of(wide + group * 4 * HB, 4 * HB)
    for i, ref in enumerate(piece_refs):
        for m in range(depth):
            lanes = (i * depth + m) * block
            ref[m, 0, pl.ds(at, 4 * HB), :] = a_grad[:, lanes : lanes + block]

    @pl.when(group == pl.num_programs(1) - 1)
    def _():
        for i, ref in enumerate(piece_refs):
            for m in range(depth):
                lanes = (i * depth + m) * block
                ref[m, 0, :wide, :] = acc_ref[:, lanes : lanes + block].astype(BF)


def attention_backward(
    query, heads_grad, heads_wide, lse, gathered, key_pos, query_pos, depth, first, inner, count
):
    _, block, width = query.shape
    length = gathered.shape[2]
    wide = RK * 2 * DH
    pieces = length // (depth * block)
    return pl.pallas_call(
        backward_body,
        grid=(count, H // HB),
        in_specs=[
            pl.BlockSpec((1, block, HB * DH), lambda s, g: (s + first, 0, g)),
            pl.BlockSpec((1, block, HB * DH), lambda s, g: (s + first, 0, g)),
            pl.BlockSpec((1, block, HB * DH), lambda s, g: (s + inner, 0, g)),
            pl.BlockSpec((1, 1, block, HB), lambda s, g: (s + inner, g, 0, 0)),
            pl.BlockSpec((1, wide, length), lambda s, g: (s + inner, 0, 0)),
            pl.BlockSpec((1, 4 * HB, length), lambda s, g: (s + inner, wide // (4 * HB) + g, 0)),
            pl.BlockSpec((1, length), lambda s, g: (0, 0)),
            pl.BlockSpec((block, 1), lambda s, g: (0, 0)),
        ],
        out_specs=[pl.BlockSpec((1, block, HB * DH), lambda s, g: (s, 0, g))]
        + [pl.BlockSpec((depth, 1, FAC, block), lambda s, g: (0, s, 0, 0))] * pieces,
        out_shape=[jax.ShapeDtypeStruct((count, block, width), F32)]
        + [jax.ShapeDtypeStruct((depth, count, FAC, block), BF)] * pieces,
        scratch_shapes=[pltpu.VMEM((wide, length), F32)],
        cost_estimate=pl.CostEstimate(
            flops=10 * count * H * block * length * DH,
            bytes_accessed=4 * count * length * FAC,
            transcendentals=count * H * block * length,
        ),
        name="attention_backward",
    )(query, heads_grad, heads_wide, lse, gathered, gathered, key_pos, query_pos)


def swap(block, axis):
    return lax.ppermute(block, axis, [(0, 1), (1, 0)])


def turn_core_head(block):
    return lax.ppermute(block, ("c", "h"), [(0, 0), (1, 2), (2, 1), (3, 3)])


def from_ahead(block, axis, distance):
    size = lax.axis_size(axis)
    return lax.ppermute(block, axis, [((i + distance) % size, i) for i in range(size)])


def to_ahead(block, axis, distance):
    size = lax.axis_size(axis)
    return lax.ppermute(block, axis, [(i, (i + distance) % size) for i in range(size)])


def ordered_gather(block, axis):
    size = lax.axis_size(axis)
    spot = lax.axis_index(axis)
    if size == 2:
        other = swap(block, axis)
        mine = spot == 0
        return jnp.stack([jnp.where(mine, block, other), jnp.where(mine, other, block)])
    parts = [block] + [from_ahead(block, axis, m) for m in range(1, size)]
    twice = jnp.stack(parts + parts[:-1])
    return lax.dynamic_slice_in_dim(twice, jnp.mod(size - spot, size), size, 0)


def ordered_scatter(block, axis, dim):
    size = lax.axis_size(axis)
    spot = lax.axis_index(axis)

    def part(m):
        return lax.dynamic_index_in_dim(block, jnp.mod(spot + m, size), dim, keepdims=False)

    total = part(0).astype(F32)
    for m in range(1, size):
        total = total + to_ahead(part(m), axis, m).astype(F32)
    return total.astype(BF)


def gather_blocks(block):
    for name in ("a", "b"):
        ahead = [from_ahead(block, name, m) for m in range(1, lax.axis_size(name))]
        block = jnp.concatenate([block] + ahead, axis=2)
    return jnp.concatenate([block, swap(block, "c")], axis=2)


def blocks_ahead():
    na, nb = lax.axis_size("a"), lax.axis_size("b")
    at = [lax.axis_index(name) for name in SEQ]
    spots = []
    for mc in range(2):
        for mb in range(nb):
            for ma in range(na):
                a = jnp.mod(at[0] + ma, na)
                b = jnp.mod(at[1] + mb, nb)
                spots.append((a * nb + b) * 2 + jnp.mod(at[2] + mc, 2))
    return jnp.stack(spots)


def scatter_core(own, theirs):
    return (own.astype(F32) + swap(theirs, "c").astype(F32)).astype(BF)


def scatter_axis(total, name):
    size = lax.axis_size(name)
    total = total.reshape(size, total.shape[0] // size, *total.shape[1:])
    part = total[0].astype(F32)
    for m in range(1, size):
        part = part + to_ahead(total[m], name, m).astype(F32)
    return part.astype(BF)


def sum_over_head(block, n_head):
    if n_head == 2:
        return block + swap(block, "h")
    return lax.psum(block, "h")


def in_core_order(own, other, axis):
    first = lax.axis_index("c") == 0
    return jnp.concatenate([jnp.where(first, own, other), jnp.where(first, other, own)], axis=axis)


def every_head(block, n_head):
    if n_head == 2:
        other = swap(block, "h")
        mine = lax.axis_index("h") == 0
        return jnp.stack([jnp.where(mine, block, other), jnp.where(mine, other, block)])
    return lax.all_gather(block, "h", axis=0)


def factor_grads_body(core_ref, x_ref, gain_ref, *refs):
    joint_refs, own_ref, sent_ref = refs[:-2], refs[-2], refs[-1]
    total = None
    at = 0
    for ref in joint_refs:
        size = ref.shape[0]
        part = lax.dot_general(x_ref[at : at + size, :], ref[...], TN, preferred_element_type=F32)
        total = part if total is None else total + part
        at += size
    na, nb, rows, _ = own_ref.shape
    width = total.shape[1]
    first = core_ref[0] == 0
    gains = jnp.transpose(gain_ref[...])[:, :2]
    for i in range(na * nb):
        low = slice(2 * i * rows, (2 * i + 1) * rows)
        high = slice((2 * i + 1) * rows, (2 * i + 2) * rows)
        for block, lanes in ((total, slice(0, width)), (gains, slice(width, width + 2))):
            own = jnp.where(first, block[low], block[high])
            sent = jnp.where(first, block[high], block[low])
            own_ref[i // nb, i % nb, :, lanes] = own.astype(BF)
            sent_ref[i // nb, i % nb, :, lanes] = sent.astype(BF)


def factor_grads(rows_of, joints, gains):
    na, nb = lax.axis_size("a"), lax.axis_size("b")
    shape = (na, nb, D // (2 * na * nb), H * RA + RA * DH + 2)
    core = lax.axis_index("c").astype(jnp.int32).reshape(1)
    vmem = pl.BlockSpec(memory_space=pltpu.VMEM)
    return pl.pallas_call(
        factor_grads_body,
        in_specs=[pl.BlockSpec(memory_space=pltpu.SMEM)] + [vmem] * (2 + len(joints)),
        out_specs=[vmem, vmem],
        out_shape=[jax.ShapeDtypeStruct(shape, BF)] * 2,
        name="factor_grads",
    )(core, rows_of, gains, *joints)


def on_device(
    tokens,
    cotangent,
    domain_ids,
    block_order,
    headwise,
    headwise_mean,
    headwise_square,
    shared_factors,
    shared_factors_mean,
    shared_factors_square,
    out_weight,
    out_weight_mean,
    out_weight_square,
    gate_up,
    gate_up_mean,
    gate_up_square,
    down_weight,
    down_weight_mean,
    down_weight_square,
    norm_gains,
    norm_gains_mean,
    norm_gains_square,
):
    n_head = lax.axis_size("h")
    n_seq = lax.axis_size(SEQ)
    paired = n_head == 2
    seq_at = lax.axis_index(SEQ)
    head_at = lax.axis_index("h")
    seq_all, block_len, _ = tokens.shape
    count = seq_all // n_head
    rows = D // n_seq
    o_cols = H * DH // n_head
    h_cols = H * RA // n_head
    s_cols = RA * DH // n_head
    f_cols = FF // n_head

    shared_part = lax.dynamic_slice_in_dim(shared_factors, head_at * s_cols, s_cols, 1)
    small = jnp.concatenate([headwise, shared_part, norm_gains.T], axis=1).astype(BF)
    if n_head == 2:
        halves = ordered_gather(small, "h")
    else:
        halves = lax.all_gather(small, "h", axis=0)
    small = jnp.concatenate(
        [halves[k, :, :h_cols] for k in range(n_head)]
        + [halves[k, :, h_cols : h_cols + s_cols] for k in range(n_head)]
        + [halves[0, :, h_cols + s_cols :]],
        axis=1,
    )
    for name in ("a", "b", "c"):
        small = ordered_gather(small, name)
    small = small.transpose(2, 1, 0, 3, 4).reshape(D, H * RA + RA * DH + 2)
    w_factors = small[:, : H * RA + RA * DH]
    gains_low = small[:, H * RA + RA * DH :].T.astype(F32)
    gain_first = gains_low[0]
    gain_second = gains_low[1]

    wide_parts = (gate_up[0], gate_up[1], down_weight.T, out_weight.T)
    wide_part = jnp.concatenate([part.astype(BF) for part in wide_parts], axis=1)
    if paired:
        wide_all = lax.all_gather(turn_core_head(wide_part), ("a", "b", "h"), axis=0, tiled=True)
    else:
        wide_all = lax.all_gather(wide_part, SEQ + ("h",), axis=0)

    spots = jnp.arange(n_seq, dtype=jnp.int32)
    own_block = jnp.sum(jnp.where(spots == seq_at, block_order, 0))
    offsets = jnp.arange(block_len, dtype=jnp.int32)
    query_pos = own_block * block_len + offsets
    ahead = blocks_ahead()
    ahead_block = jnp.sum(jnp.where(spots[None, :] == ahead[:, None], block_order[None, :], 0), axis=1)
    key_pos = (ahead_block[:, None] * block_len + offsets[None, :]).reshape(1, n_seq * block_len)
    cos_t, sin_t = rope_tables(query_pos)

    tok = lax.dynamic_slice_in_dim(tokens, head_at * count, count, 0).astype(F32)
    cot = lax.dynamic_slice_in_dim(cotangent, head_at * count, count, 0).astype(F32)
    same_domain = (domain_ids[:, None] == domain_ids[None, :]).astype(F32)
    seq_weight = lax.dynamic_slice_in_dim(1.0 / jnp.sum(same_domain, axis=1), head_at * count, count, 0)
    out_grad = cot * seq_weight[:, None, None]
    out_low = out_grad.astype(BF)

    first_hat, first_inverse = normalize(tok)
    first_normalized = (first_hat * gain_first).astype(BF)
    factors = jnp.einsum("scd,dj->sjc", first_normalized, w_factors, preferred_element_type=F32)
    query, own_factors = prologue(factors, cos_t, sin_t)
    half = max(1, count // 2)
    groups = [slice(at, at + half) for at in range(0, count, half)]
    gathered = [gather_blocks(own_factors[g]) for g in groups]
    forward = []
    for at, g in enumerate(groups):
        wide, stats = attention_forward(query, g.start, gathered[at], key_pos, query_pos[:, None])
        if at == 0:
            wide, wide_all = lax.optimization_barrier((wide, wide_all))
        forward.append((wide, stats))
    if paired:
        w_gate = wide_all[:, :f_cols]
        w_up = wide_all[:, f_cols : 2 * f_cols]
        w_down_t = wide_all[:, 2 * f_cols : 3 * f_cols]
        own_out = wide_all[:, 3 * f_cols :]
        w_out_t = in_core_order(own_out, swap(own_out, "c"), 1)
    else:
        wide_all = wide_all.reshape(n_seq, n_head, rows, 3 * f_cols + o_cols)
        w_out_t = wide_all[..., 3 * f_cols :].transpose(0, 2, 1, 3).reshape(D, H * DH)
        wide_all = wide_all[..., : 3 * f_cols].reshape(n_seq, n_head, rows, 3, f_cols)
        wide_all = wide_all.transpose(3, 0, 2, 1, 4).reshape(3, D, FF)
        w_gate, w_up, w_down_t = wide_all[0], wide_all[1], wide_all[2]
    heads_wide = jnp.concatenate([part[0] for part in forward], axis=0)
    heads_low = heads_wide.astype(BF)
    attn = jnp.einsum("sce,de->scd", heads_low, w_out_t, preferred_element_type=F32)
    middle = tok + attn
    second_hat, second_inverse = normalize(middle)
    second_normalized = (second_hat * gain_second).astype(BF)

    tokens_own = count * block_len

    def both_cores(block):
        flat = block.reshape(tokens_own, D)
        if paired:
            return jnp.concatenate([flat, swap(flat, "c")], axis=0)
        return flat

    def own_sum(partial):
        if paired:
            partial = partial[:tokens_own] + swap(partial[tokens_own:].astype(BF), "c").astype(F32)
        return partial.reshape(count, block_len, D)

    x_low = both_cores(second_normalized)
    y_low = both_cores(out_low)
    gate = jnp.dot(x_low, w_gate, preferred_element_type=F32)
    up = jnp.dot(x_low, w_up, preferred_element_type=F32)
    sigmoid_gate = jax.nn.sigmoid(gate)
    silu_gate = gate * sigmoid_gate
    hidden_low = (silu_gate * up).astype(BF)
    ffn_part = jnp.einsum("tf,df->td", hidden_low, w_down_t, preferred_element_type=F32)
    y_low, ffn_part = lax.optimization_barrier((y_low, ffn_part))
    ffn = own_sum(ffn_part)
    layer_low = (middle + ffn).astype(BF)
    down_low = jnp.einsum("td,tf->df", y_low, hidden_low, preferred_element_type=F32).astype(BF)
    layer_parts = [layer_low[g] for g in groups]
    hidden_grad = jnp.dot(y_low, w_down_t, preferred_element_type=F32)
    up_grad = (hidden_grad * silu_gate).astype(BF)
    gate_grad = (
        hidden_grad * up * (sigmoid_gate * (1.0 + gate * (1.0 - sigmoid_gate)))
    ).astype(BF)
    gate_w_grad = jnp.einsum("td,tf->df", x_low, gate_grad, preferred_element_type=F32)
    up_w_grad = jnp.einsum("td,tf->df", x_low, up_grad, preferred_element_type=F32)
    second_part = jnp.einsum("tf,df->td", gate_grad, w_gate, preferred_element_type=F32)
    second_part = second_part + jnp.einsum("tf,df->td", up_grad, w_up, preferred_element_type=F32)
    second_grad = own_sum(second_part)

    second_gain_grad = jnp.sum(second_grad * second_hat, axis=(0, 1))
    middle_grad = out_grad + norm_back(second_grad, gain_second, second_hat, second_inverse)
    middle_low = middle_grad.astype(BF)
    heads_grad = jnp.einsum("scd,de->sce", middle_low, w_out_t, preferred_element_type=F32).astype(BF)

    def out_grad_of(columns):
        return jnp.einsum("scd,sce->de", middle_low, columns, preferred_element_type=F32)

    if paired:
        core_at = lax.axis_index("c")
        mine = lax.dynamic_slice_in_dim(heads_low, core_at * o_cols, o_cols, 2)
        theirs = lax.dynamic_slice_in_dim(heads_low, (1 - core_at) * o_cols, o_cols, 2)
        sent = swap(out_grad_of(theirs).astype(BF), "c")
        out_t_grad = out_grad_of(mine) + sent.astype(F32)
    else:
        out_t_grad = out_grad_of(heads_low)
    if paired:
        wide_grads = (gate_w_grad, up_w_grad, down_low)
        wide_grad = jnp.concatenate([grad.astype(BF) for grad in wide_grads], axis=1)
        wide_grad, heads_grad = lax.optimization_barrier((wide_grad, heads_grad))
        na, nb = lax.axis_size("a"), lax.axis_size("b")
        out_sum = out_t_grad.astype(BF).reshape(na, nb, 2, rows, o_cols)
        wide_sum = lax.psum_scatter(wide_grad, ("a", "b", "h"), scatter_dimension=0, tiled=True)
        wide_sum = turn_core_head(wide_sum).astype(F32)
        gate_sum = wide_sum[:, :f_cols]
        up_sum = wide_sum[:, f_cols : 2 * f_cols]
        down_sum = wide_sum[:, 2 * f_cols :]
    else:
        wide_grads = (gate_w_grad, up_w_grad, down_low, out_t_grad)
        wide_sum = jnp.concatenate([grad.astype(BF) for grad in wide_grads], axis=1)
        wide_sum = lax.psum_scatter(wide_sum, SEQ, scatter_dimension=0, tiled=True)
        wide_sum = lax.psum(wide_sum, "h").astype(F32)
        out_sum = lax.dynamic_slice_in_dim(wide_sum, 3 * FF + head_at * o_cols, o_cols, 1)
        wide_sum = wide_sum[:, : 3 * FF].reshape(rows, 3, n_head, f_cols)
        wide_sum = lax.dynamic_index_in_dim(wide_sum, head_at, 2, keepdims=False)
        gate_sum, up_sum, down_sum = wide_sum[:, 0], wide_sum[:, 1], wide_sum[:, 2]

    def backward_call(at, inner, size, backed):
        query_grad, *pieces = attention_backward(
            query,
            backed,
            forward[at][0],
            forward[at][1],
            gathered[at],
            key_pos,
            query_pos[:, None],
            n_seq // 2,
            groups[at].start + inner,
            inner,
            size,
        )
        return query_grad, scatter_core(*pieces)

    query_grads = []
    own_grads = []
    if len(groups) > 1:
        query_grad, total = backward_call(0, 0, half, heads_grad)
        heads_grad, total, out_sum, layer_parts[0] = lax.optimization_barrier(
            (heads_grad, total, out_sum, layer_parts[0])
        )
        if paired:
            out_sum = ordered_scatter(out_sum, "b", 1)
        query_grads.append([query_grad])
        total = scatter_axis(total, "b")
        own_grads.append(total)
    last = len(groups) - 1
    sizes = [half // 2, half - half // 2] if half > 1 else [half]
    inner = 0
    calls = []
    for i, size in enumerate(sizes):
        if i and last:
            heads_grad, own_grads[0], out_sum, layer_parts[1] = lax.optimization_barrier(
                (heads_grad, own_grads[0], out_sum, layer_parts[1])
            )
        calls.append(backward_call(last, inner, size, heads_grad))
        inner += size
    query_grads.append([call[0] for call in calls])
    layer_parts = [every_head(part, n_head) for part in layer_parts]
    own_grads.append(scatter_axis(jnp.concatenate([call[1] for call in calls], axis=1), "b"))
    own_grads = [scatter_axis(total, "a")[0] for total in own_grads]
    if paired:
        out_sum = ordered_scatter(ordered_scatter(out_sum, "a", 0), "h", 0)
        out_sum = turn_core_head(out_sum).astype(F32)
    first_gain_grad = 0.0
    joints = []
    input_parts = []
    for at, g in enumerate(groups):
        inner = 0
        parts = []
        for query_grad in query_grads[at]:
            parts.append(
                epilogue(query_grad, own_grads[at], factors, cos_t, sin_t, g.start + inner, inner)
            )
            inner += query_grad.shape[0]
        joint_grad = jnp.concatenate(parts, axis=0)
        joint_grad, layer_parts[at] = lax.optimization_barrier((joint_grad, layer_parts[at]))
        first_grad = jnp.einsum("scj,dj->scd", joint_grad, w_factors, preferred_element_type=F32)
        joints.append(joint_grad.reshape(-1, joint_grad.shape[2]))
        first_gain_grad = first_gain_grad + jnp.sum(first_grad * first_hat[g], axis=(0, 1))
        part = middle_grad[g] + norm_back(first_grad, gain_first, first_hat[g], first_inverse[g])
        part = part.astype(BF)
        if at + 1 < len(groups):
            part, own_grads[at + 1] = lax.optimization_barrier((part, own_grads[at + 1]))
        input_parts.append(part)

    layer_output = jnp.concatenate(layer_parts, axis=1).reshape(seq_all, block_len, D)
    gain_rows = jnp.stack([first_gain_grad, second_gain_grad] + [jnp.zeros(D, F32)] * 6)
    input_parts = [every_head(part, n_head) for part in input_parts]
    small_own, small_sent = factor_grads(first_normalized.reshape(-1, D), joints, gain_rows)
    small_sum = scatter_core(small_own, small_sent)
    small_sum = ordered_scatter(small_sum, "b", 1)
    if len(groups) > 1:
        small_sum, input_parts[0] = lax.optimization_barrier((small_sum, input_parts[0]))
    small_sum = ordered_scatter(small_sum, "a", 0)
    small_sum, input_parts[-1] = lax.optimization_barrier((small_sum, input_parts[-1]))
    small_sum = sum_over_head(small_sum, n_head).astype(F32)
    input_grad = jnp.concatenate(input_parts, axis=1).reshape(seq_all, block_len, D).astype(F32)
    heads_sum = lax.dynamic_slice_in_dim(small_sum, head_at * h_cols, h_cols, 1)
    shared_sum = small_sum[:, H * RA : H * RA + RA * DH]
    gains_sum = small_sum[:, H * RA + RA * DH :].T
    out_sum = out_sum.T
    gate_up_sum = jnp.stack([gate_sum, up_sum])
    down_sum = down_sum.T

    rates = step_rates()
    heads_new = adam_update(headwise, headwise_mean, headwise_square, heads_sum, rates[0])
    shared_new = adam_update(
        shared_factors, shared_factors_mean, shared_factors_square, shared_sum, rates[1]
    )
    out_new = adam_update(out_weight, out_weight_mean, out_weight_square, out_sum, rates[2])
    gate_new = adam_update(gate_up, gate_up_mean, gate_up_square, gate_up_sum, rates[3])
    down_new = adam_update(down_weight, down_weight_mean, down_weight_square, down_sum, rates[4])
    gains_new = adam_update(norm_gains, norm_gains_mean, norm_gains_square, gains_sum, rates[5])
    return (
        layer_output,
        input_grad,
        *heads_new,
        *shared_new,
        *out_new,
        *gate_new,
        *down_new,
        *gains_new,
    )


def solution(mesh):
    n_seq = mesh.shape["seq"]
    n_head = mesh.shape["head"]
    inner = max(1, n_seq // 8)
    fine = Mesh(mesh.devices.reshape(n_seq // 2 // inner, inner, 2, n_head), ("a", "b", "c", "h"))
    token = P(None, SEQ, None)
    heads = P(SEQ, "h")
    shared = P(SEQ, None)
    turned = P("h", SEQ)
    gates = P(None, SEQ, "h")
    gains = P(None, SEQ)
    weights = sum(([spec] * 3 for spec in (heads, shared, turned, gates, turned, gains)), [])
    return jax.shard_map(
        on_device,
        mesh=fine,
        in_specs=(token, token, P(), P(), *weights),
        out_specs=(token, token, *weights),
        check_vma=False,
    )
```

```python
import functools

import jax
import jax.numpy as jnp
from jax import lax
from jax.experimental import pallas as pl
from jax.experimental.pallas import tpu as pltpu
from jax.sharding import Mesh
from jax.sharding import PartitionSpec as P

D = 1024
H = 16
DH = 64
RQ = 6
RK = 2
RA = RQ + 2 * RK
FF = 2816
STEP = 10
HB = 4

EPSILON = 1e-05
BETA_ONE = 0.9
BETA_TWO = 0.95
ADAM_EPS = 1e-08
DECAY = 0.1
NEGATIVE = -1e30
SCALE = DH ** (-0.5)
BF = jnp.bfloat16
F32 = jnp.float32
SEQ = ("a", "b", "c")


def rope_tables(positions):
    half_dim = DH // 2
    frequency = 10000.0 ** (-(2.0 * jnp.arange(half_dim, dtype=F32)) / DH)
    angles = frequency[:, None] * positions.astype(F32)[None, :]
    return (jnp.cos(angles), jnp.sin(angles))


def normalize(row_data):
    inverse = lax.rsqrt(jnp.mean(row_data * row_data, -1, keepdims=True) + EPSILON)
    return (row_data * inverse, inverse)


def norm_back(normed_grad, gain_row, hat_rows, inverse):
    hat_grad = normed_grad * gain_row
    return inverse * (hat_grad - hat_rows * jnp.mean(hat_grad * hat_rows, -1, keepdims=True))


def adam_update(master, mean_old, square_old, gradient, rate):
    mean_new = BETA_ONE * mean_old + (1.0 - BETA_ONE) * gradient
    square_new = BETA_TWO * square_old + (1.0 - BETA_TWO) * gradient * gradient
    mean_hat = mean_new / (1.0 - BETA_ONE**STEP)
    square_hat = square_new / (1.0 - BETA_TWO**STEP)
    master_new = master - rate * (mean_hat / (jnp.sqrt(square_hat) + ADAM_EPS) + DECAY * master)
    return (master_new, mean_new, square_new)


def step_rates():
    return (
        2.5 * (D // 4) ** (-0.5),
        2.5 * D ** (-0.5),
        2.5 * (H * DH // 32) ** (-0.5),
        2.5 * D ** (-0.5),
        2.5 * FF ** (-0.5),
        0.5,
    )


def rotated(pair, cos_t, sin_t):
    u = pair[: DH // 2]
    w = pair[DH // 2 :]
    return jnp.concatenate([u * cos_t - w * sin_t, w * cos_t + u * sin_t], axis=0)


def unrotated(pair, cos_t, sin_t):
    u = pair[: DH // 2]
    w = pair[DH // 2 :]
    return jnp.concatenate([u * cos_t + w * sin_t, w * cos_t - u * sin_t], axis=0)


def prologue_body(f_ref, cos_ref, sin_ref, q_ref, fac_ref):
    cos_t = cos_ref[...]
    sin_t = sin_ref[...]
    base = H * RA
    bq = [
        rotated(f_ref[0, base + r * DH : base + (r + 1) * DH, :], cos_t, sin_t) for r in range(RQ)
    ]
    for pair in range(H // 2):
        parts = []
        for h in (2 * pair, 2 * pair + 1):
            acc = f_ref[0, h * RA : h * RA + 1, :] * bq[0]
            for r in range(1, RQ):
                acc = acc + f_ref[0, h * RA + r : h * RA + r + 1, :] * bq[r]
            parts.append(acc)
        both = jnp.concatenate(parts, axis=0) / RQ
        rows = jnp.transpose(both).astype(BF) * SCALE
        q_ref[0, :, pair * 2 * DH : (pair + 1) * 2 * DH] = rows.astype(BF)
    for r in range(RK):
        at = base + (RQ + r) * DH
        fac_ref[0, r * 2 * DH : r * 2 * DH + DH, :] = rotated(
            f_ref[0, at : at + DH, :], cos_t, sin_t
        ).astype(BF)
        at = base + (RQ + RK + r) * DH
        fac_ref[0, r * 2 * DH + DH : (r + 1) * 2 * DH, :] = f_ref[0, at : at + DH, :].astype(BF)
    rows = [f_ref[0, h * RA + RQ : (h + 1) * RA, :] for h in range(H)]
    fac_ref[0, RK * 2 * DH :, :] = (jnp.concatenate(rows, axis=0) * (1.0 / RK)).astype(BF)


FAC = RK * 2 * DH + 2 * RK * H


def prologue(factors, cos_t, sin_t):
    count, width, block = factors.shape
    return pl.pallas_call(
        prologue_body,
        grid=(count,),
        in_specs=[
            pl.BlockSpec((1, width, block), lambda s: (s, 0, 0)),
            pl.BlockSpec((DH // 2, block), lambda s: (0, 0)),
            pl.BlockSpec((DH // 2, block), lambda s: (0, 0)),
        ],
        out_specs=[
            pl.BlockSpec((1, block, H * DH), lambda s: (s, 0, 0)),
            pl.BlockSpec((1, FAC, block), lambda s: (s, 0, 0)),
        ],
        out_shape=[
            jax.ShapeDtypeStruct((count, block, H * DH), BF),
            jax.ShapeDtypeStruct((count, FAC, block), BF),
        ],
        name="factor_prologue",
    )(factors, cos_t, sin_t)


def epilogue_body(dq_ref, df_ref, f_ref, cos_ref, sin_ref, g_ref):
    cos_t = cos_ref[...]
    sin_t = sin_ref[...]
    base = H * RA
    bq = [
        rotated(f_ref[0, base + r * DH : base + (r + 1) * DH, :], cos_t, sin_t) for r in range(RQ)
    ]
    sums = [None] * RQ
    rows = []
    wide = RK * 2 * DH
    for pair in range(H // 2):
        both = jnp.transpose(dq_ref[0, :, pair * 2 * DH : (pair + 1) * 2 * DH])
        for k in range(2):
            h = 2 * pair + k
            dq = both[k * DH : (k + 1) * DH] * (1.0 / RQ)
            for r in range(RQ):
                rows.append(jnp.sum(dq * bq[r], axis=0, keepdims=True))
                term = f_ref[0, h * RA + r : h * RA + r + 1, :] * dq
                sums[r] = term if sums[r] is None else sums[r] + term
            rows.append(df_ref[0, wide + h * 2 * RK : wide + (h + 1) * 2 * RK, :].astype(F32))
    for r in range(RQ):
        rows.append(unrotated(sums[r], cos_t, sin_t))
    for r in range(RK):
        part = df_ref[0, r * 2 * DH : r * 2 * DH + DH, :].astype(F32)
        rows.append(unrotated(part, cos_t, sin_t))
    for r in range(RK):
        rows.append(df_ref[0, r * 2 * DH + DH : (r + 1) * 2 * DH, :].astype(F32))
    g_ref[0] = jnp.transpose(jnp.concatenate(rows, axis=0)).astype(BF)


def epilogue(query_grad, factor_grad, factors, cos_t, sin_t, first, inner):
    count = query_grad.shape[0]
    _, width, block = factors.shape
    return pl.pallas_call(
        epilogue_body,
        grid=(count,),
        in_specs=[
            pl.BlockSpec((1, block, H * DH), lambda s: (s, 0, 0)),
            pl.BlockSpec((1, FAC, block), lambda s: (s + inner, 0, 0)),
            pl.BlockSpec((1, width, block), lambda s: (s + first, 0, 0)),
            pl.BlockSpec((DH // 2, block), lambda s: (0, 0)),
            pl.BlockSpec((DH // 2, block), lambda s: (0, 0)),
        ],
        out_specs=pl.BlockSpec((1, block, width), lambda s: (s, 0, 0)),
        out_shape=jax.ShapeDtypeStruct((count, block, width), BF),
        name="factor_epilogue",
    )(query_grad, factor_grad, factors, cos_t, sin_t)


def keys_values(a_rows, b_rows, h):
    a = a_rows[4 * h : 4 * h + 4]
    key_t = a[0:1] * b_rows[:DH] + a[1:2] * b_rows[2 * DH : 3 * DH]
    value_t = a[2:3] * b_rows[DH : 2 * DH] + a[3:4] * b_rows[3 * DH :]
    return key_t.astype(BF), value_t.astype(BF)


NT = (((1,), (1,)), ((), ()))
TN = (((0,), (0,)), ((), ()))


def forward_body(q_ref, b_ref, a_ref, kpos_ref, qpos_ref, o_ref, lse_ref):
    allowed = kpos_ref[...] <= qpos_ref[...]
    b_rows = b_ref[0].astype(F32)
    a_rows = a_ref[0].astype(F32)
    outs = []
    stats = []
    for h in range(HB):
        key_t, value_t = keys_values(a_rows, b_rows, h)
        scores = jnp.dot(q_ref[0, :, h * DH : (h + 1) * DH], key_t, preferred_element_type=F32)
        scores = jnp.where(allowed, scores, NEGATIVE)
        best = jnp.max(scores, axis=1, keepdims=True)
        probs = jnp.exp(scores - best)
        total = jnp.sum(probs, axis=1, keepdims=True)
        part = lax.dot_general(probs.astype(BF), value_t, NT, preferred_element_type=F32)
        outs.append(part / total)
        stats.append(best + jnp.log(total))
    o_ref[0] = jnp.concatenate(outs, axis=1)
    lse_ref[0, 0] = jnp.concatenate(stats, axis=1)


def attention_forward(query, first, gathered, key_pos, query_pos):
    _, block, width = query.shape
    count, _, length = gathered.shape
    wide = RK * 2 * DH
    return pl.pallas_call(
        forward_body,
        grid=(count, H // HB),
        in_specs=[
            pl.BlockSpec((1, block, HB * DH), lambda s, g: (s + first, 0, g)),
            pl.BlockSpec((1, wide, length), lambda s, g: (s, 0, 0)),
            pl.BlockSpec((1, 4 * HB, length), lambda s, g: (s, wide // (4 * HB) + g, 0)),
            pl.BlockSpec((1, length), lambda s, g: (0, 0)),
            pl.BlockSpec((block, 1), lambda s, g: (0, 0)),
        ],
        out_specs=[
            pl.BlockSpec((1, block, HB * DH), lambda s, g: (s, 0, g)),
            pl.BlockSpec((1, 1, block, HB), lambda s, g: (s, g, 0, 0)),
        ],
        out_shape=[
            jax.ShapeDtypeStruct((count, block, width), F32),
            jax.ShapeDtypeStruct((count, H // HB, block, HB), F32),
        ],
        cost_estimate=pl.CostEstimate(
            flops=4 * count * H * block * length * DH,
            bytes_accessed=2 * count * length * FAC,
            transcendentals=count * H * block * length,
        ),
        name="attention_forward",
    )(query, gathered, gathered, key_pos, query_pos)


def backward_body(
    q_ref, do_ref, o_ref, lse_ref, b_ref, a_ref, kpos_ref, qpos_ref, dq_ref, *refs
):
    piece_refs, acc_ref = refs[:-1], refs[-1]
    group = pl.program_id(1)
    wide = RK * 2 * DH

    @pl.when(group == 0)
    def _():
        acc_ref[...] = jnp.zeros_like(acc_ref)

    allowed = kpos_ref[...] <= qpos_ref[...]
    b_rows = b_ref[0].astype(F32)
    a_rows = a_ref[0].astype(F32)
    lse = lse_ref[0, 0]
    dqs = []
    rows = []
    for h in range(HB):
        key_t, value_t = keys_values(a_rows, b_rows, h)
        q = q_ref[0, :, h * DH : (h + 1) * DH]
        do = do_ref[0, :, h * DH : (h + 1) * DH]
        delta = jnp.sum(do.astype(F32) * o_ref[0, :, h * DH : (h + 1) * DH], axis=1, keepdims=True)
        scores = jnp.dot(q, key_t, preferred_element_type=F32)
        probs = jnp.exp(jnp.where(allowed, scores - lse[:, h : h + 1], NEGATIVE))
        prob_grad = jnp.dot(do, value_t, preferred_element_type=F32)
        score_grad = (probs * (prob_grad - delta)).astype(BF)
        dqs.append(lax.dot_general(score_grad, key_t, NT, preferred_element_type=F32) * SCALE)
        dk = lax.dot_general(q, score_grad, TN, preferred_element_type=F32)
        dv = lax.dot_general(do, probs.astype(BF), TN, preferred_element_type=F32)
        a = a_rows[4 * h : 4 * h + 4]
        acc_ref[:DH] += a[0:1] * dk
        acc_ref[DH : 2 * DH] += a[2:3] * dv
        acc_ref[2 * DH : 3 * DH] += a[1:2] * dk
        acc_ref[3 * DH :] += a[3:4] * dv
        rows.append(jnp.sum(dk * b_rows[:DH], axis=0, keepdims=True))
        rows.append(jnp.sum(dk * b_rows[2 * DH : 3 * DH], axis=0, keepdims=True))
        rows.append(jnp.sum(dv * b_rows[DH : 2 * DH], axis=0, keepdims=True))
        rows.append(jnp.sum(dv * b_rows[3 * DH :], axis=0, keepdims=True))
    dq_ref[0] = jnp.concatenate(dqs, axis=1)
    a_grad = (jnp.concatenate(rows, axis=0) * (1.0 / RK)).astype(BF)
    block = piece_refs[0].shape[3]
    depth = piece_refs[0].shape[0]
    at = pl.multiple_of(wide + group * 4 * HB, 4 * HB)
    for i, ref in enumerate(piece_refs):
        for m in range(depth):
            lanes = (i * depth + m) * block
            ref[m, 0, pl.ds(at, 4 * HB), :] = a_grad[:, lanes : lanes + block]

    @pl.when(group == pl.num_programs(1) - 1)
    def _():
        for i, ref in enumerate(piece_refs):
            for m in range(depth):
                lanes = (i * depth + m) * block
                ref[m, 0, :wide, :] = acc_ref[:, lanes : lanes + block].astype(BF)


def attention_backward(
    query, heads_grad, heads_wide, lse, gathered, key_pos, query_pos, depth, first, inner, count
):
    _, block, width = query.shape
    length = gathered.shape[2]
    wide = RK * 2 * DH
    pieces = length // (depth * block)
    return pl.pallas_call(
        backward_body,
        grid=(count, H // HB),
        in_specs=[
            pl.BlockSpec((1, block, HB * DH), lambda s, g: (s + first, 0, g)),
            pl.BlockSpec((1, block, HB * DH), lambda s, g: (s + first, 0, g)),
            pl.BlockSpec((1, block, HB * DH), lambda s, g: (s + inner, 0, g)),
            pl.BlockSpec((1, 1, block, HB), lambda s, g: (s + inner, g, 0, 0)),
            pl.BlockSpec((1, wide, length), lambda s, g: (s + inner, 0, 0)),
            pl.BlockSpec((1, 4 * HB, length), lambda s, g: (s + inner, wide // (4 * HB) + g, 0)),
            pl.BlockSpec((1, length), lambda s, g: (0, 0)),
            pl.BlockSpec((block, 1), lambda s, g: (0, 0)),
        ],
        out_specs=[pl.BlockSpec((1, block, HB * DH), lambda s, g: (s, 0, g))]
        + [pl.BlockSpec((depth, 1, FAC, block), lambda s, g: (0, s, 0, 0))] * pieces,
        out_shape=[jax.ShapeDtypeStruct((count, block, width), F32)]
        + [jax.ShapeDtypeStruct((depth, count, FAC, block), BF)] * pieces,
        scratch_shapes=[pltpu.VMEM((wide, length), F32)],
        cost_estimate=pl.CostEstimate(
            flops=10 * count * H * block * length * DH,
            bytes_accessed=4 * count * length * FAC,
            transcendentals=count * H * block * length,
        ),
        name="attention_backward",
    )(query, heads_grad, heads_wide, lse, gathered, gathered, key_pos, query_pos)


def swap(block, axis):
    return lax.ppermute(block, axis, [(0, 1), (1, 0)])


def turn_core_head(block):
    return lax.ppermute(block, ("c", "h"), [(0, 0), (1, 2), (2, 1), (3, 3)])


def from_ahead(block, axis, distance):
    size = lax.axis_size(axis)
    return lax.ppermute(block, axis, [((i + distance) % size, i) for i in range(size)])


def to_ahead(block, axis, distance):
    size = lax.axis_size(axis)
    return lax.ppermute(block, axis, [(i, (i + distance) % size) for i in range(size)])


def ordered_gather(block, axis):
    size = lax.axis_size(axis)
    spot = lax.axis_index(axis)
    if size == 2:
        other = swap(block, axis)
        mine = spot == 0
        return jnp.stack([jnp.where(mine, block, other), jnp.where(mine, other, block)])
    parts = [block] + [from_ahead(block, axis, m) for m in range(1, size)]
    twice = jnp.stack(parts + parts[:-1])
    return lax.dynamic_slice_in_dim(twice, jnp.mod(size - spot, size), size, 0)


def ordered_scatter(block, axis, dim):
    size = lax.axis_size(axis)
    spot = lax.axis_index(axis)

    def part(m):
        return lax.dynamic_index_in_dim(block, jnp.mod(spot + m, size), dim, keepdims=False)

    total = part(0).astype(F32)
    for m in range(1, size):
        total = total + to_ahead(part(m), axis, m).astype(F32)
    return total.astype(BF)


def gather_blocks(block):
    for name in ("a", "b"):
        ahead = [from_ahead(block, name, m) for m in range(1, lax.axis_size(name))]
        block = jnp.concatenate([block] + ahead, axis=2)
    return jnp.concatenate([block, swap(block, "c")], axis=2)


def blocks_ahead():
    na, nb = lax.axis_size("a"), lax.axis_size("b")
    at = [lax.axis_index(name) for name in SEQ]
    spots = []
    for mc in range(2):
        for mb in range(nb):
            for ma in range(na):
                a = jnp.mod(at[0] + ma, na)
                b = jnp.mod(at[1] + mb, nb)
                spots.append((a * nb + b) * 2 + jnp.mod(at[2] + mc, 2))
    return jnp.stack(spots)


def scatter_core(own, theirs):
    return (own.astype(F32) + swap(theirs, "c").astype(F32)).astype(BF)


def scatter_axis(total, name):
    size = lax.axis_size(name)
    total = total.reshape(size, total.shape[0] // size, *total.shape[1:])
    part = total[0].astype(F32)
    for m in range(1, size):
        part = part + to_ahead(total[m], name, m).astype(F32)
    return part.astype(BF)


def sum_over_head(block, n_head):
    if n_head == 2:
        return block + swap(block, "h")
    return lax.psum(block, "h")


def in_core_order(own, other, axis):
    first = lax.axis_index("c") == 0
    return jnp.concatenate([jnp.where(first, own, other), jnp.where(first, other, own)], axis=axis)


def every_head(block, n_head):
    if n_head == 2:
        other = swap(block, "h")
        mine = lax.axis_index("h") == 0
        return jnp.stack([jnp.where(mine, block, other), jnp.where(mine, other, block)])
    return lax.all_gather(block, "h", axis=0)


def factor_grads_body(core_ref, x_ref, gain_ref, *refs):
    joint_refs, own_ref, sent_ref = refs[:-2], refs[-2], refs[-1]
    total = None
    at = 0
    for ref in joint_refs:
        size = ref.shape[0]
        part = lax.dot_general(x_ref[at : at + size, :], ref[...], TN, preferred_element_type=F32)
        total = part if total is None else total + part
        at += size
    na, nb, rows, _ = own_ref.shape
    width = total.shape[1]
    first = core_ref[0] == 0
    gains = jnp.transpose(gain_ref[...])[:, :2]
    for i in range(na * nb):
        low = slice(2 * i * rows, (2 * i + 1) * rows)
        high = slice((2 * i + 1) * rows, (2 * i + 2) * rows)
        for block, lanes in ((total, slice(0, width)), (gains, slice(width, width + 2))):
            own = jnp.where(first, block[low], block[high])
            sent = jnp.where(first, block[high], block[low])
            own_ref[i // nb, i % nb, :, lanes] = own.astype(BF)
            sent_ref[i // nb, i % nb, :, lanes] = sent.astype(BF)


def factor_grads(rows_of, joints, gains):
    na, nb = lax.axis_size("a"), lax.axis_size("b")
    shape = (na, nb, D // (2 * na * nb), H * RA + RA * DH + 2)
    core = lax.axis_index("c").astype(jnp.int32).reshape(1)
    vmem = pl.BlockSpec(memory_space=pltpu.VMEM)
    return pl.pallas_call(
        factor_grads_body,
        in_specs=[pl.BlockSpec(memory_space=pltpu.SMEM)] + [vmem] * (2 + len(joints)),
        out_specs=[vmem, vmem],
        out_shape=[jax.ShapeDtypeStruct(shape, BF)] * 2,
        name="factor_grads",
    )(core, rows_of, gains, *joints)


def on_device(
    tokens,
    cotangent,
    domain_ids,
    block_order,
    headwise,
    headwise_mean,
    headwise_square,
    shared_factors,
    shared_factors_mean,
    shared_factors_square,
    out_weight,
    out_weight_mean,
    out_weight_square,
    gate_up,
    gate_up_mean,
    gate_up_square,
    down_weight,
    down_weight_mean,
    down_weight_square,
    norm_gains,
    norm_gains_mean,
    norm_gains_square,
):
    n_head = lax.axis_size("h")
    n_seq = lax.axis_size(SEQ)
    paired = n_head == 2
    seq_at = lax.axis_index(SEQ)
    head_at = lax.axis_index("h")
    seq_all, block_len, _ = tokens.shape
    count = seq_all // n_head
    rows = D // n_seq
    o_cols = H * DH // n_head
    h_cols = H * RA // n_head
    s_cols = RA * DH // n_head
    f_cols = FF // n_head

    shared_part = lax.dynamic_slice_in_dim(shared_factors, head_at * s_cols, s_cols, 1)
    small = jnp.concatenate([headwise, shared_part, norm_gains.T], axis=1).astype(BF)
    if n_head == 2:
        halves = ordered_gather(small, "h")
    else:
        halves = lax.all_gather(small, "h", axis=0)
    small = jnp.concatenate(
        [halves[k, :, :h_cols] for k in range(n_head)]
        + [halves[k, :, h_cols : h_cols + s_cols] for k in range(n_head)]
        + [halves[0, :, h_cols + s_cols :]],
        axis=1,
    )
    for name in ("a", "b", "c"):
        small = ordered_gather(small, name)
    small = small.transpose(2, 1, 0, 3, 4).reshape(D, H * RA + RA * DH + 2)
    w_factors = small[:, : H * RA + RA * DH]
    gains_low = small[:, H * RA + RA * DH :].T.astype(F32)
    gain_first = gains_low[0]
    gain_second = gains_low[1]

    wide_parts = (gate_up[0], gate_up[1], down_weight.T, out_weight.T)
    wide_part = jnp.concatenate([part.astype(BF) for part in wide_parts], axis=1)
    if paired:
        wide_all = lax.all_gather(turn_core_head(wide_part), ("a", "b", "h"), axis=0, tiled=True)
    else:
        wide_all = lax.all_gather(wide_part, SEQ + ("h",), axis=0)

    spots = jnp.arange(n_seq, dtype=jnp.int32)
    own_block = jnp.sum(jnp.where(spots == seq_at, block_order, 0))
    offsets = jnp.arange(block_len, dtype=jnp.int32)
    query_pos = own_block * block_len + offsets
    ahead = blocks_ahead()
    ahead_block = jnp.sum(jnp.where(spots[None, :] == ahead[:, None], block_order[None, :], 0), axis=1)
    key_pos = (ahead_block[:, None] * block_len + offsets[None, :]).reshape(1, n_seq * block_len)
    cos_t, sin_t = rope_tables(query_pos)

    tok = lax.dynamic_slice_in_dim(tokens, head_at * count, count, 0).astype(F32)
    cot = lax.dynamic_slice_in_dim(cotangent, head_at * count, count, 0).astype(F32)
    same_domain = (domain_ids[:, None] == domain_ids[None, :]).astype(F32)
    seq_weight = lax.dynamic_slice_in_dim(1.0 / jnp.sum(same_domain, axis=1), head_at * count, count, 0)
    out_grad = cot * seq_weight[:, None, None]
    out_low = out_grad.astype(BF)

    first_hat, first_inverse = normalize(tok)
    first_normalized = (first_hat * gain_first).astype(BF)
    factors = jnp.einsum("scd,dj->sjc", first_normalized, w_factors, preferred_element_type=F32)
    query, own_factors = prologue(factors, cos_t, sin_t)
    half = max(1, count // 2)
    groups = [slice(at, at + half) for at in range(0, count, half)]
    gathered = [gather_blocks(own_factors[g]) for g in groups]
    forward = []
    for at, g in enumerate(groups):
        wide, stats = attention_forward(query, g.start, gathered[at], key_pos, query_pos[:, None])
        if at == 0:
            wide, wide_all = lax.optimization_barrier((wide, wide_all))
        forward.append((wide, stats))
    if paired:
        w_gate = wide_all[:, :f_cols]
        w_up = wide_all[:, f_cols : 2 * f_cols]
        w_down_t = wide_all[:, 2 * f_cols : 3 * f_cols]
        own_out = wide_all[:, 3 * f_cols :]
        w_out_t = in_core_order(own_out, swap(own_out, "c"), 1)
    else:
        wide_all = wide_all.reshape(n_seq, n_head, rows, 3 * f_cols + o_cols)
        w_out_t = wide_all[..., 3 * f_cols :].transpose(0, 2, 1, 3).reshape(D, H * DH)
        wide_all = wide_all[..., : 3 * f_cols].reshape(n_seq, n_head, rows, 3, f_cols)
        wide_all = wide_all.transpose(3, 0, 2, 1, 4).reshape(3, D, FF)
        w_gate, w_up, w_down_t = wide_all[0], wide_all[1], wide_all[2]
    heads_wide = jnp.concatenate([part[0] for part in forward], axis=0)
    heads_low = heads_wide.astype(BF)
    attn = jnp.einsum("sce,de->scd", heads_low, w_out_t, preferred_element_type=F32)
    middle = tok + attn
    second_hat, second_inverse = normalize(middle)
    second_normalized = (second_hat * gain_second).astype(BF)

    tokens_own = count * block_len

    def both_cores(block):
        flat = block.reshape(tokens_own, D)
        if paired:
            return jnp.concatenate([flat, swap(flat, "c")], axis=0)
        return flat

    def own_sum(partial):
        if paired:
            partial = partial[:tokens_own] + swap(partial[tokens_own:].astype(BF), "c").astype(F32)
        return partial.reshape(count, block_len, D)

    x_low = both_cores(second_normalized)
    y_low = both_cores(out_low)
    gate = jnp.dot(x_low, w_gate, preferred_element_type=F32)
    up = jnp.dot(x_low, w_up, preferred_element_type=F32)
    sigmoid_gate = jax.nn.sigmoid(gate)
    silu_gate = gate * sigmoid_gate
    hidden_low = (silu_gate * up).astype(BF)
    ffn_part = jnp.einsum("tf,df->td", hidden_low, w_down_t, preferred_element_type=F32)
    y_low, ffn_part = lax.optimization_barrier((y_low, ffn_part))
    ffn = own_sum(ffn_part)
    layer_low = (middle + ffn).astype(BF)
    down_low = jnp.einsum("td,tf->df", y_low, hidden_low, preferred_element_type=F32).astype(BF)
    layer_parts = [layer_low[g] for g in groups]
    hidden_grad = jnp.dot(y_low, w_down_t, preferred_element_type=F32)
    up_grad = (hidden_grad * silu_gate).astype(BF)
    gate_grad = (
        hidden_grad * up * (sigmoid_gate * (1.0 + gate * (1.0 - sigmoid_gate)))
    ).astype(BF)
    gate_w_grad = jnp.einsum("td,tf->df", x_low, gate_grad, preferred_element_type=F32)
    up_w_grad = jnp.einsum("td,tf->df", x_low, up_grad, preferred_element_type=F32)
    second_part = jnp.einsum("tf,df->td", gate_grad, w_gate, preferred_element_type=F32)
    second_part = second_part + jnp.einsum("tf,df->td", up_grad, w_up, preferred_element_type=F32)
    second_grad = own_sum(second_part)

    second_gain_grad = jnp.sum(second_grad * second_hat, axis=(0, 1))
    middle_grad = out_grad + norm_back(second_grad, gain_second, second_hat, second_inverse)
    middle_low = middle_grad.astype(BF)
    heads_grad = jnp.einsum("scd,de->sce", middle_low, w_out_t, preferred_element_type=F32).astype(BF)

    def out_grad_of(columns):
        return jnp.einsum("scd,sce->de", middle_low, columns, preferred_element_type=F32)

    if paired:
        core_at = lax.axis_index("c")
        mine = lax.dynamic_slice_in_dim(heads_low, core_at * o_cols, o_cols, 2)
        theirs = lax.dynamic_slice_in_dim(heads_low, (1 - core_at) * o_cols, o_cols, 2)
        sent = swap(out_grad_of(theirs).astype(BF), "c")
        out_t_grad = out_grad_of(mine) + sent.astype(F32)
    else:
        out_t_grad = out_grad_of(heads_low)
    if paired:
        wide_grads = (gate_w_grad, up_w_grad, down_low, out_t_grad)
        wide_grad = jnp.concatenate([grad.astype(BF) for grad in wide_grads], axis=1)
        wide_grad, heads_grad = lax.optimization_barrier((wide_grad, heads_grad))
        wide_sum = lax.psum_scatter(wide_grad, ("a", "b", "h"), scatter_dimension=0, tiled=True)
        wide_sum = turn_core_head(wide_sum).astype(F32)
        gate_sum = wide_sum[:, :f_cols]
        up_sum = wide_sum[:, f_cols : 2 * f_cols]
        down_sum = wide_sum[:, 2 * f_cols : 3 * f_cols]
        out_sum = wide_sum[:, 3 * f_cols :]
    else:
        wide_grads = (gate_w_grad, up_w_grad, down_low, out_t_grad)
        wide_sum = jnp.concatenate([grad.astype(BF) for grad in wide_grads], axis=1)
        wide_sum = lax.psum_scatter(wide_sum, SEQ, scatter_dimension=0, tiled=True)
        wide_sum = lax.psum(wide_sum, "h").astype(F32)
        out_sum = lax.dynamic_slice_in_dim(wide_sum, 3 * FF + head_at * o_cols, o_cols, 1)
        wide_sum = wide_sum[:, : 3 * FF].reshape(rows, 3, n_head, f_cols)
        wide_sum = lax.dynamic_index_in_dim(wide_sum, head_at, 2, keepdims=False)
        gate_sum, up_sum, down_sum = wide_sum[:, 0], wide_sum[:, 1], wide_sum[:, 2]

    def backward_call(at, inner, size, backed):
        query_grad, *pieces = attention_backward(
            query,
            backed,
            forward[at][0],
            forward[at][1],
            gathered[at],
            key_pos,
            query_pos[:, None],
            n_seq // 2,
            groups[at].start + inner,
            inner,
            size,
        )
        return query_grad, scatter_core(*pieces)

    query_grads = []
    own_grads = []
    if len(groups) > 1:
        query_grad, total = backward_call(0, 0, half, heads_grad)
        heads_grad, total, layer_parts[0] = lax.optimization_barrier(
            (heads_grad, total, layer_parts[0])
        )
        query_grads.append([query_grad])
        total = scatter_axis(total, "b")
        own_grads.append(total)
    last = len(groups) - 1
    sizes = [half // 2, half - half // 2] if half > 1 else [half]
    inner = 0
    calls = []
    for i, size in enumerate(sizes):
        if i and last:
            heads_grad, own_grads[0], layer_parts[1] = lax.optimization_barrier(
                (heads_grad, own_grads[0], layer_parts[1])
            )
        calls.append(backward_call(last, inner, size, heads_grad))
        inner += size
    query_grads.append([call[0] for call in calls])
    layer_parts = [every_head(part, n_head) for part in layer_parts]
    own_grads.append(scatter_axis(jnp.concatenate([call[1] for call in calls], axis=1), "b"))
    own_grads = [scatter_axis(total, "a")[0] for total in own_grads]
    first_gain_grad = 0.0
    joints = []
    input_parts = []
    for at, g in enumerate(groups):
        inner = 0
        parts = []
        for query_grad in query_grads[at]:
            parts.append(
                epilogue(query_grad, own_grads[at], factors, cos_t, sin_t, g.start + inner, inner)
            )
            inner += query_grad.shape[0]
        joint_grad = jnp.concatenate(parts, axis=0)
        joint_grad, layer_parts[at] = lax.optimization_barrier((joint_grad, layer_parts[at]))
        first_grad = jnp.einsum("scj,dj->scd", joint_grad, w_factors, preferred_element_type=F32)
        joints.append(joint_grad.reshape(-1, joint_grad.shape[2]))
        first_gain_grad = first_gain_grad + jnp.sum(first_grad * first_hat[g], axis=(0, 1))
        part = middle_grad[g] + norm_back(first_grad, gain_first, first_hat[g], first_inverse[g])
        part = part.astype(BF)
        if at + 1 < len(groups):
            part, own_grads[at + 1] = lax.optimization_barrier((part, own_grads[at + 1]))
        input_parts.append(part)

    layer_output = jnp.concatenate(layer_parts, axis=1).reshape(seq_all, block_len, D)
    gain_rows = jnp.stack([first_gain_grad, second_gain_grad] + [jnp.zeros(D, F32)] * 6)
    input_parts = [every_head(part, n_head) for part in input_parts]
    small_own, small_sent = factor_grads(first_normalized.reshape(-1, D), joints, gain_rows)
    small_sum = scatter_core(small_own, small_sent)
    small_sum = ordered_scatter(small_sum, "b", 1)
    if len(groups) > 1:
        small_sum, input_parts[0] = lax.optimization_barrier((small_sum, input_parts[0]))
    small_sum = ordered_scatter(small_sum, "a", 0)
    small_sum, input_parts[-1] = lax.optimization_barrier((small_sum, input_parts[-1]))
    small_sum = sum_over_head(small_sum, n_head).astype(F32)
    input_grad = jnp.concatenate(input_parts, axis=1).reshape(seq_all, block_len, D).astype(F32)
    heads_sum = lax.dynamic_slice_in_dim(small_sum, head_at * h_cols, h_cols, 1)
    shared_sum = small_sum[:, H * RA : H * RA + RA * DH]
    gains_sum = small_sum[:, H * RA + RA * DH :].T
    out_sum = out_sum.T
    gate_up_sum = jnp.stack([gate_sum, up_sum])
    down_sum = down_sum.T

    rates = step_rates()
    heads_new = adam_update(headwise, headwise_mean, headwise_square, heads_sum, rates[0])
    shared_new = adam_update(
        shared_factors, shared_factors_mean, shared_factors_square, shared_sum, rates[1]
    )
    out_new = adam_update(out_weight, out_weight_mean, out_weight_square, out_sum, rates[2])
    gate_new = adam_update(gate_up, gate_up_mean, gate_up_square, gate_up_sum, rates[3])
    down_new = adam_update(down_weight, down_weight_mean, down_weight_square, down_sum, rates[4])
    gains_new = adam_update(norm_gains, norm_gains_mean, norm_gains_square, gains_sum, rates[5])
    return (
        layer_output,
        input_grad,
        *heads_new,
        *shared_new,
        *out_new,
        *gate_new,
        *down_new,
        *gains_new,
    )


def solution(mesh):
    n_seq = mesh.shape["seq"]
    n_head = mesh.shape["head"]
    inner = max(1, n_seq // 8)
    fine = Mesh(mesh.devices.reshape(n_seq // 2 // inner, inner, 2, n_head), ("a", "b", "c", "h"))
    token = P(None, SEQ, None)
    heads = P(SEQ, "h")
    shared = P(SEQ, None)
    turned = P("h", SEQ)
    gates = P(None, SEQ, "h")
    gains = P(None, SEQ)
    weights = sum(([spec] * 3 for spec in (heads, shared, turned, gates, turned, gains)), [])
    return jax.shard_map(
        on_device,
        mesh=fine,
        in_specs=(token, token, P(), P(), *weights),
        out_specs=(token, token, *weights),
        check_vma=False,
    )
```
